32 devices in a mesh: outer: 4 (over y, x), inner: 8 (over z, core).
Axes of the slice: x: 2, y: 2, z: 4, core: 2. Of those that a mesh axis runs over, the one named last changes fastest.
Arguments:
- queries: bfloat16 [8192, 1024], P(('outer', 'inner')), may hold values from -6 to 6
- keys: bfloat16 [2, 8192, 1024], P(None, ('outer', 'inner')), may hold values from -6 to 6
- values: bfloat16 [2, 8192, 1024], P(None, ('outer', 'inner')), may hold values from -6 to 6
- betas: float32 [2, 8, 8192], P(None, None, ('outer', 'inner')), may hold values from 0 to 2
- log_decay: float32 [8, 8192], P(None, ('outer', 'inner')), may hold values from -1 to 0
- out_gain: float32 [128], replicated, may hold values from 0.5 to 1.5
Outputs:
- mixed: bfloat16 [8192, 1024], P(('outer', 'inner'))
The draws below stay inside these ranges and needn't reach their ends.
All inputs are finite; a program needn't handle non-finite values.
Results may differ from the reference program's by a relative error of at most 0.0018.
Values sent between devices are 32-bit elements; how exact they have to be, the bound alone decides.
A program may use at most 128 MiB of HBM per device.

```python
import jax
import jax.numpy as jnp
from jax import lax

HEADS = 8
DK = 128
DV = 128
BLOCK_LEN = 64
TOK_DEV = 256
TOKENS = 8192


def head_speed(key):
    order = jax.random.permutation(jax.random.fold_in(key, 101), HEADS)
    quick_count = max(1, HEADS // 2)
    quick = (order < quick_count).astype(jnp.float32)
    device_log = jax.random.uniform(jax.random.fold_in(key, 102), (TOKENS // TOK_DEV,), jnp.float32, jnp.log(0.5), jnp.log(2.0))
    device_factor = jnp.repeat(jnp.exp(device_log), TOK_DEV)
    return (quick, device_factor)


def draw_log_decay(key, part):
    quick, device_factor = head_speed(key)
    quick_rate = jnp.exp(jax.random.uniform(jax.random.fold_in(key, 201), (HEADS, 1), jnp.float32, jnp.log(1.0 / 50.0), jnp.log(1.0 / 30.0)))
    slow_rate = jnp.exp(jax.random.uniform(jax.random.fold_in(key, 202), (HEADS, 1), jnp.float32, jnp.log(0.1), jnp.log(0.4))) / TOKENS
    rate = jnp.where(quick[:, None] > 0.5, quick_rate, slow_rate)
    rough = jax.random.uniform(jax.random.fold_in(key, 203), (HEADS, TOKENS), jnp.float32, 0.5, 1.5)
    base_log = -rate * rough * device_factor[None, :]
    places = jax.random.randint(jax.random.fold_in(key, 204), (2,), 0, TOKENS)
    position = jnp.arange(TOKENS, dtype=jnp.int32)
    struck = jnp.max((position[None, :] == places[:, None]).astype(jnp.float32), 0)
    depth = jax.random.uniform(jax.random.fold_in(key, 205), (HEADS, TOKENS), jnp.float32, jnp.log(0.55), jnp.log(0.8))
    return base_log + struck[None, :] * depth


def draw_betas(key, part):
    quick, device_factor = head_speed(key)
    normal_part = jnp.clip(jax.random.normal(jax.random.fold_in(key, 301), (2, HEADS, TOKENS), jnp.float32), -4.0, 4.0)
    quick_beta = 2.0 * jax.nn.sigmoid(1.2 * normal_part)
    slow_gap = 40.0 / TOKENS * jax.random.uniform(jax.random.fold_in(key, 303), (2, HEADS, TOKENS), jnp.float32, 0.5, 1.5) * device_factor[None, None, :]
    slow_beta = 2.0 - slow_gap
    return jnp.where(quick[None, :, None] > 0.5, quick_beta, slow_beta)


def level_of(own_key, dims, cuts, low, top_value):
    level, own = 1.0, jax.random.fold_in(own_key, 6)
    for dim, parts in cuts:
        draws = jnp.exp(jax.random.uniform(jax.random.fold_in(own, dim), (parts,), jnp.float32, low / len(cuts), top_value / len(cuts)))
        level = level * jnp.repeat(draws, dims[dim] // parts).reshape([-1 if axis == dim else 1 for axis in range(len(dims))])
    return level


def centred(key, dims, scale, limit, cuts=(), held_as=jnp.bfloat16):
    values = scale * jax.random.normal(key, dims, jnp.float32)
    if cuts:
        values = values * level_of(key, dims, cuts, -0.22, 0.18)
    return jnp.clip(values, -limit, limit).astype(held_as)


def setup_inputs(seed: int = 0) -> dict:
    key_list = jax.random.split(jax.random.key(seed), 7)
    return {
        "queries": centred(key_list[0], (TOKENS, HEADS * DK), 1.0, 6.0, ((0, 32),)),
        "keys": centred(key_list[1], (2, TOKENS, HEADS * DK), 1.0, 6.0, ((1, 32),)),
        "values": centred(key_list[2], (2, TOKENS, HEADS * DV), 1.0, 6.0, ((1, 32),)),
        "betas": draw_betas(jax.random.fold_in(key_list[6], 71), 0),
        "log_decay": draw_log_decay(jax.random.fold_in(key_list[6], 71), 0),
        "out_gain": jnp.clip(1.0 + 0.1 * jax.random.normal(key_list[5], (DV,), jnp.float32), 0.5, 1.5),
    }


HIGHEST = lax.Precision.HIGHEST

def prepare(queries, keys, values, betas, log_decay):
    length = queries.shape[0]
    heads = betas.shape[1]
    width_k = queries.shape[1] // heads
    width_v = values.shape[2] // heads
    blocks = length // BLOCK_LEN
    reflect = 2 * BLOCK_LEN
    query_f = queries.astype(jnp.float32).reshape(blocks, BLOCK_LEN, heads, width_k).transpose(0, 2, 1, 3)
    query_inv = lax.rsqrt(lax.optimization_barrier(jnp.sum(query_f * query_f, -1)) + 1e-06)
    query_n = query_f * query_inv[..., None]
    key_f = keys.astype(jnp.float32).reshape(2, blocks, BLOCK_LEN, heads, width_k).transpose(1, 3, 2, 0, 4)
    key_f = key_f.reshape(blocks, heads, reflect, width_k)
    key_inv = lax.rsqrt(lax.optimization_barrier(jnp.sum(key_f * key_f, -1)) + 1e-06)
    key_n = key_f * key_inv[..., None]
    value_n = values.astype(jnp.float32).reshape(2, blocks, BLOCK_LEN, heads, width_v).transpose(1, 3, 2, 0, 4)
    value_n = value_n.reshape(blocks, heads, reflect, width_v)
    beta_r = betas.reshape(2, heads, blocks, BLOCK_LEN).transpose(2, 1, 3, 0).reshape(blocks, heads, reflect)
    decay_t = log_decay.reshape(heads, blocks, BLOCK_LEN).transpose(1, 0, 2)
    decay_r = jnp.stack([decay_t, jnp.zeros_like(decay_t)], -1).reshape(blocks, heads, reflect)
    cumulative = jnp.cumsum(decay_r, -1)
    row_idx = lax.broadcasted_iota(jnp.int32, (reflect, reflect), 0)
    col_idx = lax.broadcasted_iota(jnp.int32, (reflect, reflect), 1)
    key_gram = jnp.einsum('nhrd,nhsd->nhrs', key_f, key_f, precision=HIGHEST) * key_inv[..., :, None] * key_inv[..., None, :]
    fall_off = jnp.exp(jnp.minimum(cumulative[..., :, None] - cumulative[..., None, :], 0.0))
    strict_low = jnp.where(row_idx > col_idx, key_gram * fall_off, 0.0)
    system = jnp.eye(reflect, dtype=jnp.float32) + beta_r[..., :, None] * strict_low
    scaled = jnp.exp(cumulative)
    right_side = jnp.concatenate([(beta_r * scaled)[..., None] * key_n, beta_r[..., None] * value_n], -1)
    solved = lax.linalg.triangular_solve(system, right_side, left_side=True, lower=True, unit_diagonal=True)
    write_key = solved[..., :width_k]
    write_val = solved[..., width_k:]
    tok_idx = lax.broadcasted_iota(jnp.int32, (BLOCK_LEN, reflect), 0)
    ref_idx = lax.broadcasted_iota(jnp.int32, (BLOCK_LEN, reflect), 1)
    query_cum = cumulative.reshape(blocks, heads, BLOCK_LEN, 2)[..., 1]
    query_key = jnp.einsum('nhcd,nhsd->nhcs', query_f, key_f, precision=HIGHEST) * query_inv[..., :, None] * key_inv[..., None, :]
    fade = jnp.exp(jnp.minimum(query_cum[..., :, None] - cumulative[..., None, :], 0.0))
    reach = jnp.where(ref_idx <= 2 * tok_idx + 1, query_key * fade, 0.0)
    reduced = jnp.exp(query_cum)[..., None] * query_n - jnp.einsum('nhcs,nhsd->nhcd', reach, write_key, precision=HIGHEST)
    local_out = jnp.einsum('nhcs,nhsd->nhcd', reach, write_val, precision=HIGHEST)
    last_cum = cumulative[..., -1:]
    tail = jnp.exp(last_cum - cumulative)
    trans = jnp.exp(last_cum)[..., None] * jnp.eye(width_k, dtype=jnp.float32)
    trans = trans - jnp.einsum('nhsd,nhse->nhde', tail[..., None] * write_key, key_n, precision=HIGHEST)
    inject = jnp.einsum('nhsd,nhse->nhde', tail[..., None] * write_val, key_n, precision=HIGHEST)
    return (reduced, local_out, trans, inject)

def finish(readout, out_gain):
    mean_sq = lax.optimization_barrier(jnp.mean(readout * readout, -1, keepdims=True))
    normed = readout * lax.rsqrt(mean_sq + 1e-05) * out_gain
    blocks, heads, span, width_v = normed.shape
    return normed.transpose(0, 2, 1, 3).reshape(blocks * span, heads * width_v).astype(jnp.bfloat16)

def reference(queries, keys, values, betas, log_decay, out_gain):
    groups = TOKENS // TOK_DEV
    query_g = queries.reshape(groups, TOK_DEV, HEADS * DK)
    key_g = keys.reshape(2, groups, TOK_DEV, HEADS * DK).transpose(1, 0, 2, 3)
    value_g = values.reshape(2, groups, TOK_DEV, HEADS * DV).transpose(1, 0, 2, 3)
    beta_g = betas.reshape(2, HEADS, groups, TOK_DEV).transpose(2, 0, 1, 3)
    decay_g = log_decay.reshape(HEADS, groups, TOK_DEV).transpose(1, 0, 2)

    def group_step(state, inputs):
        reduced, local_out, trans, inject = prepare(*inputs)

        def block_step(inner_state, pieces):
            red_b, loc_b, trans_b, inj_b = pieces
            readout = jnp.einsum('hcd,hed->hce', red_b, inner_state, precision=HIGHEST) + loc_b
            next_state = jnp.einsum('hde,hef->hdf', inner_state, trans_b, precision=HIGHEST) + inj_b
            return (next_state, readout)
        state, readouts = lax.scan(block_step, state, (reduced, local_out, trans, inject))
        return (state, finish(readouts, out_gain))
    start = jnp.zeros((HEADS, DV, DK), jnp.float32)
    final_state, outputs = lax.scan(group_step, start, (query_g, key_g, value_g, beta_g, decay_g))
    return outputs.reshape(TOKENS, HEADS * DV)
```

```python
import functools

import jax
import jax.numpy as jnp
from jax import lax
from jax.experimental import pallas as pl
from jax.experimental.pallas import tpu as pltpu
from jax.sharding import PartitionSpec as P

BLOCK_LEN = 64
F32 = jnp.float32
BF16 = jnp.bfloat16


def split(x):
    high = x.astype(BF16)
    low = (x - high.astype(F32)).astype(BF16)
    return high, low


def dot(a, b):
    return lax.dot_general(a, b, (((1,), (0,)), ((), ())), preferred_element_type=F32)


def dot_t(a, b):
    return lax.dot_general(a, b, (((1,), (1,)), ((), ())), preferred_element_type=F32)


def wide(x):
    return jnp.concatenate(split(x), 1)


def mul(a, b):
    a2 = wide(a)
    bh, bl = split(b)
    if b.shape[1] == 128:
        row = jnp.concatenate([bh, bl], 1)
        both = dot(a2, jnp.concatenate([row, row], 0))
        return both[:, :128] + both[:, 128:]
    return dot(a2, jnp.concatenate([bh, bh], 0)) + dot(a2[:, :128], bl)


def mul_left(a, b):
    return dot(wide(a), jnp.concatenate([b, b], 0))


def add_right(x, y):
    return jnp.concatenate([x[:, :128], x[:, 128:] + y], 1)


def masks():
    span = BLOCK_LEN
    size = 2 * span
    row = lax.broadcasted_iota(jnp.int32, (size, size), 0)
    col = lax.broadcasted_iota(jnp.int32, (size, size), 1)
    row_t, col_t = row & (span - 1), col & (span - 1)
    row_rank = 2 * row_t + (row >= span).astype(jnp.int32)
    col_rank = 2 * col_t + (col >= span).astype(jnp.int32)
    differ = row_rank ^ col_rank
    eye = row == col
    eye_f = eye.astype(F32)
    lower = row_rank > col_rank
    c_mask = (col_t <= row_t) & (col < span)
    r_mask = (row_t <= col_t) & (row < span)
    levels = []
    width = 1
    while width < size:
        levels.append(
            (differ >= width) & (differ < 2 * width) & lower
        )
        width *= 2

    return row, col_t, row_t, eye, eye_f, lower, c_mask, r_mask, levels


def head_maps(blocks, heads_in, load, emit):
    span = BLOCK_LEN
    row, col_t, row_t, eye, eye_f, lower, c_mask, r_mask, levels = masks()
    work = []
    for i, n in [(i, n) for i in range(heads_in) for n in range(blocks)]:
        q_b, k_b, v_b, d_row, beta_row = load(i, n)
        d_col = jnp.sum(jnp.where(eye, d_row, 0.0), 1, keepdims=True)
        beta_col = jnp.sum(jnp.where(eye, beta_row, 0.0), 1, keepdims=True)
        c_col = jnp.sum(jnp.where(c_mask, d_row, 0.0), 1, keepdims=True)
        c_row = jnp.sum(jnp.where(r_mask, d_col, 0.0), 0, keepdims=True)
        gram = dot_t(k_b, k_b)
        k_f = k_b.astype(F32)
        q_f = q_b.astype(F32)
        ki_col = lax.rsqrt(jnp.sum(k_f * k_f, 1, keepdims=True) + 1e-06)
        ki_row = lax.rsqrt(jnp.sum(jnp.where(eye, gram, 0.0), 0, keepdims=True) + 1e-06)
        qi_col = lax.rsqrt(jnp.sum(q_f * q_f, 1, keepdims=True) + 1e-06)
        fall = jnp.exp(jnp.minimum(c_col - c_row, 0.0))
        low = jnp.where(lower, gram * (beta_col * ki_col) * ki_row * fall, 0.0)
        reach = dot_t(q_b, k_b) * qi_col * ki_row * fall[:span]
        reach = jnp.where(col_t[:span] <= row_t[:span], reach, 0.0)
        query = q_f * (qi_col * jnp.exp(c_col[:span]))
        work.append((k_b, v_b, beta_row, c_row, c_col, ki_row, ki_col, low, reach, query))

    inverse = [eye_f - jnp.where(levels[0], w[7], 0.0) for w in work]
    for mask in levels[1:]:
        part = [mul(jnp.where(mask, w[7], 0.0), t) for w, t in zip(work, inverse)]
        inverse = [t - mul(t, p) for t, p in zip(inverse, part)]

    states = [None] * heads_in
    for n in range(blocks):
        for i in range(heads_in):
            state = states[i]
            k_b, v_b, beta_row, c_row, c_col, ki_row, ki_col, low, reach, query = work[i * blocks + n]
            t = inverse[i * blocks + n] * beta_row
            written = jnp.concatenate(
                [mul_left(t * (ki_row * jnp.exp(c_row)), k_b), mul_left(t, v_b)], 1
            )
            got = mul(reach, written)
            reduced, local_out = query - got[:, :128], got[:, 128:]
            last = c_col[span - 1 : span, :]
            tail = jnp.exp(last - c_col) * ki_col
            wh, wl = split(written * tail)
            k_t = jnp.transpose(k_b.astype(F32)).astype(BF16)
            made = dot(jnp.concatenate([k_t, k_t], 1), jnp.concatenate([wh, wl], 0))
            trans = jnp.exp(last) * eye_f - made[:, :128]
            inject = made[:, 128:]
            if state is None:
                emit(i, n, reduced, local_out)
                states[i] = jnp.concatenate([trans, inject], 1)
            else:
                read = mul(reduced, state)
                emit(i, n, read[:, :128], read[:, 128:] + local_out)
                states[i] = add_right(mul(trans, state), inject)
    return states


def local_kernel(blocks, q_ref, k_ref, v_ref, s_ref, x_ref, c_ref, b_ref):
    def load(i, n):
        at = pl.ds(n * BLOCK_LEN, BLOCK_LEN)
        k_b = jnp.concatenate([k_ref[0, at, :], k_ref[1, at, :]], 0)
        v_b = jnp.concatenate([v_ref[0, at, :], v_ref[1, at, :]], 0)
        return q_ref[at, :], k_b, v_b, s_ref[0, n : n + 1, :], s_ref[0, blocks + n : blocks + n + 1, :]

    def emit(i, n, carried, base):
        at = pl.ds(n * BLOCK_LEN, BLOCK_LEN)
        c_ref[0, at, :] = carried
        b_ref[0, at, :] = base

    x_ref[0] = head_maps(blocks, 1, load, emit)[0]


def small_rows(betas, log_decay):
    heads, length = log_decay.shape
    blocks = length // BLOCK_LEN
    beta = betas.reshape(2, heads, blocks, BLOCK_LEN).transpose(1, 2, 0, 3)
    beta = beta.reshape(heads, blocks, 2 * BLOCK_LEN)
    decay = log_decay.reshape(heads, blocks, 1, BLOCK_LEN)
    decay = jnp.concatenate([decay, decay], 2).reshape(heads, blocks, 2 * BLOCK_LEN)
    small = jnp.concatenate([decay, beta], 1)
    return small


def local_phase(queries, keys, values, betas, log_decay):
    length = queries.shape[0]
    heads = betas.shape[1]
    blocks = length // BLOCK_LEN
    small = small_rows(betas, log_decay)
    return pl.pallas_call(
        functools.partial(local_kernel, blocks),
        grid=(heads,),
        in_specs=[
            pl.BlockSpec((length, 128), lambda h: (0, h)),
            pl.BlockSpec((2, length, 128), lambda h: (0, 0, h)),
            pl.BlockSpec((2, length, 128), lambda h: (0, 0, h)),
            pl.BlockSpec((1, 2 * blocks, 128), lambda h: (h, 0, 0)),
        ],
        out_specs=[
            pl.BlockSpec((1, 128, 256), lambda h: (h, 0, 0)),
            pl.BlockSpec((1, length, 128), lambda h: (h, 0, 0)),
            pl.BlockSpec((1, length, 128), lambda h: (h, 0, 0)),
        ],
        out_shape=[
            jax.ShapeDtypeStruct((heads, 128, 256), F32),
            jax.ShapeDtypeStruct((heads, length, 128), F32),
            jax.ShapeDtypeStruct((heads, length, 128), F32),
        ],
        name="local_phase",
    )(queries, keys, values, small)


def then(earlier, later):
    return add_right(mul(later[:, :128], earlier), later[:, 128:])


def normed(carried, base, state, gain):
    readout = mul(carried, state) + base
    mean_sq = jnp.mean(readout * readout, 1, keepdims=True)
    return (readout * lax.rsqrt(mean_sq + 1e-05) * gain).astype(BF16)


def unit_vectors(eye, c_mask, r_mask, d_row):
    d_col = jnp.sum(jnp.where(eye, d_row, 0.0), 1, keepdims=True)
    c_col = jnp.sum(jnp.where(c_mask, d_row, 0.0), 1, keepdims=True)
    c_row = jnp.sum(jnp.where(r_mask, d_col, 0.0), 0, keepdims=True)
    return c_col, c_row


def systems(blocks, heads_in, load):
    row, col_t, row_t, eye, eye_f, lower, c_mask, r_mask, levels = masks()
    work = []
    for i, n in [(i, n) for i in range(heads_in) for n in range(blocks)]:
        k_b, d_row, beta_row = load(i, n)
        beta_col = jnp.sum(jnp.where(eye, beta_row, 0.0), 1, keepdims=True)
        c_col, c_row = unit_vectors(eye, c_mask, r_mask, d_row)
        gram = dot_t(k_b, k_b)
        k_f = k_b.astype(F32)
        ki_col = lax.rsqrt(jnp.sum(k_f * k_f, 1, keepdims=True) + 1e-06)
        ki_row = lax.rsqrt(jnp.sum(jnp.where(eye, gram, 0.0), 0, keepdims=True) + 1e-06)
        fall = jnp.exp(jnp.minimum(c_col - c_row, 0.0))
        low = jnp.where(lower, gram * (beta_col * ki_col) * ki_row * fall, 0.0)
        work.append((beta_row, c_row, c_col, ki_row, ki_col, low))
    inverse = [eye_f - jnp.where(levels[0], w[5], 0.0) for w in work]
    for mask in levels[1:]:
        part = [mul(jnp.where(mask, w[5], 0.0), t) for w, t in zip(work, inverse)]
        inverse = [t - mul(t, p) for t, p in zip(inverse, part)]
    return work, inverse, eye_f


def state_maps(blocks, heads_in, work, inverse, eye_f, load_kv, keep):
    span = BLOCK_LEN
    states = [None] * heads_in
    for n in range(blocks):
        for i in range(heads_in):
            state = states[i]
            k_b, v_b = load_kv(i, n)
            beta_row, c_row, c_col, ki_row, ki_col, low = work[i * blocks + n]
            t = inverse[i * blocks + n] * beta_row
            written = jnp.concatenate(
                [mul_left(t * (ki_row * jnp.exp(c_row)), k_b), mul_left(t, v_b)], 1
            )
            last = c_col[span - 1 : span, :]
            tail = jnp.exp(last - c_col) * ki_col
            wh, wl = split(written * tail)
            k_t = jnp.transpose(k_b.astype(F32)).astype(BF16)
            made = dot(jnp.concatenate([k_t, k_t], 1), jnp.concatenate([wh, wl], 0))
            trans = jnp.exp(last) * eye_f - made[:, :128]
            inject = made[:, 128:]
            keep(i, n, written, c_row, ki_row, state)
            if state is None:
                states[i] = jnp.concatenate([trans, inject], 1)
            else:
                states[i] = add_right(mul(trans, state), inject)
    return states


def reads(blocks, heads_in, load, emit):
    span = BLOCK_LEN
    row = lax.broadcasted_iota(jnp.int32, (span, 2 * span), 0)
    col = lax.broadcasted_iota(jnp.int32, (span, 2 * span), 1)
    col_t = col & (span - 1)
    seen = col_t <= row
    for i, n in [(i, n) for i in range(heads_in) for n in range(blocks)]:
        q_b, k_b, d_row, written, c_row, ki_row, state = load(i, n)
        c_col = jnp.sum(jnp.where(seen & (col < span), d_row, 0.0), 1, keepdims=True)
        q_f = q_b.astype(F32)
        qi_col = lax.rsqrt(jnp.sum(q_f * q_f, 1, keepdims=True) + 1e-06)
        fall = jnp.exp(jnp.minimum(c_col - c_row, 0.0))
        reach = jnp.where(seen, dot_t(q_b, k_b) * qi_col * ki_row * fall, 0.0)
        query = q_f * (qi_col * jnp.exp(c_col))
        got = mul(reach, written)
        reduced, local_out = query - got[:, :128], got[:, 128:]
        if n == 0:
            emit(i, n, reduced, local_out)
        else:
            read = mul(reduced, state)
            emit(i, n, read[:, :128], read[:, 128:] + local_out)


def whole_kernel(
    inner, outer, q_hbm, k_hbm, v_hbm, beta_ref, decay_ref, g_ref, o_ref,
    q_buf, k_buf, v_buf, w_buf, p_buf, vec_buf,
    away, near, own, even_map, sent, got, groups, mine, ready, came, aside, beside, c_buf, b_buf,
    load_k, load_v, load_q,
    send0, recv0, send1, recv1, send2, recv2, send3, recv3, send4, recv4, send5, recv5,
):
    mesh_id = pl.DeviceIdType.MESH
    length = q_hbm.shape[0]
    blocks = length // BLOCK_LEN
    me = lax.axis_index("inner")
    group = lax.axis_index("outer")
    core, chip, chips = me % 2, me // 2, inner // 2
    partner = chip * 2 + 1 - core
    groups[...] = jnp.zeros_like(groups)
    barrier = pltpu.get_barrier_semaphore()
    for d in range(1, chips):
        pl.semaphore_signal(
            barrier, inc=1, device_id=(group, (chip + d) % chips * 2 + core), device_id_type=mesh_id
        )
    pl.semaphore_signal(barrier, inc=1, device_id=(group, partner), device_id_type=mesh_id)
    for d in range(1, outer):
        pl.semaphore_signal(barrier, inc=1, device_id=((group + d) % outer, me), device_id_type=mesh_id)

    def target(turn):
        return (chip + turn + 1) % chips

    def lanes_of(turn):
        return pl.ds(pl.multiple_of(target(turn) * 256, 256), 256)

    def k_copy(turn):
        return pltpu.make_async_copy(k_hbm.at[:, :, lanes_of(turn)], k_buf.at[turn], load_k.at[turn])

    def v_copy(turn):
        return pltpu.make_async_copy(v_hbm.at[:, :, lanes_of(turn)], v_buf.at[turn], load_v.at[turn])

    def q_copy(turn):
        return pltpu.make_async_copy(q_hbm.at[:, lanes_of(turn)], q_buf.at[turn], load_q.at[turn])

    for t in range(chips):
        k_copy(t).start()
        v_copy(t).start()
    for t in range(chips):
        q_copy(t).start()

    def near_copy(turn):
        return pltpu.make_async_remote_copy(
            src_ref=away.at[turn], dst_ref=near.at[turn],
            send_sem=send0.at[turn], recv_sem=recv0.at[turn],
            device_id=(group, partner), device_id_type=mesh_id,
        )

    def map_copy(d):
        return pltpu.make_async_remote_copy(
            src_ref=sent.at[d], dst_ref=got.at[d],
            send_sem=send1.at[d], recv_sem=recv1.at[d],
            device_id=(group, (chip + d) % chips * 2 + core), device_id_type=mesh_id,
        )

    def chip_map(turn):
        near_copy(turn).wait()
        here, there = own[turn], near[turn]
        even = jnp.where(core == 0, here, there)
        odd = jnp.where(core == 0, there, here)
        even_map[turn] = even
        return then(even, odd)

    def parity(i):
        return core if i == 0 else 1 - core

    def head_lanes(i):
        return pl.ds(pl.multiple_of(parity(i) * 128, 128), 128)

    def rows_of(head, n):
        at = slice(n * BLOCK_LEN, (n + 1) * BLOCK_LEN)
        row = pl.ds(head, 1)
        d = decay_ref[row, :][:, at]
        b0, b1 = beta_ref[0, row, :][:, at], beta_ref[1, row, :][:, at]
        return jnp.concatenate([d, d], 1), jnp.concatenate([b0, b1], 1)

    def pair_of(buf, turn, i, n):
        at = pl.ds(n * BLOCK_LEN, BLOCK_LEN)
        return jnp.concatenate([buf[turn, 0, at, head_lanes(i)], buf[turn, 1, at, head_lanes(i)]], 0)

    def step(turn, carry):
        heads = [target(turn) * 2 + parity(i) for i in range(2)]
        k_copy(turn).wait()

        def load(i, n):
            d_row, beta_row = rows_of(heads[i], n)
            return pair_of(k_buf, turn, i, n), d_row, beta_row

        work, inverse, eye_f = systems(blocks, 2, load)

        @pl.when(turn == 0)
        def _():
            pl.semaphore_wait(barrier, chips + outer - 1)

        @pl.when(turn > 0)
        def _():
            sent[turn] = chip_map(turn - 1)
            map_copy(turn).start()

        v_copy(turn).wait()

        def load_kv(i, n):
            return pair_of(k_buf, turn, i, n), pair_of(v_buf, turn, i, n)

        def keep(i, n, written, c_row, ki_row, state):
            w_buf[turn, i, n] = written
            vec_buf[turn, i, n, 0:1, :] = c_row
            vec_buf[turn, i, n, 1:2, :] = ki_row
            if n:
                p_buf[turn, i, n] = state

        states = state_maps(blocks, 2, work, inverse, eye_f, load_kv, keep)
        away[turn] = states[1]
        own[turn] = states[0]

        near_copy(turn).start()
        return carry

    lax.fori_loop(0, chips, step, 0)

    def read_step(turn, carry):
        heads = [target(turn) * 2 + parity(i) for i in range(2)]
        q_copy(turn).wait()

        def load(i, n):
            at = pl.ds(n * BLOCK_LEN, BLOCK_LEN)
            d_row, _ = rows_of(heads[i], n)
            return (
                q_buf[turn, at, head_lanes(i)], pair_of(k_buf, turn, i, n), d_row, w_buf[turn, i, n],
                vec_buf[turn, i, n, 0:1, :], vec_buf[turn, i, n, 1:2, :], p_buf[turn, i, n] if n else None,
            )

        def emit(i, n, carried, base):
            at = pl.ds(n * BLOCK_LEN, BLOCK_LEN)
            c_buf[turn, i, at, :] = carried
            b_buf[turn, i, at, :] = base

        reads(blocks, 2, load, emit)
        return carry

    lax.fori_loop(0, chips // 2, read_step, 0)
    got[0] = chip_map(chips - 1)
    for d in range(1, chips):
        map_copy(d).wait()

    maps = [got[(chip - i + chips) % chips] for i in range(chips)]

    def tree(parts):
        if len(parts) == 1:
            return parts
        half = len(parts) // 2
        pairs = [then(parts[2 * i], parts[2 * i + 1]) for i in range(half)]
        return pairs

    level = maps
    levels = [maps]
    while len(level) > 1:
        level = tree(level)
        levels.append(level)
    mine[0] = level[0][:, :128]
    mine[1] = level[0][:, 128:]

    def group_copy(part, d):
        sems = (send2, recv2) if part == 0 else (send5, recv5)
        return pltpu.make_async_remote_copy(
            src_ref=mine.at[part], dst_ref=groups.at[part, d],
            send_sem=sems[0].at[d], recv_sem=sems[1].at[d],
            device_id=((group + d) % outer, me), device_id_type=mesh_id,
        )

    for d in range(outer - 1, 0, -1):

        @pl.when(group + d < outer)
        def _():
            group_copy(1, d).start()

    for d in range(outer - 1, 0, -1):

        @pl.when((group + d < outer) & (group > 0))
        def _():
            group_copy(0, d).start()

    before = {}
    for i in range(1, chips):
        low = i & -i
        height = low.bit_length() - 1
        part = levels[height][(i - low) >> height]
        before[i] = part if i == low else then(before[i - low], part)
    left = wide(jnp.concatenate([before[i][:, :128] for i in range(1, chips)], 0))
    right = jnp.concatenate([before[i][:, 128:] for i in range(1, chips)], 0)

    lax.fori_loop(chips // 2, chips, read_step, 0)

    for d in range(1, outer):

        @pl.when(group + d < outer)
        def _():
            group_copy(1, d).wait_send()

        @pl.when((group + d < outer) & (group > 0))
        def _():
            group_copy(0, d).wait_send()

        @pl.when(group - d >= 0)
        def _():
            group_copy(1, d).wait_recv()

        @pl.when(group - d > 0)
        def _():
            group_copy(0, d).wait_recv()

    start = jnp.zeros((128, 128), F32)
    for g in range(outer - 1):
        at = (group - g + outer) % outer
        moved = groups[1, at]
        if g:
            moved = mul(groups[0, at], start) + moved
        start = jnp.where(g < group, moved, start)

    sh, sl = split(start)
    row = jnp.concatenate([sh, sl], 1)
    both = dot(left, jnp.concatenate([row, row], 0))
    ready[0] = start
    ready[pl.ds(1, chips - 1)] = (both[:, :128] + both[:, 128:] + right).reshape(chips - 1, 128, 128)

    def back_copy(d):
        to = (chip + d) % chips
        return pltpu.make_async_remote_copy(
            src_ref=ready.at[to], dst_ref=came.at[d],
            send_sem=send3.at[d], recv_sem=recv3.at[d],
            device_id=(group, to * 2 + core), device_id_type=mesh_id,
        )

    def side_copy(d):
        return pltpu.make_async_remote_copy(
            src_ref=aside.at[d], dst_ref=beside.at[d],
            send_sem=send4.at[d], recv_sem=recv4.at[d],
            device_id=(group, partner), device_id_type=mesh_id,
        )

    for d in range(1, chips):
        back_copy(d).start()

    def out(turn, i, state):
        head = target(turn) * 2 + parity(i)
        lanes = pl.ds(pl.multiple_of(head * 128, 128), 128)
        o_ref[:, lanes] = normed(c_buf[turn, i], b_buf[turn, i], state, g_ref[...])

    for d in range(chips):
        turn = chips - 1 - d
        if d:
            back_copy(d).wait()
            enter = came[d]
        else:
            enter = ready[chip]
        pair = even_map[turn]
        after = mul(pair[:, :128], enter) + pair[:, 128:]
        aside[d] = jnp.where(core == 0, after, enter)
        side_copy(d).start()
        out(turn, 0, jnp.where(core == 0, enter, after))
        if d:
            side_copy(d - 1).wait()
            out(turn + 1, 1, beside[d - 1])
    side_copy(chips - 1).wait()
    out(0, 1, beside[chips - 1])


def whole(inner, outer, queries, keys, values, betas, log_decay, out_gain):
    length, width = queries.shape
    blocks = length // BLOCK_LEN
    chips = inner // 2
    vmem = pl.BlockSpec(memory_space=pltpu.VMEM)
    hbm = pl.BlockSpec(memory_space=pltpu.HBM)
    dma = pltpu.SemaphoreType.DMA
    return pl.pallas_call(
        functools.partial(whole_kernel, inner, outer),
        in_specs=[hbm] * 3 + [vmem] * 3,
        out_specs=vmem,
        out_shape=jax.ShapeDtypeStruct((length, width), BF16),
        scratch_shapes=[
            pltpu.VMEM((chips, length, 256), BF16),
            *[pltpu.VMEM((chips, 2, length, 256), BF16)] * 2,
            *[pltpu.VMEM((chips, 2, blocks, 128, 256), F32)] * 2,
            pltpu.VMEM((chips, 2, blocks, 8, 128), F32),
            *[pltpu.VMEM((chips, 128, 256), F32)] * 6,
            pltpu.VMEM((2, outer, 128, 128), F32),
            pltpu.VMEM((2, 128, 128), F32),
            *[pltpu.VMEM((chips, 128, 128), F32)] * 4,
            *[pltpu.VMEM((chips, 2, length, 128), F32)] * 2,
            *[dma((chips,))] * 3,
            *[dma((chips,))] * 4,
            *[dma((outer,))] * 2,
            *[dma((chips,))] * 4,
            *[dma((outer,))] * 2,
        ],
        compiler_params=pltpu.CompilerParams(
            collective_id=0, has_side_effects=True, vmem_limit_bytes=53 * 1024 * 1024
        ),
        name="whole",
    )(queries, keys, values, betas, log_decay, out_gain.reshape(1, 128))


HIGHEST = lax.Precision.HIGHEST


def join(earlier, later):
    moved = jnp.einsum("hde,hef->hdf", later[..., :128], earlier, precision=HIGHEST)
    return jnp.concatenate([moved[..., :128], moved[..., 128:] + later[..., 128:]], -1)


def entering(pairs, axis, begin):
    gathered = lax.all_gather(pairs, axis)

    def one(hop, state):
        return join(state, lax.dynamic_index_in_dim(gathered, hop, 0, False))

    return lax.fori_loop(0, lax.axis_index(axis), one, begin)


def exchange_plain(pairs):
    eye = jnp.concatenate([jnp.eye(128, dtype=F32), jnp.zeros((128, 128), F32)], 1)
    begin = jnp.zeros_like(pairs) + eye
    before = entering(pairs, "inner", begin)
    through = join(before, pairs)
    last = lax.axis_index("inner") == lax.axis_size("inner") - 1
    total = lax.psum(jnp.where(last, through, 0.0), "inner")
    start = entering(total, "outer", begin)
    return join(start, before)[..., 128:]


def finish_kernel(c_ref, b_ref, e_ref, g_ref, o_ref):
    readout = mul(c_ref[0], e_ref[0]) + b_ref[0]
    mean_sq = jnp.mean(readout * readout, 1, keepdims=True)
    o_ref[...] = (readout * lax.rsqrt(mean_sq + 1e-05) * g_ref[...]).astype(BF16)


def finish(carried, base, state, out_gain):
    heads, length, _ = carried.shape
    return pl.pallas_call(
        finish_kernel,
        grid=(heads,),
        in_specs=[
            pl.BlockSpec((1, length, 128), lambda h: (h, 0, 0)),
            pl.BlockSpec((1, length, 128), lambda h: (h, 0, 0)),
            pl.BlockSpec((1, 128, 128), lambda h: (h, 0, 0)),
            pl.BlockSpec((1, 128), lambda h: (0, 0)),
        ],
        out_specs=pl.BlockSpec((length, 128), lambda h: (0, h)),
        out_shape=jax.ShapeDtypeStruct((length, heads * 128), BF16),
        name="finish",
    )(carried, base, state, out_gain.reshape(1, 128))


def per_device(inner, outer, queries, keys, values, betas, log_decay, out_gain):
    heads = betas.shape[1]
    if inner == heads:
        return whole(inner, outer, queries, keys, values, betas, log_decay, out_gain)
    pairs, carried, base = local_phase(queries, keys, values, betas, log_decay)
    return finish(carried, base, exchange_plain(pairs), out_gain)


def solution(mesh):
    both = ("outer", "inner")
    placed = (P(both, None), P(None, both, None), P(None, both, None), P(None, None, both), P(None, both), P())
    return jax.shard_map(
        functools.partial(per_device, mesh.shape["inner"], mesh.shape["outer"]),
        mesh=mesh,
        in_specs=placed,
        out_specs=P(both, None),
        check_vma=False,
    )
```

```python
import functools

import jax
import jax.numpy as jnp
from jax import lax
from jax.experimental import pallas as pl
from jax.experimental.pallas import tpu as pltpu
from jax.sharding import PartitionSpec as P

BLOCK_LEN = 64
F32 = jnp.float32
BF16 = jnp.bfloat16


def split(x):
    high = x.astype(BF16)
    low = (x - high.astype(F32)).astype(BF16)
    return high, low


def dot(a, b):
    return lax.dot_general(a, b, (((1,), (0,)), ((), ())), preferred_element_type=F32)


def dot_t(a, b):
    return lax.dot_general(a, b, (((1,), (1,)), ((), ())), preferred_element_type=F32)


def wide(x):
    return jnp.concatenate(split(x), 1)


def mul(a, b):
    a2 = wide(a)
    bh, bl = split(b)
    if b.shape[1] == 128:
        row = jnp.concatenate([bh, bl], 1)
        both = dot(a2, jnp.concatenate([row, row], 0))
        return both[:, :128] + both[:, 128:]
    return dot(a2, jnp.concatenate([bh, bh], 0)) + dot(a2[:, :128], bl)


def mul_left(a, b):
    return dot(wide(a), jnp.concatenate([b, b], 0))


def add_right(x, y):
    return jnp.concatenate([x[:, :128], x[:, 128:] + y], 1)


def masks():
    span = BLOCK_LEN
    size = 2 * span
    row = lax.broadcasted_iota(jnp.int32, (size, size), 0)
    col = lax.broadcasted_iota(jnp.int32, (size, size), 1)
    row_t, col_t = row & (span - 1), col & (span - 1)
    row_rank = 2 * row_t + (row >= span).astype(jnp.int32)
    col_rank = 2 * col_t + (col >= span).astype(jnp.int32)
    differ = row_rank ^ col_rank
    eye = row == col
    eye_f = eye.astype(F32)
    lower = row_rank > col_rank
    c_mask = (col_t <= row_t) & (col < span)
    r_mask = (row_t <= col_t) & (row < span)
    levels = []
    width = 1
    while width < size:
        levels.append(
            (differ >= width) & (differ < 2 * width) & lower
        )
        width *= 2

    return row, col_t, row_t, eye, eye_f, lower, c_mask, r_mask, levels


def head_maps(blocks, heads_in, load, emit):
    span = BLOCK_LEN
    row, col_t, row_t, eye, eye_f, lower, c_mask, r_mask, levels = masks()
    work = []
    for i, n in [(i, n) for i in range(heads_in) for n in range(blocks)]:
        q_b, k_b, v_b, d_row, beta_row = load(i, n)
        d_col = jnp.sum(jnp.where(eye, d_row, 0.0), 1, keepdims=True)
        beta_col = jnp.sum(jnp.where(eye, beta_row, 0.0), 1, keepdims=True)
        c_col = jnp.sum(jnp.where(c_mask, d_row, 0.0), 1, keepdims=True)
        c_row = jnp.sum(jnp.where(r_mask, d_col, 0.0), 0, keepdims=True)
        gram = dot_t(k_b, k_b)
        k_f = k_b.astype(F32)
        q_f = q_b.astype(F32)
        ki_col = lax.rsqrt(jnp.sum(k_f * k_f, 1, keepdims=True) + 1e-06)
        ki_row = lax.rsqrt(jnp.sum(jnp.where(eye, gram, 0.0), 0, keepdims=True) + 1e-06)
        qi_col = lax.rsqrt(jnp.sum(q_f * q_f, 1, keepdims=True) + 1e-06)
        fall = jnp.exp(jnp.minimum(c_col - c_row, 0.0))
        low = jnp.where(lower, gram * (beta_col * ki_col) * ki_row * fall, 0.0)
        reach = dot_t(q_b, k_b) * qi_col * ki_row * fall[:span]
        reach = jnp.where(col_t[:span] <= row_t[:span], reach, 0.0)
        query = q_f * (qi_col * jnp.exp(c_col[:span]))
        work.append((k_b, v_b, beta_row, c_row, c_col, ki_row, ki_col, low, reach, query))

    inverse = [eye_f - jnp.where(levels[0], w[7], 0.0) for w in work]
    for mask in levels[1:]:
        part = [mul(jnp.where(mask, w[7], 0.0), t) for w, t in zip(work, inverse)]
        inverse = [t - mul(t, p) for t, p in zip(inverse, part)]

    states = [None] * heads_in
    for n in range(blocks):
        for i in range(heads_in):
            state = states[i]
            k_b, v_b, beta_row, c_row, c_col, ki_row, ki_col, low, reach, query = work[i * blocks + n]
            t = inverse[i * blocks + n] * beta_row
            written = jnp.concatenate(
                [mul_left(t * (ki_row * jnp.exp(c_row)), k_b), mul_left(t, v_b)], 1
            )
            got = mul(reach, written)
            reduced, local_out = query - got[:, :128], got[:, 128:]
            last = c_col[span - 1 : span, :]
            tail = jnp.exp(last - c_col) * ki_col
            wh, wl = split(written * tail)
            k_t = jnp.transpose(k_b.astype(F32)).astype(BF16)
            made = dot(jnp.concatenate([k_t, k_t], 1), jnp.concatenate([wh, wl], 0))
            trans = jnp.exp(last) * eye_f - made[:, :128]
            inject = made[:, 128:]
            if state is None:
                emit(i, n, reduced, local_out)
                states[i] = jnp.concatenate([trans, inject], 1)
            else:
                read = mul(reduced, state)
                emit(i, n, read[:, :128], read[:, 128:] + local_out)
                states[i] = add_right(mul(trans, state), inject)
    return states


def local_kernel(blocks, q_ref, k_ref, v_ref, s_ref, x_ref, c_ref, b_ref):
    def load(i, n):
        at = pl.ds(n * BLOCK_LEN, BLOCK_LEN)
        k_b = jnp.concatenate([k_ref[0, at, :], k_ref[1, at, :]], 0)
        v_b = jnp.concatenate([v_ref[0, at, :], v_ref[1, at, :]], 0)
        return q_ref[at, :], k_b, v_b, s_ref[0, n : n + 1, :], s_ref[0, blocks + n : blocks + n + 1, :]

    def emit(i, n, carried, base):
        at = pl.ds(n * BLOCK_LEN, BLOCK_LEN)
        c_ref[0, at, :] = carried
        b_ref[0, at, :] = base

    x_ref[0] = head_maps(blocks, 1, load, emit)[0]


def small_rows(betas, log_decay):
    heads, length = log_decay.shape
    blocks = length // BLOCK_LEN
    beta = betas.reshape(2, heads, blocks, BLOCK_LEN).transpose(1, 2, 0, 3)
    beta = beta.reshape(heads, blocks, 2 * BLOCK_LEN)
    decay = log_decay.reshape(heads, blocks, 1, BLOCK_LEN)
    decay = jnp.concatenate([decay, decay], 2).reshape(heads, blocks, 2 * BLOCK_LEN)
    small = jnp.concatenate([decay, beta], 1)
    return small


def local_phase(queries, keys, values, betas, log_decay):
    length = queries.shape[0]
    heads = betas.shape[1]
    blocks = length // BLOCK_LEN
    small = small_rows(betas, log_decay)
    return pl.pallas_call(
        functools.partial(local_kernel, blocks),
        grid=(heads,),
        in_specs=[
            pl.BlockSpec((length, 128), lambda h: (0, h)),
            pl.BlockSpec((2, length, 128), lambda h: (0, 0, h)),
            pl.BlockSpec((2, length, 128), lambda h: (0, 0, h)),
            pl.BlockSpec((1, 2 * blocks, 128), lambda h: (h, 0, 0)),
        ],
        out_specs=[
            pl.BlockSpec((1, 128, 256), lambda h: (h, 0, 0)),
            pl.BlockSpec((1, length, 128), lambda h: (h, 0, 0)),
            pl.BlockSpec((1, length, 128), lambda h: (h, 0, 0)),
        ],
        out_shape=[
            jax.ShapeDtypeStruct((heads, 128, 256), F32),
            jax.ShapeDtypeStruct((heads, length, 128), F32),
            jax.ShapeDtypeStruct((heads, length, 128), F32),
        ],
        name="local_phase",
    )(queries, keys, values, small)


def then(earlier, later):
    return add_right(mul(later[:, :128], earlier), later[:, 128:])


def normed(carried, base, state, gain):
    readout = mul(carried, state) + base
    mean_sq = jnp.mean(readout * readout, 1, keepdims=True)
    return (readout * lax.rsqrt(mean_sq + 1e-05) * gain).astype(BF16)


LOG2E = 1.4426950408889634


def split3(x):
    high = x.astype(BF16)
    rest = x - high.astype(F32)
    mid = rest.astype(BF16)
    low = rest - mid.astype(F32)
    return high.astype(F32), mid.astype(F32), low


def tokens_of(shape, dim):
    at = lax.broadcasted_iota(jnp.int32, shape, dim)
    return at & (BLOCK_LEN - 1), at >> 6


def fill_spread(spread_ref):
    t_r, j_r = tokens_of((128, 128), 0)
    t_c, j_c = tokens_of((128, 128), 1)
    rank = 2 * (t_r & 7) + j_r
    same = (t_r >> 3) == (t_c >> 3)
    for p in range(8):
        parts = [jnp.where(same & (rank == 2 * p + q), 1.0, 0.0) for q in range(2)]
        spread_ref[p] = jnp.concatenate(parts, 1).astype(BF16)


def odd_starts(width):
    return [j * BLOCK_LEN + t for j in range(2) for t in range(width, BLOCK_LEN, 2 * width)]


def odd_rows(x, width):
    return jnp.concatenate([x[s : s + width] for s in odd_starts(width)], 0)


def twice(high, low):
    row = jnp.concatenate([high, low], 1)
    return jnp.concatenate([row, row], 0)


def halves(x):
    return x[:, :128] + x[:, 128:]


def systems(blocks, heads_in, load, spread_ref):
    units = [(i, n) for i in range(heads_in) for n in range(blocks)]
    count = len(units)
    loaded = [load(i, n) for i, n in units]
    t_r, j_r = tokens_of((128, 128), 0)
    t_c, j_c = tokens_of((128, 128), 1)
    eye = (t_r == t_c) & (j_r == j_c)
    running = jnp.where((t_r <= t_c) & (j_r == 0), 1.0, 0.0).astype(BF16)
    decay = jnp.concatenate([u[1] for u in loaded], 0)
    beta = jnp.concatenate([u[2] for u in loaded], 0)
    total = dot(
        jnp.concatenate(split3(decay), 1).astype(BF16), jnp.concatenate([running] * 3, 0)
    )
    grams = [dot_t(u[0], u[0]) for u in loaded]
    squares = jnp.concatenate([jnp.sum(jnp.where(eye, g, 0.0), 0, keepdims=True) for g in grams], 0) + 1e-06
    inv = lax.rsqrt(squares)
    inv_log = -0.5 * jnp.log2(squares)
    fallen = total * LOG2E
    last = fallen[:, BLOCK_LEN - 1 : BLOCK_LEN]
    scale_k = jnp.exp2(fallen) * inv
    tail = jnp.exp2(last - fallen) * inv
    keep_all = jnp.exp2(last)
    ones = jnp.ones((count, 128), F32)
    zeros = jnp.zeros((count, 128), F32)
    stack = [*split3(fallen + inv_log), ones, ones, ones, *split3(beta), *split3(tail)]
    columns = jnp.transpose(jnp.concatenate(stack + [zeros] * (128 // count - len(stack)), 0)).astype(BF16)
    later = split3(inv_log - fallen)
    sub = lax.broadcasted_iota(jnp.int32, (count, 128), 0)

    lane_t, lane_j = tokens_of((8, 128), 1)
    row8 = lax.broadcasted_iota(jnp.int32, (8, 128), 0)
    in_block = [(lane_t >> 3) == b for b in range(8)]
    lane_rank = 2 * (lane_t & 7) + lane_j
    lower_0, lower_1 = 2 * row8 > lane_rank, 2 * row8 + 1 > lane_rank
    first_0 = jnp.where(2 * row8 == lane_rank, 1.0, 0.0)
    first_1 = jnp.where(2 * row8 + 1 == lane_rank, 1.0, 0.0)
    t16 = lax.broadcasted_iota(jnp.int32, (128, 128), 0) & (BLOCK_LEN - 1)
    own_block = jnp.where((t16 >> 3) == (t_c >> 3), 1.0, 0.0).astype(BF16)

    lows, tails, compact = [], [], []
    for u in range(count):
        pick = sub == u
        one = jnp.where(pick, 1.0, 0.0)
        right = [one] * 3 + [jnp.where(pick, g, 0.0) for g in later]
        none = [zeros]
        fill = 128 // count
        cols = [
            right + none * (fill - 6),
            none * 6 + [one] * 3 + none * (fill - 9),
            none * 9 + [one] * 3 + none * (fill - 12),
        ]
        right = jnp.concatenate([jnp.concatenate(c, 0) for c in cols], 1).astype(BF16)
        spread = dot(columns, right)
        low = grams[u] * jnp.exp2(spread[:, :128]) * spread[:, 128:256]
        lows.append(low)
        tails.append(spread[:, 256:])
        for j, lower in ((0, lower_0), (1, lower_1)):
            part = low[j * BLOCK_LEN : j * BLOCK_LEN + 8]
            for b in range(1, 8):
                at = j * BLOCK_LEN + 8 * b
                part = jnp.where(in_block[b], low[at : at + 8], part)
            compact.append(jnp.where(lower, part, 0.0))

    packed = wide(jnp.concatenate(compact, 0))
    pairs = [dot(packed, jnp.concatenate([spread_ref[p]] * 2, 0)) for p in range(8)]
    small = [[first_0, first_1] for _ in range(count)]
    for s in range(15):
        t, j, lanes = s // 2, s % 2, slice(128 * (s % 2), 128 * (s % 2) + 128)
        for u in range(count):
            x0, x1 = small[u]
            source = (x0, x1)[j][t : t + 1]
            coef = pairs[s // 2][16 * u : 16 * u + 16, lanes]
            small[u] = [x0 - coef[:8] * source, x1 - coef[8:] * source]

    highs, slims, updates = [], [], [[] for _ in range(count)]
    pair_of_8 = []
    for u in range(count):
        tiles = []
        for x in small[u]:
            both = jnp.concatenate([x, x], 0)
            tiles.append(split(both))
        high = jnp.concatenate([tiles[0][0]] * 4 + [tiles[1][0]] * 4, 0)
        slim = jnp.concatenate([tiles[0][1]] * 4 + [tiles[1][1]] * 4, 0)
        highs.append(high * own_block)
        slims.append(slim * own_block)
        pair_of_8.append(tiles)

    q = lax.broadcasted_iota(jnp.int32, (64, 128), 0) & 31
    c_t = lax.broadcasted_iota(jnp.int32, (64, 128), 1) & (BLOCK_LEN - 1)
    for width in (8, 16, 32):
        bits = width.bit_length()
        row_t = ((q >> (bits - 1)) << bits) + width + (q & (width - 1))
        mask = ((c_t & width) == 0) & ((c_t >> bits) == (row_t >> bits))
        if width == 8:
            odd_own = jnp.where((c_t >> 3) == (row_t >> 3), 1.0, 0.0).astype(BF16)
        parts = []
        for u in range(count):
            a = wide(jnp.where(mask, odd_rows(lows[u], width), 0.0))
            parts.append(halves(dot(a, twice(highs[u], slims[u]))))
        for u in range(count):
            p = parts[u]
            if width == 8:
                ph = p.astype(BF16).astype(F32)
                pl_ = p - ph
                doubled = [
                    jnp.concatenate([x[8 * (g // 2) : 8 * (g // 2) + 8] for g in range(16)], 0).astype(BF16)
                    for x in (ph, pl_)
                ]
                tiles = pair_of_8[u]
                odd = [jnp.concatenate([tiles[0][k]] * 2 + [tiles[1][k]] * 2, 0) * odd_own for k in range(2)]
            else:
                groups = range(64 // width)
                doubled = [
                    jnp.concatenate([x[width * g : width * g + width] for g in groups for _ in range(2)], 0)
                    for x in split(p)
                ]
                odd = [odd_rows(highs[u], width), odd_rows(slims[u], width)]
            update = halves(dot(jnp.concatenate(odd, 1), twice(*doubled)))
            updates[u].append(update)
            if width == 32:
                continue
            if width == 8:
                uh = update.astype(BF16).astype(F32)
                gap = jnp.zeros((8, 128), F32)
                spaced = [
                    jnp.concatenate(
                        [x[8 * (g // 2) : 8 * (g // 2) + 8] if g % 2 else gap for g in range(16)], 0
                    ).astype(BF16)
                    for x in (uh, update - uh)
                ]
            else:
                gap = jnp.zeros((width, 128), BF16)
                spaced = [
                    jnp.concatenate(
                        [
                            x[width * (g // 2) : width * (g // 2) + width] if g % 2 else gap
                            for g in range(128 // width)
                        ],
                        0,
                    )
                    for x in split(update)
                ]
            highs[u] = highs[u] - spaced[0]
            slims[u] = slims[u] - spaced[1]

    work = []
    for u in range(count):
        rows = []
        for j in range(2):
            for b in range(8):
                x = jnp.where(in_block[b], small[u][j], 0.0)
                for width, update in zip((8, 16, 32), updates[u]):
                    t = 8 * b
                    if t & width:
                        at = j * 32 + (t // (2 * width)) * width + t % width
                        x = x - update[at : at + 8]
                rows.append(x)
        at = slice(u, u + 1)
        inverse = jnp.concatenate(rows, 0)
        work.append((inverse, beta[at], scale_k[at], tails[u], keep_all[at], total[at], inv[at]))
    return work, jnp.where(eye, 1.0, 0.0)


def state_maps(blocks, heads_in, work, eye_f, load_kv, keep):
    states = [None] * heads_in
    for n in range(blocks):
        for i in range(heads_in):
            state = states[i]
            k_b, v_b = load_kv(i, n)
            inverse, beta_row, scale_k, tail, keep_all, c_row, ki_row = work[i * blocks + n]
            t = inverse * beta_row
            written = jnp.concatenate([mul_left(t * scale_k, k_b), mul_left(t, v_b)], 1)
            wh, wl = split(jnp.concatenate([written[:, :128] * tail, written[:, 128:] * tail], 1))
            k_t = jnp.transpose(k_b.astype(F32)).astype(BF16)
            made = dot(jnp.concatenate([k_t, k_t], 1), jnp.concatenate([wh, wl], 0))
            trans = keep_all * eye_f - made[:, :128]
            inject = made[:, 128:]
            keep(i, n, written, c_row, ki_row, state)
            if state is None:
                states[i] = jnp.concatenate([trans, inject], 1)
            else:
                states[i] = add_right(mul(trans, state), inject)
    return states


def reads(blocks, heads_in, load, emit):
    span = BLOCK_LEN
    row = lax.broadcasted_iota(jnp.int32, (span, 2 * span), 0)
    col = lax.broadcasted_iota(jnp.int32, (span, 2 * span), 1)
    col_t = col & (span - 1)
    seen = col_t <= row
    for i, n in [(i, n) for i in range(heads_in) for n in range(blocks)]:
        q_b, k_b, d_row, written, c_row, ki_row, state = load(i, n)
        c_col = jnp.sum(jnp.where(seen & (col < span), d_row, 0.0), 1, keepdims=True)
        q_f = q_b.astype(F32)
        qi_col = lax.rsqrt(jnp.sum(q_f * q_f, 1, keepdims=True) + 1e-06)
        fall = jnp.exp(jnp.minimum(c_col - c_row, 0.0))
        reach = jnp.where(seen, dot_t(q_b, k_b) * qi_col * ki_row * fall, 0.0)
        query = q_f * (qi_col * jnp.exp(c_col))
        got = mul(reach, written)
        reduced, local_out = query - got[:, :128], got[:, 128:]
        if n == 0:
            emit(i, n, reduced, local_out)
        else:
            read = mul(reduced, state)
            emit(i, n, read[:, :128], read[:, 128:] + local_out)


def whole_kernel(
    inner, outer, q_hbm, k_hbm, v_hbm, small_ref, o_ref,
    spread_buf, q_buf, k_buf, v_buf, w_buf, p_buf, vec_buf,
    away, near, own, even_map, sent, got, groups, mine, ready, came, aside, beside, c_buf, b_buf,
    load_k, load_v, load_q,
    send0, recv0, send1, recv1, send2, recv2, send3, recv3, send4, recv4, send5, recv5,
):
    mesh_id = pl.DeviceIdType.MESH
    length = q_hbm.shape[0]
    blocks = length // BLOCK_LEN
    me = lax.axis_index("inner")
    group = lax.axis_index("outer")
    core, chip, chips = me % 2, me // 2, inner // 2
    partner = chip * 2 + 1 - core
    groups[...] = jnp.zeros_like(groups)
    barrier = pltpu.get_barrier_semaphore()
    for d in range(1, chips):
        pl.semaphore_signal(
            barrier, inc=1, device_id=(group, (chip + d) % chips * 2 + core), device_id_type=mesh_id
        )
    pl.semaphore_signal(barrier, inc=1, device_id=(group, partner), device_id_type=mesh_id)
    for d in range(1, outer):
        pl.semaphore_signal(barrier, inc=1, device_id=((group + d) % outer, me), device_id_type=mesh_id)

    def target(turn):
        return (chip + turn + 1) % chips

    def lanes_of(turn):
        return pl.ds(pl.multiple_of(target(turn) * 256, 256), 256)

    def k_copy(turn):
        return pltpu.make_async_copy(k_hbm.at[:, :, lanes_of(turn)], k_buf.at[turn], load_k.at[turn])

    def v_copy(turn):
        return pltpu.make_async_copy(v_hbm.at[:, :, lanes_of(turn)], v_buf.at[turn], load_v.at[turn])

    def q_copy(turn):
        return pltpu.make_async_copy(q_hbm.at[:, lanes_of(turn)], q_buf.at[turn], load_q.at[turn])

    for t in range(chips):
        k_copy(t).start()
        v_copy(t).start()
    for t in range(chips):
        q_copy(t).start()

    fill_spread(spread_buf)

    def near_copy(turn):
        return pltpu.make_async_remote_copy(
            src_ref=away.at[turn], dst_ref=near.at[turn],
            send_sem=send0.at[turn], recv_sem=recv0.at[turn],
            device_id=(group, partner), device_id_type=mesh_id,
        )

    def map_copy(d):
        return pltpu.make_async_remote_copy(
            src_ref=sent.at[d], dst_ref=got.at[d],
            send_sem=send1.at[d], recv_sem=recv1.at[d],
            device_id=(group, (chip + d) % chips * 2 + core), device_id_type=mesh_id,
        )

    def chip_map(turn):
        near_copy(turn).wait()
        here, there = own[turn], near[turn]
        even = jnp.where(core == 0, here, there)
        odd = jnp.where(core == 0, there, here)
        even_map[turn] = even
        return then(even, odd)

    def parity(i):
        return core if i == 0 else 1 - core

    def head_lanes(i):
        return pl.ds(pl.multiple_of(parity(i) * 128, 128), 128)

    def rows_of(head, n):
        at = slice(n * BLOCK_LEN, (n + 1) * BLOCK_LEN)
        row = pl.ds(head, 1)
        b0, b1 = small_ref[0, row, :][:, at], small_ref[1, row, :][:, at]
        d = small_ref[2, row, :][:, at]
        return jnp.concatenate([d, d], 1), jnp.concatenate([b0, b1], 1)

    def pair_of(buf, turn, i, n):
        at = pl.ds(n * BLOCK_LEN, BLOCK_LEN)
        return jnp.concatenate([buf[turn, 0, at, head_lanes(i)], buf[turn, 1, at, head_lanes(i)]], 0)

    def step(turn, carry):
        heads = [target(turn) * 2 + parity(i) for i in range(2)]
        k_copy(turn).wait()

        def load(i, n):
            d_row, beta_row = rows_of(heads[i], n)
            return pair_of(k_buf, turn, i, n), d_row, beta_row

        work, eye_f = systems(blocks, 2, load, spread_buf)

        @pl.when(turn == 0)
        def _():
            pl.semaphore_wait(barrier, chips + outer - 1)

        @pl.when(turn > 0)
        def _():
            sent[turn] = chip_map(turn - 1)
            map_copy(turn).start()

        v_copy(turn).wait()

        def load_kv(i, n):
            return pair_of(k_buf, turn, i, n), pair_of(v_buf, turn, i, n)

        def keep(i, n, written, c_row, ki_row, state):
            w_buf[turn, i, n] = written
            vec_buf[turn, i, n, 0:1, :] = c_row
            vec_buf[turn, i, n, 1:2, :] = ki_row
            if n:
                p_buf[turn, i, n] = state

        states = state_maps(blocks, 2, work, eye_f, load_kv, keep)
        away[turn] = states[1]
        own[turn] = states[0]

        near_copy(turn).start()
        return carry

    lax.fori_loop(0, chips, step, 0)

    def read_step(turn, carry):
        heads = [target(turn) * 2 + parity(i) for i in range(2)]
        q_copy(turn).wait()

        def load(i, n):
            at = pl.ds(n * BLOCK_LEN, BLOCK_LEN)
            d_row, _ = rows_of(heads[i], n)
            return (
                q_buf[turn, at, head_lanes(i)], pair_of(k_buf, turn, i, n), d_row, w_buf[turn, i, n],
                vec_buf[turn, i, n, 0:1, :], vec_buf[turn, i, n, 1:2, :], p_buf[turn, i, n] if n else None,
            )

        def emit(i, n, carried, base):
            at = pl.ds(n * BLOCK_LEN, BLOCK_LEN)
            c_buf[turn, i, at, :] = carried
            b_buf[turn, i, at, :] = base

        reads(blocks, 2, load, emit)
        return carry

    lax.fori_loop(0, chips // 2, read_step, 0)
    got[0] = chip_map(chips - 1)
    for d in range(1, chips):
        map_copy(d).wait()

    maps = [got[(chip - i + chips) % chips] for i in range(chips)]

    def tree(parts):
        if len(parts) == 1:
            return parts
        half = len(parts) // 2
        pairs = [then(parts[2 * i], parts[2 * i + 1]) for i in range(half)]
        return pairs

    level = maps
    levels = [maps]
    while len(level) > 1:
        level = tree(level)
        levels.append(level)
    mine[0] = level[0][:, :128]
    mine[1] = level[0][:, 128:]

    def group_copy(part, d):
        sems = (send2, recv2) if part == 0 else (send5, recv5)
        return pltpu.make_async_remote_copy(
            src_ref=mine.at[part], dst_ref=groups.at[part, d],
            send_sem=sems[0].at[d], recv_sem=sems[1].at[d],
            device_id=((group + d) % outer, me), device_id_type=mesh_id,
        )

    for d in range(outer - 1, 0, -1):

        @pl.when(group + d < outer)
        def _():
            group_copy(1, d).start()

    for d in range(outer - 1, 0, -1):

        @pl.when((group + d < outer) & (group > 0))
        def _():
            group_copy(0, d).start()

    before = {}
    for i in range(1, chips):
        low = i & -i
        height = low.bit_length() - 1
        part = levels[height][(i - low) >> height]
        before[i] = part if i == low else then(before[i - low], part)
    left = wide(jnp.concatenate([before[i][:, :128] for i in range(1, chips)], 0))
    right = jnp.concatenate([before[i][:, 128:] for i in range(1, chips)], 0)

    lax.fori_loop(chips // 2, chips, read_step, 0)

    for d in range(1, outer):

        @pl.when(group + d < outer)
        def _():
            group_copy(1, d).wait_send()

        @pl.when((group + d < outer) & (group > 0))
        def _():
            group_copy(0, d).wait_send()

        @pl.when(group - d >= 0)
        def _():
            group_copy(1, d).wait_recv()

        @pl.when(group - d > 0)
        def _():
            group_copy(0, d).wait_recv()

    start = jnp.zeros((128, 128), F32)
    for g in range(outer - 1):
        at = (group - g + outer) % outer
        moved = groups[1, at]
        if g:
            moved = mul(groups[0, at], start) + moved
        start = jnp.where(g < group, moved, start)

    sh, sl = split(start)
    row = jnp.concatenate([sh, sl], 1)
    both = dot(left, jnp.concatenate([row, row], 0))
    ready[0] = start
    ready[pl.ds(1, chips - 1)] = (both[:, :128] + both[:, 128:] + right).reshape(chips - 1, 128, 128)

    def back_copy(d):
        to = (chip + d) % chips
        return pltpu.make_async_remote_copy(
            src_ref=ready.at[to], dst_ref=came.at[d],
            send_sem=send3.at[d], recv_sem=recv3.at[d],
            device_id=(group, to * 2 + core), device_id_type=mesh_id,
        )

    def side_copy(d):
        return pltpu.make_async_remote_copy(
            src_ref=aside.at[d], dst_ref=beside.at[d],
            send_sem=send4.at[d], recv_sem=recv4.at[d],
            device_id=(group, partner), device_id_type=mesh_id,
        )

    for d in range(1, chips):
        back_copy(d).start()

    def out(turn, i, state):
        head = target(turn) * 2 + parity(i)
        lanes = pl.ds(pl.multiple_of(head * 128, 128), 128)
        o_ref[:, lanes] = normed(c_buf[turn, i], b_buf[turn, i], state, small_ref[3, 0:1, :128])

    for d in range(chips):
        turn = chips - 1 - d
        if d:
            back_copy(d).wait()
            enter = came[d]
        else:
            enter = ready[chip]
        pair = even_map[turn]
        after = mul(pair[:, :128], enter) + pair[:, 128:]
        aside[d] = jnp.where(core == 0, after, enter)
        side_copy(d).start()
        out(turn, 0, jnp.where(core == 0, enter, after))
        if d:
            side_copy(d - 1).wait()
            out(turn + 1, 1, beside[d - 1])
    side_copy(chips - 1).wait()
    out(0, 1, beside[chips - 1])


def whole(inner, outer, queries, keys, values, betas, log_decay, out_gain):
    length, width = queries.shape
    blocks = length // BLOCK_LEN
    chips = inner // 2
    gain = jnp.pad(out_gain[None, :], ((0, inner - 1), (0, length - 128)))
    small = jnp.concatenate([betas, log_decay[None], gain[None]], 0)
    vmem = pl.BlockSpec(memory_space=pltpu.VMEM)
    hbm = pl.BlockSpec(memory_space=pltpu.HBM)
    dma = pltpu.SemaphoreType.DMA
    return pl.pallas_call(
        functools.partial(whole_kernel, inner, outer),
        in_specs=[hbm] * 3 + [vmem],
        out_specs=vmem,
        out_shape=jax.ShapeDtypeStruct((length, width), BF16),
        scratch_shapes=[
            pltpu.VMEM((8, 128, 256), BF16),
            pltpu.VMEM((chips, length, 256), BF16),
            *[pltpu.VMEM((chips, 2, length, 256), BF16)] * 2,
            *[pltpu.VMEM((chips, 2, blocks, 128, 256), F32)] * 2,
            pltpu.VMEM((chips, 2, blocks, 8, 128), F32),
            *[pltpu.VMEM((chips, 128, 256), F32)] * 6,
            pltpu.VMEM((2, outer, 128, 128), F32),
            pltpu.VMEM((2, 128, 128), F32),
            *[pltpu.VMEM((chips, 128, 128), F32)] * 4,
            *[pltpu.VMEM((chips, 2, length, 128), F32)] * 2,
            *[dma((chips,))] * 3,
            *[dma((chips,))] * 4,
            *[dma((outer,))] * 2,
            *[dma((chips,))] * 4,
            *[dma((outer,))] * 2,
        ],
        compiler_params=pltpu.CompilerParams(
            collective_id=0, has_side_effects=True, vmem_limit_bytes=53 * 1024 * 1024
        ),
        name="whole",
    )(queries, keys, values, small)


HIGHEST = lax.Precision.HIGHEST


def join(earlier, later):
    moved = jnp.einsum("hde,hef->hdf", later[..., :128], earlier, precision=HIGHEST)
    return jnp.concatenate([moved[..., :128], moved[..., 128:] + later[..., 128:]], -1)


def entering(pairs, axis, begin):
    gathered = lax.all_gather(pairs, axis)

    def one(hop, state):
        return join(state, lax.dynamic_index_in_dim(gathered, hop, 0, False))

    return lax.fori_loop(0, lax.axis_index(axis), one, begin)


def exchange_plain(pairs):
    eye = jnp.concatenate([jnp.eye(128, dtype=F32), jnp.zeros((128, 128), F32)], 1)
    begin = jnp.zeros_like(pairs) + eye
    before = entering(pairs, "inner", begin)
    through = join(before, pairs)
    last = lax.axis_index("inner") == lax.axis_size("inner") - 1
    total = lax.psum(jnp.where(last, through, 0.0), "inner")
    start = entering(total, "outer", begin)
    return join(start, before)[..., 128:]


def finish_kernel(c_ref, b_ref, e_ref, g_ref, o_ref):
    readout = mul(c_ref[0], e_ref[0]) + b_ref[0]
    mean_sq = jnp.mean(readout * readout, 1, keepdims=True)
    o_ref[...] = (readout * lax.rsqrt(mean_sq + 1e-05) * g_ref[...]).astype(BF16)


def finish(carried, base, state, out_gain):
    heads, length, _ = carried.shape
    return pl.pallas_call(
        finish_kernel,
        grid=(heads,),
        in_specs=[
            pl.BlockSpec((1, length, 128), lambda h: (h, 0, 0)),
            pl.BlockSpec((1, length, 128), lambda h: (h, 0, 0)),
            pl.BlockSpec((1, 128, 128), lambda h: (h, 0, 0)),
            pl.BlockSpec((1, 128), lambda h: (0, 0)),
        ],
        out_specs=pl.BlockSpec((length, 128), lambda h: (0, h)),
        out_shape=jax.ShapeDtypeStruct((length, heads * 128), BF16),
        name="finish",
    )(carried, base, state, out_gain.reshape(1, 128))


def per_device(inner, outer, queries, keys, values, betas, log_decay, out_gain):
    heads = betas.shape[1]
    if inner == heads:
        return whole(inner, outer, queries, keys, values, betas, log_decay, out_gain)
    pairs, carried, base = local_phase(queries, keys, values, betas, log_decay)
    return finish(carried, base, exchange_plain(pairs), out_gain)


def solution(mesh):
    both = ("outer", "inner")
    placed = (P(both, None), P(None, both, None), P(None, both, None), P(None, None, both), P(None, both), P())
    return jax.shard_map(
        functools.partial(per_device, mesh.shape["inner"], mesh.shape["outer"]),
        mesh=mesh,
        in_specs=placed,
        out_specs=P(both, None),
        check_vma=False,
    )
```

```python
import functools

import jax
import jax.numpy as jnp
from jax import lax
from jax.experimental import pallas as pl
from jax.experimental.pallas import tpu as pltpu
from jax.sharding import PartitionSpec as P

BLOCK_LEN = 64
F32 = jnp.float32
BF16 = jnp.bfloat16


def split(x):
    high = x.astype(BF16)
    low = (x - high.astype(F32)).astype(BF16)
    return high, low


def dot(a, b):
    return lax.dot_general(a, b, (((1,), (0,)), ((), ())), preferred_element_type=F32)


def dot_t(a, b):
    return lax.dot_general(a, b, (((1,), (1,)), ((), ())), preferred_element_type=F32)


def wide(x):
    return jnp.concatenate(split(x), 1)


def mul(a, b):
    a2 = wide(a)
    bh, bl = split(b)
    if b.shape[1] == 128:
        row = jnp.concatenate([bh, bl], 1)
        both = dot(a2, jnp.concatenate([row, row], 0))
        return both[:, :128] + both[:, 128:]
    return dot(a2, jnp.concatenate([bh, bh], 0)) + dot(a2[:, :128], bl)


def mul_left(a, b):
    return dot(wide(a), jnp.concatenate([b, b], 0))


def add_right(x, y):
    return jnp.concatenate([x[:, :128], x[:, 128:] + y], 1)


def masks():
    span = BLOCK_LEN
    size = 2 * span
    row = lax.broadcasted_iota(jnp.int32, (size, size), 0)
    col = lax.broadcasted_iota(jnp.int32, (size, size), 1)
    row_t, col_t = row & (span - 1), col & (span - 1)
    row_rank = 2 * row_t + (row >= span).astype(jnp.int32)
    col_rank = 2 * col_t + (col >= span).astype(jnp.int32)
    differ = row_rank ^ col_rank
    eye = row == col
    eye_f = eye.astype(F32)
    lower = row_rank > col_rank
    c_mask = (col_t <= row_t) & (col < span)
    r_mask = (row_t <= col_t) & (row < span)
    levels = []
    width = 1
    while width < size:
        levels.append(
            (differ >= width) & (differ < 2 * width) & lower
        )
        width *= 2

    return row, col_t, row_t, eye, eye_f, lower, c_mask, r_mask, levels


def head_maps(blocks, heads_in, load, emit):
    span = BLOCK_LEN
    row, col_t, row_t, eye, eye_f, lower, c_mask, r_mask, levels = masks()
    work = []
    for i, n in [(i, n) for i in range(heads_in) for n in range(blocks)]:
        q_b, k_b, v_b, d_row, beta_row = load(i, n)
        d_col = jnp.sum(jnp.where(eye, d_row, 0.0), 1, keepdims=True)
        beta_col = jnp.sum(jnp.where(eye, beta_row, 0.0), 1, keepdims=True)
        c_col = jnp.sum(jnp.where(c_mask, d_row, 0.0), 1, keepdims=True)
        c_row = jnp.sum(jnp.where(r_mask, d_col, 0.0), 0, keepdims=True)
        gram = dot_t(k_b, k_b)
        k_f = k_b.astype(F32)
        q_f = q_b.astype(F32)
        ki_col = lax.rsqrt(jnp.sum(k_f * k_f, 1, keepdims=True) + 1e-06)
        ki_row = lax.rsqrt(jnp.sum(jnp.where(eye, gram, 0.0), 0, keepdims=True) + 1e-06)
        qi_col = lax.rsqrt(jnp.sum(q_f * q_f, 1, keepdims=True) + 1e-06)
        fall = jnp.exp(jnp.minimum(c_col - c_row, 0.0))
        low = jnp.where(lower, gram * (beta_col * ki_col) * ki_row * fall, 0.0)
        reach = dot_t(q_b, k_b) * qi_col * ki_row * fall[:span]
        reach = jnp.where(col_t[:span] <= row_t[:span], reach, 0.0)
        query = q_f * (qi_col * jnp.exp(c_col[:span]))
        work.append((k_b, v_b, beta_row, c_row, c_col, ki_row, ki_col, low, reach, query))

    inverse = [eye_f - jnp.where(levels[0], w[7], 0.0) for w in work]
    for mask in levels[1:]:
        part = [mul(jnp.where(mask, w[7], 0.0), t) for w, t in zip(work, inverse)]
        inverse = [t - mul(t, p) for t, p in zip(inverse, part)]

    states = [None] * heads_in
    for n in range(blocks):
        for i in range(heads_in):
            state = states[i]
            k_b, v_b, beta_row, c_row, c_col, ki_row, ki_col, low, reach, query = work[i * blocks + n]
            t = inverse[i * blocks + n] * beta_row
            written = jnp.concatenate(
                [mul_left(t * (ki_row * jnp.exp(c_row)), k_b), mul_left(t, v_b)], 1
            )
            got = mul(reach, written)
            reduced, local_out = query - got[:, :128], got[:, 128:]
            last = c_col[span - 1 : span, :]
            tail = jnp.exp(last - c_col) * ki_col
            wh, wl = split(written * tail)
            k_t = jnp.transpose(k_b.astype(F32)).astype(BF16)
            made = dot(jnp.concatenate([k_t, k_t], 1), jnp.concatenate([wh, wl], 0))
            trans = jnp.exp(last) * eye_f - made[:, :128]
            inject = made[:, 128:]
            if state is None:
                emit(i, n, reduced, local_out)
                states[i] = jnp.concatenate([trans, inject], 1)
            else:
                read = mul(reduced, state)
                emit(i, n, read[:, :128], read[:, 128:] + local_out)
                states[i] = add_right(mul(trans, state), inject)
    return states


def local_kernel(blocks, q_ref, k_ref, v_ref, s_ref, x_ref, c_ref, b_ref):
    def load(i, n):
        at = pl.ds(n * BLOCK_LEN, BLOCK_LEN)
        k_b = jnp.concatenate([k_ref[0, at, :], k_ref[1, at, :]], 0)
        v_b = jnp.concatenate([v_ref[0, at, :], v_ref[1, at, :]], 0)
        return q_ref[at, :], k_b, v_b, s_ref[0, n : n + 1, :], s_ref[0, blocks + n : blocks + n + 1, :]

    def emit(i, n, carried, base):
        at = pl.ds(n * BLOCK_LEN, BLOCK_LEN)
        c_ref[0, at, :] = carried
        b_ref[0, at, :] = base

    x_ref[0] = head_maps(blocks, 1, load, emit)[0]


def small_rows(betas, log_decay):
    heads, length = log_decay.shape
    blocks = length // BLOCK_LEN
    beta = betas.reshape(2, heads, blocks, BLOCK_LEN).transpose(1, 2, 0, 3)
    beta = beta.reshape(heads, blocks, 2 * BLOCK_LEN)
    decay = log_decay.reshape(heads, blocks, 1, BLOCK_LEN)
    decay = jnp.concatenate([decay, decay], 2).reshape(heads, blocks, 2 * BLOCK_LEN)
    small = jnp.concatenate([decay, beta], 1)
    return small


def local_phase(queries, keys, values, betas, log_decay):
    length = queries.shape[0]
    heads = betas.shape[1]
    blocks = length // BLOCK_LEN
    small = small_rows(betas, log_decay)
    return pl.pallas_call(
        functools.partial(local_kernel, blocks),
        grid=(heads,),
        in_specs=[
            pl.BlockSpec((length, 128), lambda h: (0, h)),
            pl.BlockSpec((2, length, 128), lambda h: (0, 0, h)),
            pl.BlockSpec((2, length, 128), lambda h: (0, 0, h)),
            pl.BlockSpec((1, 2 * blocks, 128), lambda h: (h, 0, 0)),
        ],
        out_specs=[
            pl.BlockSpec((1, 128, 256), lambda h: (h, 0, 0)),
            pl.BlockSpec((1, length, 128), lambda h: (h, 0, 0)),
            pl.BlockSpec((1, length, 128), lambda h: (h, 0, 0)),
        ],
        out_shape=[
            jax.ShapeDtypeStruct((heads, 128, 256), F32),
            jax.ShapeDtypeStruct((heads, length, 128), F32),
            jax.ShapeDtypeStruct((heads, length, 128), F32),
        ],
        name="local_phase",
    )(queries, keys, values, small)


def then(earlier, later):
    return add_right(mul(later[:, :128], earlier), later[:, 128:])


def normed(carried, base, state, gain):
    readout = mul(carried, state) + base
    mean_sq = jnp.mean(readout * readout, 1, keepdims=True)
    return (readout * lax.rsqrt(mean_sq + 1e-05) * gain).astype(BF16)


LOG2E = 1.4426950408889634


def split3(x):
    high = x.astype(BF16)
    rest = x - high.astype(F32)
    mid = rest.astype(BF16)
    low = rest - mid.astype(F32)
    return high.astype(F32), mid.astype(F32), low


def tokens_of(shape, dim):
    at = lax.broadcasted_iota(jnp.int32, shape, dim)
    return at & (BLOCK_LEN - 1), at >> 6


def fill_spread(spread_ref):
    t_r, j_r = tokens_of((128, 128), 0)
    t_c, j_c = tokens_of((128, 128), 1)
    rank = 2 * (t_r & 7) + j_r
    same = (t_r >> 3) == (t_c >> 3)
    for p in range(8):
        parts = [jnp.where(same & (rank == 2 * p + q), 1.0, 0.0) for q in range(2)]
        spread_ref[p] = jnp.concatenate(parts, 1).astype(BF16)


def odd_starts(width):
    return [j * BLOCK_LEN + t for j in range(2) for t in range(width, BLOCK_LEN, 2 * width)]


def odd_rows(x, width):
    return jnp.concatenate([x[s : s + width] for s in odd_starts(width)], 0)


def stacked(left, right):
    rows = left[0].shape[0]
    both = dot(jnp.concatenate(left, 0), jnp.concatenate(right, 1))
    return both[:rows, :128] + (both[:rows, 128:] + both[rows:, :128])


def systems(blocks, heads_in, load, spread_ref):
    units = [(i, n) for i in range(heads_in) for n in range(blocks)]
    count = len(units)
    loaded = [load(i, n) for i, n in units]
    t_r, j_r = tokens_of((128, 128), 0)
    t_c, j_c = tokens_of((128, 128), 1)
    eye = (t_r == t_c) & (j_r == j_c)
    running = jnp.where((t_r <= t_c) & (j_r == 0), 1.0, 0.0).astype(BF16)
    decay = jnp.concatenate([u[1] for u in loaded], 0)
    beta = jnp.concatenate([u[2] for u in loaded], 0)
    total = dot(
        jnp.concatenate(split3(decay), 1).astype(BF16), jnp.concatenate([running] * 3, 0)
    )
    grams = [dot_t(u[0], u[0]) for u in loaded]
    squares = jnp.concatenate([jnp.sum(jnp.where(eye, g, 0.0), 0, keepdims=True) for g in grams], 0) + 1e-06
    inv = lax.rsqrt(squares)
    inv_log = -0.5 * jnp.log2(squares)
    fallen = total * LOG2E
    last = fallen[:, BLOCK_LEN - 1 : BLOCK_LEN]
    scale_k = jnp.exp2(fallen) * inv
    tail = jnp.exp2(last - fallen) * inv
    keep_all = jnp.exp2(last)
    ones = jnp.ones((count, 128), F32)
    zeros = jnp.zeros((count, 128), F32)
    stack = [*split3(fallen + inv_log), ones, ones, ones, *split3(beta), *split3(tail)]
    columns = jnp.transpose(jnp.concatenate(stack + [zeros] * (128 // count - len(stack)), 0)).astype(BF16)
    later = split3(inv_log - fallen)
    sub = lax.broadcasted_iota(jnp.int32, (count, 128), 0)

    lane_t, lane_j = tokens_of((8, 128), 1)
    row8 = lax.broadcasted_iota(jnp.int32, (8, 128), 0)
    in_block = [(lane_t >> 3) == b for b in range(8)]
    lane_rank = 2 * (lane_t & 7) + lane_j
    lower_0, lower_1 = 2 * row8 > lane_rank, 2 * row8 + 1 > lane_rank
    first_0 = jnp.where(2 * row8 == lane_rank, 1.0, 0.0)
    first_1 = jnp.where(2 * row8 + 1 == lane_rank, 1.0, 0.0)
    t16 = lax.broadcasted_iota(jnp.int32, (128, 128), 0) & (BLOCK_LEN - 1)
    own_block = jnp.where((t16 >> 3) == (t_c >> 3), 1.0, 0.0).astype(BF16)

    lows, tails, compact = [], [], []
    for u in range(count):
        pick = sub == u
        one = jnp.where(pick, 1.0, 0.0)
        right = [one] * 3 + [jnp.where(pick, g, 0.0) for g in later]
        none = [zeros]
        fill = 128 // count
        cols = [
            right + none * (fill - 6),
            none * 6 + [one] * 3 + none * (fill - 9),
            none * 9 + [one] * 3 + none * (fill - 12),
        ]
        right = jnp.concatenate([jnp.concatenate(c, 0) for c in cols], 1).astype(BF16)
        spread = dot(columns, right)
        low = grams[u] * jnp.exp2(spread[:, :128]) * spread[:, 128:256]
        lows.append(low)
        tails.append(spread[:, 256:])
        for j, lower in ((0, lower_0), (1, lower_1)):
            part = low[j * BLOCK_LEN : j * BLOCK_LEN + 8]
            for b in range(1, 8):
                at = j * BLOCK_LEN + 8 * b
                part = jnp.where(in_block[b], low[at : at + 8], part)
            compact.append(jnp.where(lower, part, 0.0))

    packed = wide(jnp.concatenate(compact, 0))
    pairs = [dot(packed, jnp.concatenate([spread_ref[p]] * 2, 0)) for p in range(8)]
    small = [[first_0, first_1] for _ in range(count)]
    for s in range(15):
        t, j, lanes = s // 2, s % 2, slice(128 * (s % 2), 128 * (s % 2) + 128)
        for u in range(count):
            x0, x1 = small[u]
            source = (x0, x1)[j][t : t + 1]
            coef = pairs[s // 2][16 * u : 16 * u + 16, lanes]
            small[u] = [x0 - coef[:8] * source, x1 - coef[8:] * source]

    highs, slims, updates = [], [], [[] for _ in range(count)]
    pair_of_8 = []
    for u in range(count):
        tiles = []
        for x in small[u]:
            both = jnp.concatenate([x, x], 0)
            tiles.append(split(both))
        high = jnp.concatenate([tiles[0][0]] * 4 + [tiles[1][0]] * 4, 0)
        slim = jnp.concatenate([tiles[0][1]] * 4 + [tiles[1][1]] * 4, 0)
        highs.append(high * own_block)
        slims.append(slim * own_block)
        pair_of_8.append(tiles)

    q = lax.broadcasted_iota(jnp.int32, (64, 128), 0) & 31
    c_t = lax.broadcasted_iota(jnp.int32, (64, 128), 1) & (BLOCK_LEN - 1)
    for width in (8, 16, 32):
        bits = width.bit_length()
        row_t = ((q >> (bits - 1)) << bits) + width + (q & (width - 1))
        mask = ((c_t & width) == 0) & ((c_t >> bits) == (row_t >> bits))
        if width == 8:
            odd_own = jnp.where((c_t >> 3) == (row_t >> 3), 1.0, 0.0).astype(BF16)
        parts = []
        for u in range(count):
            a = split(jnp.where(mask, odd_rows(lows[u], width), 0.0))
            parts.append(stacked(a, (highs[u], slims[u])))
        for u in range(count):
            p = parts[u]
            if width == 8:
                ph = p.astype(BF16).astype(F32)
                pl_ = p - ph
                doubled = [
                    jnp.concatenate([x[8 * (g // 2) : 8 * (g // 2) + 8] for g in range(16)], 0).astype(BF16)
                    for x in (ph, pl_)
                ]
                tiles = pair_of_8[u]
                odd = [jnp.concatenate([tiles[0][k]] * 2 + [tiles[1][k]] * 2, 0) * odd_own for k in range(2)]
            else:
                groups = range(64 // width)
                doubled = [
                    jnp.concatenate([x[width * g : width * g + width] for g in groups for _ in range(2)], 0)
                    for x in split(p)
                ]
                odd = [odd_rows(highs[u], width), odd_rows(slims[u], width)]
            update = stacked(odd, doubled)
            updates[u].append(update)
            if width == 32:
                continue
            if width == 8:
                uh = update.astype(BF16).astype(F32)
                gap = jnp.zeros((8, 128), F32)
                spaced = [
                    jnp.concatenate(
                        [x[8 * (g // 2) : 8 * (g // 2) + 8] if g % 2 else gap for g in range(16)], 0
                    ).astype(BF16)
                    for x in (uh, update - uh)
                ]
            else:
                gap = jnp.zeros((width, 128), BF16)
                spaced = [
                    jnp.concatenate(
                        [
                            x[width * (g // 2) : width * (g // 2) + width] if g % 2 else gap
                            for g in range(128 // width)
                        ],
                        0,
                    )
                    for x in split(update)
                ]
            highs[u] = highs[u] - spaced[0]
            slims[u] = slims[u] - spaced[1]

    work = []
    for u in range(count):
        rows = []
        for j in range(2):
            for b in range(8):
                x = jnp.where(in_block[b], small[u][j], 0.0)
                for width, update in zip((8, 16, 32), updates[u]):
                    t = 8 * b
                    if t & width:
                        at = j * 32 + (t // (2 * width)) * width + t % width
                        x = x - update[at : at + 8]
                rows.append(x)
        at = slice(u, u + 1)
        inverse = jnp.concatenate(rows, 0)
        work.append((inverse, beta[at], scale_k[at], tails[u], keep_all[at], total[at], inv[at]))
    return work, jnp.where(eye, 1.0, 0.0)


def state_maps(blocks, heads_in, work, eye_f, load_kv, keep):
    units = [(i, n) for n in range(blocks) for i in range(heads_in)]
    wrote, pieces = {}, {}
    for i, n in units:
        k_b, v_b = load_kv(i, n)
        inverse, beta_row, scale_k = work[i * blocks + n][:3]
        t = inverse * beta_row
        wrote[i, n] = mul_left(t * scale_k, k_b), mul_left(t, v_b)
    for i, n in units:
        k_b, _ = load_kv(i, n)
        tail, keep_all = work[i * blocks + n][3:5]
        wk, wv = wrote[i, n]
        wh, wl = split(jnp.concatenate([wk * tail, wv * tail], 1))
        k_t = jnp.transpose(k_b.astype(F32)).astype(BF16)
        made = dot(jnp.concatenate([k_t, k_t], 1), jnp.concatenate([wh, wl], 0))
        pieces[i, n] = jnp.concatenate([keep_all * eye_f - made[:, :128], made[:, 128:]], 1)
    states = [None] * heads_in
    for i, n in units:
        c_row, ki_row = work[i * blocks + n][5:7]
        keep(i, n, jnp.concatenate(wrote[i, n], 1), c_row, ki_row, states[i])
        states[i] = pieces[i, n] if n == 0 else then(states[i], pieces[i, n])
    return states


def reads(blocks, heads_in, load, emit):
    span = BLOCK_LEN
    row = lax.broadcasted_iota(jnp.int32, (span, 2 * span), 0)
    col = lax.broadcasted_iota(jnp.int32, (span, 2 * span), 1)
    col_t = col & (span - 1)
    seen = col_t <= row
    for i, n in [(i, n) for i in range(heads_in) for n in range(blocks)]:
        q_b, k_b, d_row, written, c_row, ki_row, state = load(i, n)
        c_col = jnp.sum(jnp.where(seen & (col < span), d_row, 0.0), 1, keepdims=True)
        q_f = q_b.astype(F32)
        qi_col = lax.rsqrt(jnp.sum(q_f * q_f, 1, keepdims=True) + 1e-06)
        fall = jnp.exp(jnp.minimum(c_col - c_row, 0.0))
        reach = jnp.where(seen, dot_t(q_b, k_b) * qi_col * ki_row * fall, 0.0)
        query = q_f * (qi_col * jnp.exp(c_col))
        got = mul(reach, written)
        reduced, local_out = query - got[:, :128], got[:, 128:]
        if n == 0:
            emit(i, n, reduced, local_out)
        else:
            read = mul(reduced, state)
            emit(i, n, read[:, :128], read[:, 128:] + local_out)


def whole_kernel(
    inner, outer, q_hbm, k_hbm, v_hbm, small_ref, o_ref,
    spread_buf, q_buf, k_buf, v_buf, w_buf, p_buf, vec_buf,
    away, near, own, even_map, sent, got, groups, mine, ready, came, aside, beside, c_buf, b_buf,
    load_k, load_v, load_q,
    send0, recv0, send1, recv1, send2, recv2, send3, recv3, send4, recv4, send5, recv5,
):
    mesh_id = pl.DeviceIdType.MESH
    length = q_hbm.shape[0]
    blocks = length // BLOCK_LEN
    me = lax.axis_index("inner")
    group = lax.axis_index("outer")
    core, chip, chips = me % 2, me // 2, inner // 2
    partner = chip * 2 + 1 - core
    groups[...] = jnp.zeros_like(groups)
    barrier = pltpu.get_barrier_semaphore()
    for d in range(1, chips):
        pl.semaphore_signal(
            barrier, inc=1, device_id=(group, (chip + d) % chips * 2 + core), device_id_type=mesh_id
        )
    pl.semaphore_signal(barrier, inc=1, device_id=(group, partner), device_id_type=mesh_id)
    for d in range(1, outer):
        pl.semaphore_signal(barrier, inc=1, device_id=((group + d) % outer, me), device_id_type=mesh_id)

    def target(turn):
        return (chip + turn + 1) % chips

    def lanes_of(turn):
        return pl.ds(pl.multiple_of(target(turn) * 256, 256), 256)

    def k_copy(turn):
        return pltpu.make_async_copy(k_hbm.at[:, :, lanes_of(turn)], k_buf.at[turn], load_k.at[turn])

    def v_copy(turn):
        return pltpu.make_async_copy(v_hbm.at[:, :, lanes_of(turn)], v_buf.at[turn], load_v.at[turn])

    def q_copy(turn):
        return pltpu.make_async_copy(q_hbm.at[:, lanes_of(turn)], q_buf.at[turn], load_q.at[turn])

    for t in range(chips):
        k_copy(t).start()
        v_copy(t).start()
    for t in range(chips):
        q_copy(t).start()

    fill_spread(spread_buf)

    def near_copy(turn):
        return pltpu.make_async_remote_copy(
            src_ref=away.at[turn], dst_ref=near.at[turn],
            send_sem=send0.at[turn], recv_sem=recv0.at[turn],
            device_id=(group, partner), device_id_type=mesh_id,
        )

    def map_copy(d):
        return pltpu.make_async_remote_copy(
            src_ref=sent.at[d], dst_ref=got.at[d],
            send_sem=send1.at[d], recv_sem=recv1.at[d],
            device_id=(group, (chip + d) % chips * 2 + core), device_id_type=mesh_id,
        )

    def chip_map(turn):
        near_copy(turn).wait()
        here, there = own[turn], near[turn]
        even = jnp.where(core == 0, here, there)
        odd = jnp.where(core == 0, there, here)
        even_map[turn] = even
        return then(even, odd)

    def parity(i):
        return core if i == 0 else 1 - core

    def head_lanes(i):
        return pl.ds(pl.multiple_of(parity(i) * 128, 128), 128)

    def rows_of(head, n):
        at = slice(n * BLOCK_LEN, (n + 1) * BLOCK_LEN)
        row = pl.ds(head, 1)
        b0, b1 = small_ref[0, row, :][:, at], small_ref[1, row, :][:, at]
        d = small_ref[2, row, :][:, at]
        return jnp.concatenate([d, d], 1), jnp.concatenate([b0, b1], 1)

    def pair_of(buf, turn, i, n):
        at = pl.ds(n * BLOCK_LEN, BLOCK_LEN)
        return jnp.concatenate([buf[turn, 0, at, head_lanes(i)], buf[turn, 1, at, head_lanes(i)]], 0)

    def step(turn, carry):
        heads = [target(turn) * 2 + parity(i) for i in range(2)]
        k_copy(turn).wait()

        def load(i, n):
            d_row, beta_row = rows_of(heads[i], n)
            return pair_of(k_buf, turn, i, n), d_row, beta_row

        work, eye_f = systems(blocks, 2, load, spread_buf)

        @pl.when(turn == 0)
        def _():
            pl.semaphore_wait(barrier, chips + outer - 1)

        @pl.when(turn > 0)
        def _():
            sent[turn] = chip_map(turn - 1)
            map_copy(turn).start()

        v_copy(turn).wait()

        def load_kv(i, n):
            return pair_of(k_buf, turn, i, n), pair_of(v_buf, turn, i, n)

        def keep(i, n, written, c_row, ki_row, state):
            w_buf[turn, i, n] = written
            vec_buf[turn, i, n, 0:1, :] = c_row
            vec_buf[turn, i, n, 1:2, :] = ki_row
            if n:
                p_buf[turn, i, n] = state

        states = state_maps(blocks, 2, work, eye_f, load_kv, keep)
        away[turn] = states[1]
        own[turn] = states[0]

        near_copy(turn).start()
        return carry

    lax.fori_loop(0, chips, step, 0)

    def read_step(turn, carry):
        heads = [target(turn) * 2 + parity(i) for i in range(2)]
        q_copy(turn).wait()

        def load(i, n):
            at = pl.ds(n * BLOCK_LEN, BLOCK_LEN)
            d_row, _ = rows_of(heads[i], n)
            return (
                q_buf[turn, at, head_lanes(i)], pair_of(k_buf, turn, i, n), d_row, w_buf[turn, i, n],
                vec_buf[turn, i, n, 0:1, :], vec_buf[turn, i, n, 1:2, :], p_buf[turn, i, n] if n else None,
            )

        def emit(i, n, carried, base):
            at = pl.ds(n * BLOCK_LEN, BLOCK_LEN)
            c_buf[turn, i, at, :] = carried
            b_buf[turn, i, at, :] = base

        reads(blocks, 2, load, emit)
        return carry

    lax.fori_loop(0, chips // 2, read_step, 0)
    got[0] = chip_map(chips - 1)
    for d in range(1, chips):
        map_copy(d).wait()

    maps = [got[(chip - i + chips) % chips] for i in range(chips)]

    def tree(parts):
        if len(parts) == 1:
            return parts
        half = len(parts) // 2
        pairs = [then(parts[2 * i], parts[2 * i + 1]) for i in range(half)]
        return pairs

    level = maps
    levels = [maps]
    while len(level) > 1:
        level = tree(level)
        levels.append(level)
    mine[0] = level[0][:, :128]
    mine[1] = level[0][:, 128:]

    def group_copy(part, d):
        sems = (send2, recv2) if part == 0 else (send5, recv5)
        return pltpu.make_async_remote_copy(
            src_ref=mine.at[part], dst_ref=groups.at[part, d],
            send_sem=sems[0].at[d], recv_sem=sems[1].at[d],
            device_id=((group + d) % outer, me), device_id_type=mesh_id,
        )

    for d in range(outer - 1, 0, -1):

        @pl.when(group + d < outer)
        def _():
            group_copy(1, d).start()

    for d in range(outer - 1, 0, -1):

        @pl.when((group + d < outer) & (group > 0))
        def _():
            group_copy(0, d).start()

    before = {}
    for i in range(1, chips):
        low = i & -i
        height = low.bit_length() - 1
        part = levels[height][(i - low) >> height]
        before[i] = part if i == low else then(before[i - low], part)
    left = wide(jnp.concatenate([before[i][:, :128] for i in range(1, chips)], 0))
    right = jnp.concatenate([before[i][:, 128:] for i in range(1, chips)], 0)

    lax.fori_loop(chips // 2, chips, read_step, 0)

    start = jnp.zeros((128, 128), F32)
    for g in range(outer - 1):
        at = (group - g + outer) % outer

        @pl.when(group > g)
        def _():
            group_copy(1, at).wait_recv()
            if g:
                group_copy(0, at).wait_recv()

        moved = groups[1, at]
        if g:
            moved = mul(groups[0, at], start) + moved
        start = jnp.where(g < group, moved, start)

    sh, sl = split(start)
    row = jnp.concatenate([sh, sl], 1)
    both = dot(left, jnp.concatenate([row, row], 0))
    ready[0] = start
    ready[pl.ds(1, chips - 1)] = (both[:, :128] + both[:, 128:] + right).reshape(chips - 1, 128, 128)

    def back_copy(d):
        to = (chip + d) % chips
        return pltpu.make_async_remote_copy(
            src_ref=ready.at[to], dst_ref=came.at[d],
            send_sem=send3.at[d], recv_sem=recv3.at[d],
            device_id=(group, to * 2 + core), device_id_type=mesh_id,
        )

    def side_copy(d):
        return pltpu.make_async_remote_copy(
            src_ref=aside.at[d], dst_ref=beside.at[d],
            send_sem=send4.at[d], recv_sem=recv4.at[d],
            device_id=(group, partner), device_id_type=mesh_id,
        )

    for d in range(1, chips):
        back_copy(d).start()

    def out(turn, i, state):
        head = target(turn) * 2 + parity(i)
        lanes = pl.ds(pl.multiple_of(head * 128, 128), 128)
        o_ref[:, lanes] = normed(c_buf[turn, i], b_buf[turn, i], state, small_ref[3, 0:1, :128])

    for d in range(chips):
        turn = chips - 1 - d
        if d:
            back_copy(d).wait()
            enter = came[d]
        else:
            enter = ready[chip]
        pair = even_map[turn]
        after = mul(pair[:, :128], enter) + pair[:, 128:]
        aside[d] = jnp.where(core == 0, after, enter)
        side_copy(d).start()
        out(turn, 0, jnp.where(core == 0, enter, after))
        if d:
            side_copy(d - 1).wait()
            out(turn + 1, 1, beside[d - 1])
    side_copy(chips - 1).wait()
    out(0, 1, beside[chips - 1])
    for d in range(1, outer):

        @pl.when(group + d < outer)
        def _():
            group_copy(1, d).wait_send()

        @pl.when((group + d < outer) & (group > 0))
        def _():
            group_copy(0, d).wait_send()


def whole(inner, outer, queries, keys, values, betas, log_decay, out_gain):
    length, width = queries.shape
    blocks = length // BLOCK_LEN
    chips = inner // 2
    gain = lax.broadcast_in_dim(jnp.pad(out_gain, (0, length - 128)), (1, inner, length), (2,))
    small = jnp.concatenate([betas, log_decay[None], gain], 0)
    vmem = pl.BlockSpec(memory_space=pltpu.VMEM)
    hbm = pl.BlockSpec(memory_space=pltpu.HBM)
    dma = pltpu.SemaphoreType.DMA
    return pl.pallas_call(
        functools.partial(whole_kernel, inner, outer),
        in_specs=[hbm] * 3 + [vmem],
        out_specs=vmem,
        out_shape=jax.ShapeDtypeStruct((length, width), BF16),
        scratch_shapes=[
            pltpu.VMEM((8, 128, 256), BF16),
            pltpu.VMEM((chips, length, 256), BF16),
            *[pltpu.VMEM((chips, 2, length, 256), BF16)] * 2,
            *[pltpu.VMEM((chips, 2, blocks, 128, 256), F32)] * 2,
            pltpu.VMEM((chips, 2, blocks, 8, 128), F32),
            *[pltpu.VMEM((chips, 128, 256), F32)] * 6,
            pltpu.VMEM((2, outer, 128, 128), F32),
            pltpu.VMEM((2, 128, 128), F32),
            *[pltpu.VMEM((chips, 128, 128), F32)] * 4,
            *[pltpu.VMEM((chips, 2, length, 128), F32)] * 2,
            *[dma((chips,))] * 3,
            *[dma((chips,))] * 4,
            *[dma((outer,))] * 2,
            *[dma((chips,))] * 4,
            *[dma((outer,))] * 2,
        ],
        compiler_params=pltpu.CompilerParams(
            collective_id=0, has_side_effects=True, vmem_limit_bytes=53 * 1024 * 1024
        ),
        name="whole",
    )(queries, keys, values, small)


HIGHEST = lax.Precision.HIGHEST


def join(earlier, later):
    moved = jnp.einsum("hde,hef->hdf", later[..., :128], earlier, precision=HIGHEST)
    return jnp.concatenate([moved[..., :128], moved[..., 128:] + later[..., 128:]], -1)


def entering(pairs, axis, begin):
    gathered = lax.all_gather(pairs, axis)

    def one(hop, state):
        return join(state, lax.dynamic_index_in_dim(gathered, hop, 0, False))

    return lax.fori_loop(0, lax.axis_index(axis), one, begin)


def exchange_plain(pairs):
    eye = jnp.concatenate([jnp.eye(128, dtype=F32), jnp.zeros((128, 128), F32)], 1)
    begin = jnp.zeros_like(pairs) + eye
    before = entering(pairs, "inner", begin)
    through = join(before, pairs)
    last = lax.axis_index("inner") == lax.axis_size("inner") - 1
    total = lax.psum(jnp.where(last, through, 0.0), "inner")
    start = entering(total, "outer", begin)
    return join(start, before)[..., 128:]


def finish_kernel(c_ref, b_ref, e_ref, g_ref, o_ref):
    readout = mul(c_ref[0], e_ref[0]) + b_ref[0]
    mean_sq = jnp.mean(readout * readout, 1, keepdims=True)
    o_ref[...] = (readout * lax.rsqrt(mean_sq + 1e-05) * g_ref[...]).astype(BF16)


def finish(carried, base, state, out_gain):
    heads, length, _ = carried.shape
    return pl.pallas_call(
        finish_kernel,
        grid=(heads,),
        in_specs=[
            pl.BlockSpec((1, length, 128), lambda h: (h, 0, 0)),
            pl.BlockSpec((1, length, 128), lambda h: (h, 0, 0)),
            pl.BlockSpec((1, 128, 128), lambda h: (h, 0, 0)),
            pl.BlockSpec((1, 128), lambda h: (0, 0)),
        ],
        out_specs=pl.BlockSpec((length, 128), lambda h: (0, h)),
        out_shape=jax.ShapeDtypeStruct((length, heads * 128), BF16),
        name="finish",
    )(carried, base, state, out_gain.reshape(1, 128))


def per_device(inner, outer, queries, keys, values, betas, log_decay, out_gain):
    heads = betas.shape[1]
    if inner == heads:
        return whole(inner, outer, queries, keys, values, betas, log_decay, out_gain)
    pairs, carried, base = local_phase(queries, keys, values, betas, log_decay)
    return finish(carried, base, exchange_plain(pairs), out_gain)


def solution(mesh):
    both = ("outer", "inner")
    placed = (P(both, None), P(None, both, None), P(None, both, None), P(None, None, both), P(None, both), P())
    return jax.shard_map(
        functools.partial(per_device, mesh.shape["inner"], mesh.shape["outer"]),
        mesh=mesh,
        in_specs=placed,
        out_specs=P(both, None),
        check_vma=False,
    )
```

```python
import functools

import jax
import jax.numpy as jnp
from jax import lax
from jax.experimental import pallas as pl
from jax.experimental.pallas import tpu as pltpu
from jax.sharding import PartitionSpec as P

BLOCK_LEN = 64
F32 = jnp.float32
BF16 = jnp.bfloat16


def split(x):
    high = x.astype(BF16)
    low = (x - high.astype(F32)).astype(BF16)
    return high, low


def dot(a, b):
    return lax.dot_general(a, b, (((1,), (0,)), ((), ())), preferred_element_type=F32)


def dot_t(a, b):
    return lax.dot_general(a, b, (((1,), (1,)), ((), ())), preferred_element_type=F32)


def wide(x):
    return jnp.concatenate(split(x), 1)


def mul(a, b):
    a2 = wide(a)
    bh, bl = split(b)
    if b.shape[1] == 128:
        row = jnp.concatenate([bh, bl], 1)
        both = dot(a2, jnp.concatenate([row, row], 0))
        return both[:, :128] + both[:, 128:]
    return dot(a2, jnp.concatenate([bh, bh], 0)) + dot(a2[:, :128], bl)


def mul_left(a, b):
    return dot(wide(a), jnp.concatenate([b, b], 0))


def add_right(x, y):
    return jnp.concatenate([x[:, :128], x[:, 128:] + y], 1)


def masks():
    span = BLOCK_LEN
    size = 2 * span
    row = lax.broadcasted_iota(jnp.int32, (size, size), 0)
    col = lax.broadcasted_iota(jnp.int32, (size, size), 1)
    row_t, col_t = row & (span - 1), col & (span - 1)
    row_rank = 2 * row_t + (row >= span).astype(jnp.int32)
    col_rank = 2 * col_t + (col >= span).astype(jnp.int32)
    differ = row_rank ^ col_rank
    eye = row == col
    eye_f = eye.astype(F32)
    lower = row_rank > col_rank
    c_mask = (col_t <= row_t) & (col < span)
    r_mask = (row_t <= col_t) & (row < span)
    levels = []
    width = 1
    while width < size:
        levels.append(
            (differ >= width) & (differ < 2 * width) & lower
        )
        width *= 2

    return row, col_t, row_t, eye, eye_f, lower, c_mask, r_mask, levels


def head_maps(blocks, heads_in, load, emit):
    span = BLOCK_LEN
    row, col_t, row_t, eye, eye_f, lower, c_mask, r_mask, levels = masks()
    work = []
    for i, n in [(i, n) for i in range(heads_in) for n in range(blocks)]:
        q_b, k_b, v_b, d_row, beta_row = load(i, n)
        d_col = jnp.sum(jnp.where(eye, d_row, 0.0), 1, keepdims=True)
        beta_col = jnp.sum(jnp.where(eye, beta_row, 0.0), 1, keepdims=True)
        c_col = jnp.sum(jnp.where(c_mask, d_row, 0.0), 1, keepdims=True)
        c_row = jnp.sum(jnp.where(r_mask, d_col, 0.0), 0, keepdims=True)
        gram = dot_t(k_b, k_b)
        k_f = k_b.astype(F32)
        q_f = q_b.astype(F32)
        ki_col = lax.rsqrt(jnp.sum(k_f * k_f, 1, keepdims=True) + 1e-06)
        ki_row = lax.rsqrt(jnp.sum(jnp.where(eye, gram, 0.0), 0, keepdims=True) + 1e-06)
        qi_col = lax.rsqrt(jnp.sum(q_f * q_f, 1, keepdims=True) + 1e-06)
        fall = jnp.exp(jnp.minimum(c_col - c_row, 0.0))
        low = jnp.where(lower, gram * (beta_col * ki_col) * ki_row * fall, 0.0)
        reach = dot_t(q_b, k_b) * qi_col * ki_row * fall[:span]
        reach = jnp.where(col_t[:span] <= row_t[:span], reach, 0.0)
        query = q_f * (qi_col * jnp.exp(c_col[:span]))
        work.append((k_b, v_b, beta_row, c_row, c_col, ki_row, ki_col, low, reach, query))

    inverse = [eye_f - jnp.where(levels[0], w[7], 0.0) for w in work]
    for mask in levels[1:]:
        part = [mul(jnp.where(mask, w[7], 0.0), t) for w, t in zip(work, inverse)]
        inverse = [t - mul(t, p) for t, p in zip(inverse, part)]

    states = [None] * heads_in
    for n in range(blocks):
        for i in range(heads_in):
            state = states[i]
            k_b, v_b, beta_row, c_row, c_col, ki_row, ki_col, low, reach, query = work[i * blocks + n]
            t = inverse[i * blocks + n] * beta_row
            written = jnp.concatenate(
                [mul_left(t * (ki_row * jnp.exp(c_row)), k_b), mul_left(t, v_b)], 1
            )
            got = mul(reach, written)
            reduced, local_out = query - got[:, :128], got[:, 128:]
            last = c_col[span - 1 : span, :]
            tail = jnp.exp(last - c_col) * ki_col
            wh, wl = split(written * tail)
            k_t = jnp.transpose(k_b.astype(F32)).astype(BF16)
            made = dot(jnp.concatenate([k_t, k_t], 1), jnp.concatenate([wh, wl], 0))
            trans = jnp.exp(last) * eye_f - made[:, :128]
            inject = made[:, 128:]
            if state is None:
                emit(i, n, reduced, local_out)
                states[i] = jnp.concatenate([trans, inject], 1)
            else:
                read = mul(reduced, state)
                emit(i, n, read[:, :128], read[:, 128:] + local_out)
                states[i] = add_right(mul(trans, state), inject)
    return states


def local_kernel(blocks, q_ref, k_ref, v_ref, s_ref, x_ref, c_ref, b_ref):
    def load(i, n):
        at = pl.ds(n * BLOCK_LEN, BLOCK_LEN)
        k_b = jnp.concatenate([k_ref[0, at, :], k_ref[1, at, :]], 0)
        v_b = jnp.concatenate([v_ref[0, at, :], v_ref[1, at, :]], 0)
        return q_ref[at, :], k_b, v_b, s_ref[0, n : n + 1, :], s_ref[0, blocks + n : blocks + n + 1, :]

    def emit(i, n, carried, base):
        at = pl.ds(n * BLOCK_LEN, BLOCK_LEN)
        c_ref[0, at, :] = carried
        b_ref[0, at, :] = base

    x_ref[0] = head_maps(blocks, 1, load, emit)[0]


def small_rows(betas, log_decay):
    heads, length = log_decay.shape
    blocks = length // BLOCK_LEN
    beta = betas.reshape(2, heads, blocks, BLOCK_LEN).transpose(1, 2, 0, 3)
    beta = beta.reshape(heads, blocks, 2 * BLOCK_LEN)
    decay = log_decay.reshape(heads, blocks, 1, BLOCK_LEN)
    decay = jnp.concatenate([decay, decay], 2).reshape(heads, blocks, 2 * BLOCK_LEN)
    small = jnp.concatenate([decay, beta], 1)
    return small


def local_phase(queries, keys, values, betas, log_decay):
    length = queries.shape[0]
    heads = betas.shape[1]
    blocks = length // BLOCK_LEN
    small = small_rows(betas, log_decay)
    return pl.pallas_call(
        functools.partial(local_kernel, blocks),
        grid=(heads,),
        in_specs=[
            pl.BlockSpec((length, 128), lambda h: (0, h)),
            pl.BlockSpec((2, length, 128), lambda h: (0, 0, h)),
            pl.BlockSpec((2, length, 128), lambda h: (0, 0, h)),
            pl.BlockSpec((1, 2 * blocks, 128), lambda h: (h, 0, 0)),
        ],
        out_specs=[
            pl.BlockSpec((1, 128, 256), lambda h: (h, 0, 0)),
            pl.BlockSpec((1, length, 128), lambda h: (h, 0, 0)),
            pl.BlockSpec((1, length, 128), lambda h: (h, 0, 0)),
        ],
        out_shape=[
            jax.ShapeDtypeStruct((heads, 128, 256), F32),
            jax.ShapeDtypeStruct((heads, length, 128), F32),
            jax.ShapeDtypeStruct((heads, length, 128), F32),
        ],
        name="local_phase",
    )(queries, keys, values, small)


def then(earlier, later):
    return add_right(mul(later[:, :128], earlier), later[:, 128:])


def normed(carried, base, state, gain):
    readout = mul(carried, state) + base
    mean_sq = jnp.mean(readout * readout, 1, keepdims=True)
    return (readout * lax.rsqrt(mean_sq + 1e-05) * gain).astype(BF16)


LOG2E = 1.4426950408889634


def split3(x):
    high = x.astype(BF16)
    rest = x - high.astype(F32)
    mid = rest.astype(BF16)
    low = rest - mid.astype(F32)
    return high.astype(F32), mid.astype(F32), low


def tokens_of(shape, dim):
    at = lax.broadcasted_iota(jnp.int32, shape, dim)
    return at & (BLOCK_LEN - 1), at >> 6


def fill_spread(spread_ref):
    t_r, j_r = tokens_of((128, 128), 0)
    t_c, j_c = tokens_of((128, 128), 1)
    rank = 2 * (t_r & 7) + j_r
    same = (t_r >> 3) == (t_c >> 3)
    for p in range(8):
        parts = [jnp.where(same & (rank == 2 * p + q), 1.0, 0.0) for q in range(2)]
        spread_ref[p] = jnp.concatenate(parts, 1).astype(BF16)


def odd_starts(width):
    return [j * BLOCK_LEN + t for j in range(2) for t in range(width, BLOCK_LEN, 2 * width)]


def odd_rows(x, width):
    return jnp.concatenate([x[s : s + width] for s in odd_starts(width)], 0)


def stacked(left, right):
    rows = left[0].shape[0]
    both = dot(jnp.concatenate(left, 0), jnp.concatenate(right, 1))
    return both[:rows, :128] + (both[:rows, 128:] + both[rows:, :128])


def systems(blocks, heads_in, load, spread_ref):
    units = [(i, n) for i in range(heads_in) for n in range(blocks)]
    count = len(units)
    loaded = [load(i, n) for i, n in units]
    t_r, j_r = tokens_of((128, 128), 0)
    t_c, j_c = tokens_of((128, 128), 1)
    eye = (t_r == t_c) & (j_r == j_c)
    running = jnp.where((t_r <= t_c) & (j_r == 0), 1.0, 0.0).astype(BF16)
    decay = jnp.concatenate([u[1] for u in loaded], 0)
    beta = jnp.concatenate([u[2] for u in loaded], 0)
    total = dot(
        jnp.concatenate(split3(decay), 1).astype(BF16), jnp.concatenate([running] * 3, 0)
    )
    grams = [dot_t(u[0], u[0]) for u in loaded]
    squares = jnp.concatenate([jnp.sum(jnp.where(eye, g, 0.0), 0, keepdims=True) for g in grams], 0) + 1e-06
    inv = lax.rsqrt(squares)
    inv_log = -0.5 * jnp.log2(squares)
    fallen = total * LOG2E
    last = fallen[:, BLOCK_LEN - 1 : BLOCK_LEN]
    scale_k = jnp.exp2(fallen) * inv
    tail = jnp.exp2(last - fallen) * inv
    keep_all = jnp.exp2(last)
    ones = jnp.ones((count, 128), F32)
    zeros = jnp.zeros((count, 128), F32)
    stack = [*split3(fallen + inv_log), ones, ones, ones, *split3(beta), *split3(tail)]
    columns = jnp.transpose(jnp.concatenate(stack + [zeros] * (128 // count - len(stack)), 0)).astype(BF16)
    later = split3(inv_log - fallen)
    sub = lax.broadcasted_iota(jnp.int32, (count, 128), 0)

    lane_t, lane_j = tokens_of((8, 128), 1)
    row8 = lax.broadcasted_iota(jnp.int32, (8, 128), 0)
    in_block = [(lane_t >> 3) == b for b in range(8)]
    lane_rank = 2 * (lane_t & 7) + lane_j
    lower_0, lower_1 = 2 * row8 > lane_rank, 2 * row8 + 1 > lane_rank
    first_0 = jnp.where(2 * row8 == lane_rank, 1.0, 0.0)
    first_1 = jnp.where(2 * row8 + 1 == lane_rank, 1.0, 0.0)
    t16 = lax.broadcasted_iota(jnp.int32, (128, 128), 0) & (BLOCK_LEN - 1)
    own_block = jnp.where((t16 >> 3) == (t_c >> 3), 1.0, 0.0).astype(BF16)

    lows, tails, compact = [], [], []
    for u in range(count):
        pick = sub == u
        one = jnp.where(pick, 1.0, 0.0)
        right = [one] * 3 + [jnp.where(pick, g, 0.0) for g in later]
        none = [zeros]
        fill = 128 // count
        cols = [
            right + none * (fill - 6),
            none * 6 + [one] * 3 + none * (fill - 9),
            none * 9 + [one] * 3 + none * (fill - 12),
        ]
        right = jnp.concatenate([jnp.concatenate(c, 0) for c in cols], 1).astype(BF16)
        spread = dot(columns, right)
        low = grams[u] * jnp.exp2(spread[:, :128]) * spread[:, 128:256]
        lows.append(low)
        tails.append(spread[:, 256:])
        for j, lower in ((0, lower_0), (1, lower_1)):
            part = low[j * BLOCK_LEN : j * BLOCK_LEN + 8]
            for b in range(1, 8):
                at = j * BLOCK_LEN + 8 * b
                part = jnp.where(in_block[b], low[at : at + 8], part)
            compact.append(jnp.where(lower, part, 0.0))

    packed = wide(jnp.concatenate(compact, 0))
    pairs = [dot(packed, jnp.concatenate([spread_ref[p]] * 2, 0)) for p in range(8)]
    small = [[first_0, first_1] for _ in range(count)]
    for s in range(15):
        t, j, lanes = s // 2, s % 2, slice(128 * (s % 2), 128 * (s % 2) + 128)
        for u in range(count):
            x0, x1 = small[u]
            source = (x0, x1)[j][t : t + 1]
            coef = pairs[s // 2][16 * u : 16 * u + 16, lanes]
            small[u] = [x0 - coef[:8] * source, x1 - coef[8:] * source]

    highs, slims, updates = [], [], [[] for _ in range(count)]
    pair_of_8 = []
    for u in range(count):
        tiles = []
        for x in small[u]:
            both = jnp.concatenate([x, x], 0)
            tiles.append(split(both))
        high = jnp.concatenate([tiles[0][0]] * 4 + [tiles[1][0]] * 4, 0)
        slim = jnp.concatenate([tiles[0][1]] * 4 + [tiles[1][1]] * 4, 0)
        highs.append(high * own_block)
        slims.append(slim * own_block)
        pair_of_8.append(tiles)

    q = lax.broadcasted_iota(jnp.int32, (64, 128), 0) & 31
    c_t = lax.broadcasted_iota(jnp.int32, (64, 128), 1) & (BLOCK_LEN - 1)
    for width in (8, 16, 32):
        bits = width.bit_length()
        row_t = ((q >> (bits - 1)) << bits) + width + (q & (width - 1))
        mask = ((c_t & width) == 0) & ((c_t >> bits) == (row_t >> bits))
        if width == 8:
            odd_own = jnp.where((c_t >> 3) == (row_t >> 3), 1.0, 0.0).astype(BF16)
        parts = []
        for u in range(count):
            a = split(jnp.where(mask, odd_rows(lows[u], width), 0.0))
            parts.append(stacked(a, (highs[u], slims[u])))
        for u in range(count):
            p = parts[u]
            if width == 8:
                ph = p.astype(BF16).astype(F32)
                pl_ = p - ph
                doubled = [
                    jnp.concatenate([x[8 * (g // 2) : 8 * (g // 2) + 8] for g in range(16)], 0).astype(BF16)
                    for x in (ph, pl_)
                ]
                tiles = pair_of_8[u]
                odd = [jnp.concatenate([tiles[0][k]] * 2 + [tiles[1][k]] * 2, 0) * odd_own for k in range(2)]
            else:
                groups = range(64 // width)
                doubled = [
                    jnp.concatenate([x[width * g : width * g + width] for g in groups for _ in range(2)], 0)
                    for x in split(p)
                ]
                odd = [odd_rows(highs[u], width), odd_rows(slims[u], width)]
            update = stacked(odd, doubled)
            updates[u].append(update)
            if width == 32:
                continue
            if width == 8:
                uh = update.astype(BF16).astype(F32)
                gap = jnp.zeros((8, 128), F32)
                spaced = [
                    jnp.concatenate(
                        [x[8 * (g // 2) : 8 * (g // 2) + 8] if g % 2 else gap for g in range(16)], 0
                    ).astype(BF16)
                    for x in (uh, update - uh)
                ]
            else:
                gap = jnp.zeros((width, 128), BF16)
                spaced = [
                    jnp.concatenate(
                        [
                            x[width * (g // 2) : width * (g // 2) + width] if g % 2 else gap
                            for g in range(128 // width)
                        ],
                        0,
                    )
                    for x in split(update)
                ]
            highs[u] = highs[u] - spaced[0]
            slims[u] = slims[u] - spaced[1]

    work = []
    for u in range(count):
        rows = []
        for j in range(2):
            for b in range(8):
                x = jnp.where(in_block[b], small[u][j], 0.0)
                for width, update in zip((8, 16, 32), updates[u]):
                    t = 8 * b
                    if t & width:
                        at = j * 32 + (t // (2 * width)) * width + t % width
                        x = x - update[at : at + 8]
                rows.append(x)
        at = slice(u, u + 1)
        inverse = jnp.concatenate(rows, 0)
        work.append((inverse, beta[at], scale_k[at], tails[u], keep_all[at], total[at], inv[at]))
    return work, jnp.where(eye, 1.0, 0.0)


def state_maps(blocks, heads_in, work, eye_f, load_kv, keep):
    units = [(i, n) for n in range(blocks) for i in range(heads_in)]
    wrote, pieces = {}, {}
    for i, n in units:
        k_b, v_b = load_kv(i, n)
        inverse, beta_row, scale_k = work[i * blocks + n][:3]
        t = inverse * beta_row
        wrote[i, n] = mul_left(t * scale_k, k_b), mul_left(t, v_b)
    for i, n in units:
        k_b, _ = load_kv(i, n)
        tail, keep_all = work[i * blocks + n][3:5]
        wk, wv = wrote[i, n]
        wh, wl = split(jnp.concatenate([wk * tail, wv * tail], 1))
        k_t = jnp.transpose(k_b.astype(F32)).astype(BF16)
        made = dot(jnp.concatenate([k_t, k_t], 1), jnp.concatenate([wh, wl], 0))
        pieces[i, n] = jnp.concatenate([keep_all * eye_f - made[:, :128], made[:, 128:]], 1)
    firsts = [then(pieces[i, 0], pieces[i, 1]) for i in range(heads_in)]
    seconds = [then(pieces[i, 2], pieces[i, 3]) for i in range(heads_in)]
    states = [then(a, b) for a, b in zip(firsts, seconds)]
    for i, n in units:
        c_row, ki_row = work[i * blocks + n][5:7]
        part = (None, pieces[i, 0], firsts[i], pieces[i, 2])[n]
        keep(i, n, jnp.concatenate(wrote[i, n], 1), c_row, ki_row, part)
    return states


def reads(blocks, heads_in, load, emit):
    span = BLOCK_LEN
    row = lax.broadcasted_iota(jnp.int32, (span, 2 * span), 0)
    col = lax.broadcasted_iota(jnp.int32, (span, 2 * span), 1)
    col_t = col & (span - 1)
    seen = col_t <= row
    for i, n in [(i, n) for i in range(heads_in) for n in range(blocks)]:
        q_b, k_b, d_row, written, c_row, ki_row, state = load(i, n)
        c_col = jnp.sum(jnp.where(seen & (col < span), d_row, 0.0), 1, keepdims=True)
        q_f = q_b.astype(F32)
        qi_col = lax.rsqrt(jnp.sum(q_f * q_f, 1, keepdims=True) + 1e-06)
        fall = jnp.exp(jnp.minimum(c_col - c_row, 0.0))
        reach = jnp.where(seen, dot_t(q_b, k_b) * qi_col * ki_row * fall, 0.0)
        query = q_f * (qi_col * jnp.exp(c_col))
        got = mul(reach, written)
        reduced, local_out = query - got[:, :128], got[:, 128:]
        if n == 0:
            emit(i, n, reduced, local_out)
        else:
            read = mul(reduced, state)
            emit(i, n, read[:, :128], read[:, 128:] + local_out)


def whole_kernel(
    inner, outer, q_hbm, k_hbm, v_hbm, small_ref, o_ref,
    spread_buf, q_buf, k_buf, v_buf, w_buf, p_buf, vec_buf,
    away, near, own, even_map, sent, got, pair_buf, groups, mine, ready, came, aside, beside, c_buf, b_buf,
    load_k, load_v, load_q,
    send0, recv0, send1, recv1, send2, recv2, send3, recv3, send4, recv4, send5, recv5,
):
    mesh_id = pl.DeviceIdType.MESH
    length = q_hbm.shape[0]
    blocks = length // BLOCK_LEN
    me = lax.axis_index("inner")
    group = lax.axis_index("outer")
    core, chip, chips = me % 2, me // 2, inner // 2
    partner = chip * 2 + 1 - core
    groups[...] = jnp.zeros_like(groups)
    barrier = pltpu.get_barrier_semaphore()
    for d in range(1, chips):
        pl.semaphore_signal(
            barrier, inc=1, device_id=(group, (chip + d) % chips * 2 + core), device_id_type=mesh_id
        )
    pl.semaphore_signal(barrier, inc=1, device_id=(group, partner), device_id_type=mesh_id)
    for d in range(1, outer):
        pl.semaphore_signal(barrier, inc=1, device_id=((group + d) % outer, me), device_id_type=mesh_id)

    def flip(x):
        return (chip % 2 + x % 2) % 2 + (chip // 2 + x // 2) % 2 * 2

    def target(turn):
        return flip(chips - 1 - turn)

    def lanes_of(turn):
        return pl.ds(pl.multiple_of(target(turn) * 256, 256), 256)

    def k_copy(turn):
        return pltpu.make_async_copy(k_hbm.at[:, :, lanes_of(turn)], k_buf.at[turn], load_k.at[turn])

    def v_copy(turn):
        return pltpu.make_async_copy(v_hbm.at[:, :, lanes_of(turn)], v_buf.at[turn], load_v.at[turn])

    def q_copy(turn):
        return pltpu.make_async_copy(q_hbm.at[:, lanes_of(turn)], q_buf.at[turn], load_q.at[turn])

    for t in range(chips):
        k_copy(t).start()
        v_copy(t).start()
    for t in range(chips):
        q_copy(t).start()

    fill_spread(spread_buf)

    def near_copy(turn):
        return pltpu.make_async_remote_copy(
            src_ref=away.at[turn], dst_ref=near.at[turn],
            send_sem=send0.at[turn], recv_sem=recv0.at[turn],
            device_id=(group, partner), device_id_type=mesh_id,
        )

    def map_copy(d):
        return pltpu.make_async_remote_copy(
            src_ref=sent.at[d], dst_ref=got.at[d],
            send_sem=send1.at[d], recv_sem=recv1.at[d],
            device_id=(group, flip(chips - d) * 2 + core), device_id_type=mesh_id,
        )

    def chip_map(turn):
        near_copy(turn).wait()
        here, there = own[turn], near[turn]
        even = jnp.where(core == 0, here, there)
        odd = jnp.where(core == 0, there, here)
        even_map[turn] = even
        return then(even, odd)

    def parity(i):
        return core if i == 0 else 1 - core

    def head_lanes(i):
        return pl.ds(pl.multiple_of(parity(i) * 128, 128), 128)

    def rows_of(head, n):
        at = slice(n * BLOCK_LEN, (n + 1) * BLOCK_LEN)
        row = pl.ds(head, 1)
        b0, b1 = small_ref[0, row, :][:, at], small_ref[1, row, :][:, at]
        d = small_ref[2, row, :][:, at]
        return jnp.concatenate([d, d], 1), jnp.concatenate([b0, b1], 1)

    def pair_of(buf, turn, i, n):
        at = pl.ds(n * BLOCK_LEN, BLOCK_LEN)
        return jnp.concatenate([buf[turn, 0, at, head_lanes(i)], buf[turn, 1, at, head_lanes(i)]], 0)

    def step(turn, carry):
        heads = [target(turn) * 2 + parity(i) for i in range(2)]
        k_copy(turn).wait()

        def load(i, n):
            d_row, beta_row = rows_of(heads[i], n)
            return pair_of(k_buf, turn, i, n), d_row, beta_row

        work, eye_f = systems(blocks, 2, load, spread_buf)

        @pl.when(turn == 0)
        def _():
            pl.semaphore_wait(barrier, chips + outer - 1)

        @pl.when(turn > 0)
        def _():
            sent[turn] = chip_map(turn - 1)
            map_copy(turn).start()

        v_copy(turn).wait()

        def load_kv(i, n):
            return pair_of(k_buf, turn, i, n), pair_of(v_buf, turn, i, n)

        def keep(i, n, written, c_row, ki_row, state):
            w_buf[turn, i, n] = written
            vec_buf[turn, i, n, 0:1, :] = c_row
            vec_buf[turn, i, n, 1:2, :] = ki_row
            if n:
                p_buf[turn, i, n] = state

        states = state_maps(blocks, 2, work, eye_f, load_kv, keep)
        away[turn] = states[1]
        own[turn] = states[0]

        near_copy(turn).start()
        return carry

    lax.fori_loop(0, chips, step, 0)

    def read_step(turn, carry):
        heads = [target(turn) * 2 + parity(i) for i in range(2)]
        q_copy(turn).wait()

        before = []
        for i in range(2):
            first = p_buf[turn, i, 2]
            before.append([None, p_buf[turn, i, 1], first, then(first, p_buf[turn, i, 3])])

        def load(i, n):
            at = pl.ds(n * BLOCK_LEN, BLOCK_LEN)
            d_row, _ = rows_of(heads[i], n)
            return (
                q_buf[turn, at, head_lanes(i)], pair_of(k_buf, turn, i, n), d_row, w_buf[turn, i, n],
                vec_buf[turn, i, n, 0:1, :], vec_buf[turn, i, n, 1:2, :], before[i][n],
            )

        def emit(i, n, carried, base):
            at = pl.ds(n * BLOCK_LEN, BLOCK_LEN)
            c_buf[turn, i, at, :] = carried
            b_buf[turn, i, at, :] = base

        reads(blocks, 2, load, emit)
        return carry

    lax.fori_loop(0, chips // 2, read_step, 0)
    def slot(i):
        return (chips - flip(i)) % chips

    def pair_map(side):
        return then(got[slot(2 * side)], got[slot(2 * side + 1)])

    got[0] = chip_map(chips - 1)
    map_copy(1).wait()
    map_copy(2).wait()
    pair_buf[1 - chip // 2] = pair_map(1 - chip // 2)
    map_copy(3).wait()
    pair_buf[chip // 2] = pair_map(chip // 2)
    total = then(pair_buf[0], pair_buf[1])
    mine[0] = total[:, :128]
    mine[1] = total[:, 128:]

    def group_copy(part, d):
        sems = (send2, recv2) if part == 0 else (send5, recv5)
        return pltpu.make_async_remote_copy(
            src_ref=mine.at[part], dst_ref=groups.at[part, d],
            send_sem=sems[0].at[d], recv_sem=sems[1].at[d],
            device_id=((group + d) % outer, me), device_id_type=mesh_id,
        )

    for d in range(outer - 1, 0, -1):

        @pl.when(group + d < outer)
        def _():
            group_copy(1, d).start()

    for d in range(outer - 1, 0, -1):

        @pl.when((group + d < outer) & (group > 0))
        def _():
            group_copy(0, d).start()

    before = [None, got[slot(0)], pair_buf[0], then(pair_buf[0], got[slot(2)])]
    left = wide(jnp.concatenate([before[i][:, :128] for i in range(1, chips)], 0))
    right = jnp.concatenate([before[i][:, 128:] for i in range(1, chips)], 0)

    lax.fori_loop(chips // 2, chips, read_step, 0)

    start = jnp.zeros((128, 128), F32)
    for g in range(outer - 1):
        at = (group - g + outer) % outer

        @pl.when(group > g)
        def _():
            group_copy(1, at).wait_recv()
            if g:
                group_copy(0, at).wait_recv()

        moved = groups[1, at]
        if g:
            moved = mul(groups[0, at], start) + moved
        start = jnp.where(g < group, moved, start)

    sh, sl = split(start)
    row = jnp.concatenate([sh, sl], 1)
    both = dot(left, jnp.concatenate([row, row], 0))
    ready[0] = start
    ready[pl.ds(1, chips - 1)] = (both[:, :128] + both[:, 128:] + right).reshape(chips - 1, 128, 128)

    def back_copy(d):
        to = flip(d)
        return pltpu.make_async_remote_copy(
            src_ref=ready.at[to], dst_ref=came.at[d],
            send_sem=send3.at[d], recv_sem=recv3.at[d],
            device_id=(group, to * 2 + core), device_id_type=mesh_id,
        )

    def side_copy(d):
        return pltpu.make_async_remote_copy(
            src_ref=aside.at[d], dst_ref=beside.at[d],
            send_sem=send4.at[d], recv_sem=recv4.at[d],
            device_id=(group, partner), device_id_type=mesh_id,
        )

    for d in range(1, chips):
        back_copy(d).start()

    def out(turn, i, state):
        head = target(turn) * 2 + parity(i)
        lanes = pl.ds(pl.multiple_of(head * 128, 128), 128)
        o_ref[:, lanes] = normed(c_buf[turn, i], b_buf[turn, i], state, small_ref[3, 0:1, :128])

    for d in range(chips):
        turn = chips - 1 - d
        if d:
            back_copy(d).wait_recv()
            enter = came[d]
        else:
            enter = ready[chip]
        pair = even_map[turn]
        after = mul(pair[:, :128], enter) + pair[:, 128:]
        aside[d] = jnp.where(core == 0, after, enter)
        side_copy(d).start()
        out(turn, 0, jnp.where(core == 0, enter, after))
        if d:
            side_copy(d - 1).wait_recv()
            out(turn + 1, 1, beside[d - 1])
    side_copy(chips - 1).wait_recv()
    out(0, 1, beside[chips - 1])
    for d in range(chips):
        if d:
            back_copy(d).wait_send()
        side_copy(d).wait_send()
    for d in range(1, outer):

        @pl.when(group + d < outer)
        def _():
            group_copy(1, d).wait_send()

        @pl.when((group + d < outer) & (group > 0))
        def _():
            group_copy(0, d).wait_send()


def whole(inner, outer, queries, keys, values, betas, log_decay, out_gain):
    length, width = queries.shape
    blocks = length // BLOCK_LEN
    chips = inner // 2
    gain = lax.broadcast_in_dim(jnp.pad(out_gain, (0, length - 128)), (1, inner, length), (2,))
    small = jnp.concatenate([betas, log_decay[None], gain], 0)
    vmem = pl.BlockSpec(memory_space=pltpu.VMEM)
    hbm = pl.BlockSpec(memory_space=pltpu.HBM)
    dma = pltpu.SemaphoreType.DMA
    return pl.pallas_call(
        functools.partial(whole_kernel, inner, outer),
        in_specs=[hbm] * 3 + [vmem],
        out_specs=vmem,
        out_shape=jax.ShapeDtypeStruct((length, width), BF16),
        scratch_shapes=[
            pltpu.VMEM((8, 128, 256), BF16),
            pltpu.VMEM((chips, length, 256), BF16),
            *[pltpu.VMEM((chips, 2, length, 256), BF16)] * 2,
            *[pltpu.VMEM((chips, 2, blocks, 128, 256), F32)] * 2,
            pltpu.VMEM((chips, 2, blocks, 8, 128), F32),
            *[pltpu.VMEM((chips, 128, 256), F32)] * 6,
            pltpu.VMEM((2, 128, 256), F32),
            pltpu.VMEM((2, outer, 128, 128), F32),
            pltpu.VMEM((2, 128, 128), F32),
            *[pltpu.VMEM((chips, 128, 128), F32)] * 4,
            *[pltpu.VMEM((chips, 2, length, 128), F32)] * 2,
            *[dma((chips,))] * 3,
            *[dma((chips,))] * 4,
            *[dma((outer,))] * 2,
            *[dma((chips,))] * 4,
            *[dma((outer,))] * 2,
        ],
        compiler_params=pltpu.CompilerParams(
            collective_id=0, has_side_effects=True, vmem_limit_bytes=53 * 1024 * 1024
        ),
        name="whole",
    )(queries, keys, values, small)


HIGHEST = lax.Precision.HIGHEST


def join(earlier, later):
    moved = jnp.einsum("hde,hef->hdf", later[..., :128], earlier, precision=HIGHEST)
    return jnp.concatenate([moved[..., :128], moved[..., 128:] + later[..., 128:]], -1)


def entering(pairs, axis, begin):
    gathered = lax.all_gather(pairs, axis)

    def one(hop, state):
        return join(state, lax.dynamic_index_in_dim(gathered, hop, 0, False))

    return lax.fori_loop(0, lax.axis_index(axis), one, begin)


def exchange_plain(pairs):
    eye = jnp.concatenate([jnp.eye(128, dtype=F32), jnp.zeros((128, 128), F32)], 1)
    begin = jnp.zeros_like(pairs) + eye
    before = entering(pairs, "inner", begin)
    through = join(before, pairs)
    last = lax.axis_index("inner") == lax.axis_size("inner") - 1
    total = lax.psum(jnp.where(last, through, 0.0), "inner")
    start = entering(total, "outer", begin)
    return join(start, before)[..., 128:]


def finish_kernel(c_ref, b_ref, e_ref, g_ref, o_ref):
    readout = mul(c_ref[0], e_ref[0]) + b_ref[0]
    mean_sq = jnp.mean(readout * readout, 1, keepdims=True)
    o_ref[...] = (readout * lax.rsqrt(mean_sq + 1e-05) * g_ref[...]).astype(BF16)


def finish(carried, base, state, out_gain):
    heads, length, _ = carried.shape
    return pl.pallas_call(
        finish_kernel,
        grid=(heads,),
        in_specs=[
            pl.BlockSpec((1, length, 128), lambda h: (h, 0, 0)),
            pl.BlockSpec((1, length, 128), lambda h: (h, 0, 0)),
            pl.BlockSpec((1, 128, 128), lambda h: (h, 0, 0)),
            pl.BlockSpec((1, 128), lambda h: (0, 0)),
        ],
        out_specs=pl.BlockSpec((length, 128), lambda h: (0, h)),
        out_shape=jax.ShapeDtypeStruct((length, heads * 128), BF16),
        name="finish",
    )(carried, base, state, out_gain.reshape(1, 128))


def per_device(inner, outer, queries, keys, values, betas, log_decay, out_gain):
    heads = betas.shape[1]
    if inner == heads == 8:
        return whole(inner, outer, queries, keys, values, betas, log_decay, out_gain)
    pairs, carried, base = local_phase(queries, keys, values, betas, log_decay)
    return finish(carried, base, exchange_plain(pairs), out_gain)


def solution(mesh):
    both = ("outer", "inner")
    placed = (P(both, None), P(None, both, None), P(None, both, None), P(None, None, both), P(None, both), P())
    return jax.shard_map(
        functools.partial(per_device, mesh.shape["inner"], mesh.shape["outer"]),
        mesh=mesh,
        in_specs=placed,
        out_specs=P(both, None),
        check_vma=False,
    )
```

```python
import functools

import jax
import jax.numpy as jnp
from jax import lax
from jax.experimental import pallas as pl
from jax.experimental.pallas import tpu as pltpu
from jax.sharding import PartitionSpec as P

BLOCK_LEN = 64
F32 = jnp.float32
BF16 = jnp.bfloat16


def split(x):
    high = x.astype(BF16)
    low = (x - high.astype(F32)).astype(BF16)
    return high, low


def dot(a, b):
    return lax.dot_general(a, b, (((1,), (0,)), ((), ())), preferred_element_type=F32)


def dot_t(a, b):
    return lax.dot_general(a, b, (((1,), (1,)), ((), ())), preferred_element_type=F32)


def wide(x):
    return jnp.concatenate(split(x), 1)


def mul(a, b):
    a2 = wide(a)
    bh, bl = split(b)
    if b.shape[1] == 128:
        row = jnp.concatenate([bh, bl], 1)
        both = dot(a2, jnp.concatenate([row, row], 0))
        return both[:, :128] + both[:, 128:]
    return dot(a2, jnp.concatenate([bh, bh], 0)) + dot(a2[:, :128], bl)


def mul_left(a, b):
    return dot(wide(a), jnp.concatenate([b, b], 0))


def add_right(x, y):
    return jnp.concatenate([x[:, :128], x[:, 128:] + y], 1)


def masks():
    span = BLOCK_LEN
    size = 2 * span
    row = lax.broadcasted_iota(jnp.int32, (size, size), 0)
    col = lax.broadcasted_iota(jnp.int32, (size, size), 1)
    row_t, col_t = row & (span - 1), col & (span - 1)
    row_rank = 2 * row_t + (row >= span).astype(jnp.int32)
    col_rank = 2 * col_t + (col >= span).astype(jnp.int32)
    differ = row_rank ^ col_rank
    eye = row == col
    eye_f = eye.astype(F32)
    lower = row_rank > col_rank
    c_mask = (col_t <= row_t) & (col < span)
    r_mask = (row_t <= col_t) & (row < span)
    levels = []
    width = 1
    while width < size:
        levels.append(
            (differ >= width) & (differ < 2 * width) & lower
        )
        width *= 2

    return row, col_t, row_t, eye, eye_f, lower, c_mask, r_mask, levels


def head_maps(blocks, heads_in, load, emit):
    span = BLOCK_LEN
    row, col_t, row_t, eye, eye_f, lower, c_mask, r_mask, levels = masks()
    work = []
    for i, n in [(i, n) for i in range(heads_in) for n in range(blocks)]:
        q_b, k_b, v_b, d_row, beta_row = load(i, n)
        d_col = jnp.sum(jnp.where(eye, d_row, 0.0), 1, keepdims=True)
        beta_col = jnp.sum(jnp.where(eye, beta_row, 0.0), 1, keepdims=True)
        c_col = jnp.sum(jnp.where(c_mask, d_row, 0.0), 1, keepdims=True)
        c_row = jnp.sum(jnp.where(r_mask, d_col, 0.0), 0, keepdims=True)
        gram = dot_t(k_b, k_b)
        k_f = k_b.astype(F32)
        q_f = q_b.astype(F32)
        ki_col = lax.rsqrt(jnp.sum(k_f * k_f, 1, keepdims=True) + 1e-06)
        ki_row = lax.rsqrt(jnp.sum(jnp.where(eye, gram, 0.0), 0, keepdims=True) + 1e-06)
        qi_col = lax.rsqrt(jnp.sum(q_f * q_f, 1, keepdims=True) + 1e-06)
        fall = jnp.exp(jnp.minimum(c_col - c_row, 0.0))
        low = jnp.where(lower, gram * (beta_col * ki_col) * ki_row * fall, 0.0)
        reach = dot_t(q_b, k_b) * qi_col * ki_row * fall[:span]
        reach = jnp.where(col_t[:span] <= row_t[:span], reach, 0.0)
        query = q_f * (qi_col * jnp.exp(c_col[:span]))
        work.append((k_b, v_b, beta_row, c_row, c_col, ki_row, ki_col, low, reach, query))

    inverse = [eye_f - jnp.where(levels[0], w[7], 0.0) for w in work]
    for mask in levels[1:]:
        part = [mul(jnp.where(mask, w[7], 0.0), t) for w, t in zip(work, inverse)]
        inverse = [t - mul(t, p) for t, p in zip(inverse, part)]

    states = [None] * heads_in
    for n in range(blocks):
        for i in range(heads_in):
            state = states[i]
            k_b, v_b, beta_row, c_row, c_col, ki_row, ki_col, low, reach, query = work[i * blocks + n]
            t = inverse[i * blocks + n] * beta_row
            written = jnp.concatenate(
                [mul_left(t * (ki_row * jnp.exp(c_row)), k_b), mul_left(t, v_b)], 1
            )
            got = mul(reach, written)
            reduced, local_out = query - got[:, :128], got[:, 128:]
            last = c_col[span - 1 : span, :]
            tail = jnp.exp(last - c_col) * ki_col
            wh, wl = split(written * tail)
            k_t = jnp.transpose(k_b.astype(F32)).astype(BF16)
            made = dot(jnp.concatenate([k_t, k_t], 1), jnp.concatenate([wh, wl], 0))
            trans = jnp.exp(last) * eye_f - made[:, :128]
            inject = made[:, 128:]
            if state is None:
                emit(i, n, reduced, local_out)
                states[i] = jnp.concatenate([trans, inject], 1)
            else:
                read = mul(reduced, state)
                emit(i, n, read[:, :128], read[:, 128:] + local_out)
                states[i] = add_right(mul(trans, state), inject)
    return states


def local_kernel(blocks, q_ref, k_ref, v_ref, s_ref, x_ref, c_ref, b_ref):
    def load(i, n):
        at = pl.ds(n * BLOCK_LEN, BLOCK_LEN)
        k_b = jnp.concatenate([k_ref[0, at, :], k_ref[1, at, :]], 0)
        v_b = jnp.concatenate([v_ref[0, at, :], v_ref[1, at, :]], 0)
        return q_ref[at, :], k_b, v_b, s_ref[0, n : n + 1, :], s_ref[0, blocks + n : blocks + n + 1, :]

    def emit(i, n, carried, base):
        at = pl.ds(n * BLOCK_LEN, BLOCK_LEN)
        c_ref[0, at, :] = carried
        b_ref[0, at, :] = base

    x_ref[0] = head_maps(blocks, 1, load, emit)[0]


def small_rows(betas, log_decay):
    heads, length = log_decay.shape
    blocks = length // BLOCK_LEN
    beta = betas.reshape(2, heads, blocks, BLOCK_LEN).transpose(1, 2, 0, 3)
    beta = beta.reshape(heads, blocks, 2 * BLOCK_LEN)
    decay = log_decay.reshape(heads, blocks, 1, BLOCK_LEN)
    decay = jnp.concatenate([decay, decay], 2).reshape(heads, blocks, 2 * BLOCK_LEN)
    small = jnp.concatenate([decay, beta], 1)
    return small


def local_phase(queries, keys, values, betas, log_decay):
    length = queries.shape[0]
    heads = betas.shape[1]
    blocks = length // BLOCK_LEN
    small = small_rows(betas, log_decay)
    return pl.pallas_call(
        functools.partial(local_kernel, blocks),
        grid=(heads,),
        in_specs=[
            pl.BlockSpec((length, 128), lambda h: (0, h)),
            pl.BlockSpec((2, length, 128), lambda h: (0, 0, h)),
            pl.BlockSpec((2, length, 128), lambda h: (0, 0, h)),
            pl.BlockSpec((1, 2 * blocks, 128), lambda h: (h, 0, 0)),
        ],
        out_specs=[
            pl.BlockSpec((1, 128, 256), lambda h: (h, 0, 0)),
            pl.BlockSpec((1, length, 128), lambda h: (h, 0, 0)),
            pl.BlockSpec((1, length, 128), lambda h: (h, 0, 0)),
        ],
        out_shape=[
            jax.ShapeDtypeStruct((heads, 128, 256), F32),
            jax.ShapeDtypeStruct((heads, length, 128), F32),
            jax.ShapeDtypeStruct((heads, length, 128), F32),
        ],
        name="local_phase",
    )(queries, keys, values, small)


def then(earlier, later):
    return add_right(mul(later[:, :128], earlier), later[:, 128:])


def normed(carried, base, state, gain):
    readout = mul(carried, state) + base
    mean_sq = jnp.mean(readout * readout, 1, keepdims=True)
    return (readout * lax.rsqrt(mean_sq + 1e-05) * gain).astype(BF16)


LOG2E = 1.4426950408889634


def split3(x):
    high = x.astype(BF16)
    rest = x - high.astype(F32)
    mid = rest.astype(BF16)
    low = rest - mid.astype(F32)
    return high.astype(F32), mid.astype(F32), low


def tokens_of(shape, dim):
    at = lax.broadcasted_iota(jnp.int32, shape, dim)
    return at & (BLOCK_LEN - 1), at >> 6


def fill_spread(spread_ref):
    t_r, j_r = tokens_of((128, 128), 0)
    t_c, j_c = tokens_of((128, 128), 1)
    rank = 2 * (t_r & 7) + j_r
    same = (t_r >> 3) == (t_c >> 3)
    for p in range(8):
        parts = [jnp.where(same & (rank == 2 * p + q), 1.0, 0.0) for q in range(2)]
        spread_ref[p] = jnp.concatenate(parts, 1).astype(BF16)


def odd_starts(width):
    return [j * BLOCK_LEN + t for j in range(2) for t in range(width, BLOCK_LEN, 2 * width)]


def odd_rows(x, width):
    return jnp.concatenate([x[s : s + width] for s in odd_starts(width)], 0)


def stacked(left, right):
    rows = left[0].shape[0]
    both = dot(jnp.concatenate(left, 0), jnp.concatenate(right, 1))
    return both[:rows, :128] + (both[:rows, 128:] + both[rows:, :128])


def systems(blocks, heads_in, load, spread_ref):
    units = [(i, n) for i in range(heads_in) for n in range(blocks)]
    count = len(units)
    loaded = [load(i, n) for i, n in units]
    t_r, j_r = tokens_of((128, 128), 0)
    t_c, j_c = tokens_of((128, 128), 1)
    eye = (t_r == t_c) & (j_r == j_c)
    running = jnp.where((t_r <= t_c) & (j_r == 0), 1.0, 0.0).astype(BF16)
    decay = jnp.concatenate([u[1] for u in loaded], 0)
    beta = jnp.concatenate([u[2] for u in loaded], 0)
    total = dot(
        jnp.concatenate(split3(decay), 1).astype(BF16), jnp.concatenate([running] * 3, 0)
    )
    grams = [dot_t(u[0], u[0]) for u in loaded]
    squares = jnp.concatenate([jnp.sum(jnp.where(eye, g, 0.0), 0, keepdims=True) for g in grams], 0) + 1e-06
    inv = lax.rsqrt(squares)
    inv_log = -0.5 * jnp.log2(squares)
    fallen = total * LOG2E
    last = fallen[:, BLOCK_LEN - 1 : BLOCK_LEN]
    scale_k = jnp.exp2(fallen) * inv
    tail = jnp.exp2(last - fallen) * inv
    keep_all = jnp.exp2(last)
    ones = jnp.ones((count, 128), F32)
    zeros = jnp.zeros((count, 128), F32)
    stack = [*split3(fallen + inv_log), ones, ones, ones, *split3(beta), *split3(tail)]
    columns = jnp.transpose(jnp.concatenate(stack + [zeros] * (128 // count - len(stack)), 0)).astype(BF16)
    later = split3(inv_log - fallen)
    sub = lax.broadcasted_iota(jnp.int32, (count, 128), 0)

    lane_t, lane_j = tokens_of((8, 128), 1)
    row8 = lax.broadcasted_iota(jnp.int32, (8, 128), 0)
    in_block = [(lane_t >> 3) == b for b in range(8)]
    lane_rank = 2 * (lane_t & 7) + lane_j
    lower_0, lower_1 = 2 * row8 > lane_rank, 2 * row8 + 1 > lane_rank
    first_0 = jnp.where(2 * row8 == lane_rank, 1.0, 0.0)
    first_1 = jnp.where(2 * row8 + 1 == lane_rank, 1.0, 0.0)
    t16 = lax.broadcasted_iota(jnp.int32, (128, 128), 0) & (BLOCK_LEN - 1)
    own_block = jnp.where((t16 >> 3) == (t_c >> 3), 1.0, 0.0).astype(BF16)

    lows, tails, compact = [], [], []
    for u in range(count):
        pick = sub == u
        one = jnp.where(pick, 1.0, 0.0)
        right = [one] * 3 + [jnp.where(pick, g, 0.0) for g in later]
        none = [zeros]
        fill = 128 // count
        cols = [
            right + none * (fill - 6),
            none * 6 + [one] * 3 + none * (fill - 9),
            none * 9 + [one] * 3 + none * (fill - 12),
        ]
        right = jnp.concatenate([jnp.concatenate(c, 0) for c in cols], 1).astype(BF16)
        spread = dot(columns, right)
        low = grams[u] * jnp.exp2(spread[:, :128]) * spread[:, 128:256]
        lows.append(low)
        tails.append(spread[:, 256:])
        for j, lower in ((0, lower_0), (1, lower_1)):
            part = low[j * BLOCK_LEN : j * BLOCK_LEN + 8]
            for b in range(1, 8):
                at = j * BLOCK_LEN + 8 * b
                part = jnp.where(in_block[b], low[at : at + 8], part)
            compact.append(jnp.where(lower, part, 0.0))

    packed = wide(jnp.concatenate(compact, 0))
    pairs = [dot(packed, jnp.concatenate([spread_ref[p]] * 2, 0)) for p in range(8)]
    small = [[first_0, first_1] for _ in range(count)]
    for s in range(15):
        t, j, lanes = s // 2, s % 2, slice(128 * (s % 2), 128 * (s % 2) + 128)
        for u in range(count):
            x0, x1 = small[u]
            source = (x0, x1)[j][t : t + 1]
            coef = pairs[s // 2][16 * u : 16 * u + 16, lanes]
            small[u] = [x0 - coef[:8] * source, x1 - coef[8:] * source]

    highs, slims, updates = [], [], [[] for _ in range(count)]
    pair_of_8 = []
    for u in range(count):
        tiles = []
        for x in small[u]:
            both = jnp.concatenate([x, x], 0)
            tiles.append(split(both))
        high = jnp.concatenate([tiles[0][0]] * 4 + [tiles[1][0]] * 4, 0)
        slim = jnp.concatenate([tiles[0][1]] * 4 + [tiles[1][1]] * 4, 0)
        highs.append(high * own_block)
        slims.append(slim * own_block)
        pair_of_8.append(tiles)

    q = lax.broadcasted_iota(jnp.int32, (64, 128), 0) & 31
    c_t = lax.broadcasted_iota(jnp.int32, (64, 128), 1) & (BLOCK_LEN - 1)
    for width in (8, 16, 32):
        bits = width.bit_length()
        row_t = ((q >> (bits - 1)) << bits) + width + (q & (width - 1))
        mask = ((c_t & width) == 0) & ((c_t >> bits) == (row_t >> bits))
        if width == 8:
            odd_own = jnp.where((c_t >> 3) == (row_t >> 3), 1.0, 0.0).astype(BF16)
        parts = []
        for u in range(count):
            a = split(jnp.where(mask, odd_rows(lows[u], width), 0.0))
            parts.append(stacked(a, (highs[u], slims[u])))
        for u in range(count):
            p = parts[u]
            if width == 8:
                ph = p.astype(BF16).astype(F32)
                pl_ = p - ph
                doubled = [
                    jnp.concatenate([x[8 * (g // 2) : 8 * (g // 2) + 8] for g in range(16)], 0).astype(BF16)
                    for x in (ph, pl_)
                ]
                tiles = pair_of_8[u]
                odd = [jnp.concatenate([tiles[0][k]] * 2 + [tiles[1][k]] * 2, 0) * odd_own for k in range(2)]
            else:
                groups = range(64 // width)
                doubled = [
                    jnp.concatenate([x[width * g : width * g + width] for g in groups for _ in range(2)], 0)
                    for x in split(p)
                ]
                odd = [odd_rows(highs[u], width), odd_rows(slims[u], width)]
            update = stacked(odd, doubled)
            updates[u].append(update)
            if width == 32:
                continue
            if width == 8:
                uh = update.astype(BF16).astype(F32)
                gap = jnp.zeros((8, 128), F32)
                spaced = [
                    jnp.concatenate(
                        [x[8 * (g // 2) : 8 * (g // 2) + 8] if g % 2 else gap for g in range(16)], 0
                    ).astype(BF16)
                    for x in (uh, update - uh)
                ]
            else:
                gap = jnp.zeros((width, 128), BF16)
                spaced = [
                    jnp.concatenate(
                        [
                            x[width * (g // 2) : width * (g // 2) + width] if g % 2 else gap
                            for g in range(128 // width)
                        ],
                        0,
                    )
                    for x in split(update)
                ]
            highs[u] = highs[u] - spaced[0]
            slims[u] = slims[u] - spaced[1]

    work = []
    for u in range(count):
        rows = []
        for j in range(2):
            for b in range(8):
                x = jnp.where(in_block[b], small[u][j], 0.0)
                for width, update in zip((8, 16, 32), updates[u]):
                    t = 8 * b
                    if t & width:
                        at = j * 32 + (t // (2 * width)) * width + t % width
                        x = x - update[at : at + 8]
                rows.append(x)
        at = slice(u, u + 1)
        inverse = jnp.concatenate(rows, 0)
        work.append((inverse, beta[at], scale_k[at], tails[u], keep_all[at], total[at], inv[at]))
    return work, jnp.where(eye, 1.0, 0.0)


def state_maps(blocks, heads_in, work, eye_f, load_kv, keep):
    units = [(i, n) for n in range(blocks) for i in range(heads_in)]
    wrote, pieces = {}, {}
    for i, n in units:
        k_b, v_b = load_kv(i, n)
        inverse, beta_row, scale_k = work[i * blocks + n][:3]
        t = inverse * beta_row
        wrote[i, n] = mul_left(t * scale_k, k_b), mul_left(t, v_b)
    for i, n in units:
        k_b, _ = load_kv(i, n)
        tail, keep_all = work[i * blocks + n][3:5]
        wk, wv = wrote[i, n]
        wh, wl = split(jnp.concatenate([wk * tail, wv * tail], 1))
        k_t = jnp.transpose(k_b.astype(F32)).astype(BF16)
        made = dot(jnp.concatenate([k_t, k_t], 1), jnp.concatenate([wh, wl], 0))
        pieces[i, n] = jnp.concatenate([keep_all * eye_f - made[:, :128], made[:, 128:]], 1)
    firsts = [then(pieces[i, 0], pieces[i, 1]) for i in range(heads_in)]
    seconds = [then(pieces[i, 2], pieces[i, 3]) for i in range(heads_in)]
    states = [then(a, b) for a, b in zip(firsts, seconds)]
    for i, n in units:
        c_row, ki_row = work[i * blocks + n][5:7]
        part = (None, pieces[i, 0], firsts[i], pieces[i, 2])[n]
        keep(i, n, jnp.concatenate(wrote[i, n], 1), c_row, ki_row, part)
    return states


def reads(blocks, heads_in, load, emit):
    span = BLOCK_LEN
    row = lax.broadcasted_iota(jnp.int32, (span, 2 * span), 0)
    col = lax.broadcasted_iota(jnp.int32, (span, 2 * span), 1)
    col_t = col & (span - 1)
    seen = col_t <= row
    for i, n in [(i, n) for i in range(heads_in) for n in range(blocks)]:
        q_b, k_b, d_row, written, c_row, ki_row, state = load(i, n)
        c_col = jnp.sum(jnp.where(seen & (col < span), d_row, 0.0), 1, keepdims=True)
        q_f = q_b.astype(F32)
        qi_col = lax.rsqrt(jnp.sum(q_f * q_f, 1, keepdims=True) + 1e-06)
        fall = jnp.exp(jnp.minimum(c_col - c_row, 0.0))
        reach = jnp.where(seen, dot_t(q_b, k_b) * qi_col * ki_row * fall, 0.0)
        query = q_f * (qi_col * jnp.exp(c_col))
        got = mul(reach, written)
        reduced, local_out = query - got[:, :128], got[:, 128:]
        if n == 0:
            emit(i, n, reduced, local_out)
        else:
            read = mul(reduced, state)
            emit(i, n, read[:, :128], read[:, 128:] + local_out)


def whole_kernel(
    inner, outer, q_hbm, k_hbm, v_hbm, small_ref, o_ref,
    spread_buf, q_buf, k_buf, v_buf, w_buf, p_buf, vec_buf,
    away, near, own, even_map, sent, got, pair_buf, groups, mine, ready, came, aside, beside, c_buf, b_buf,
    load_k, load_v, load_q,
    send0, recv0, send1, recv1, send2, recv2, send3, recv3, send4, recv4, send5, recv5,
):
    mesh_id = pl.DeviceIdType.MESH
    length = q_hbm.shape[0]
    blocks = length // BLOCK_LEN
    me = lax.axis_index("inner")
    group = lax.axis_index("outer")
    core, chip, chips = me % 2, me // 2, inner // 2
    partner = chip * 2 + 1 - core
    groups[...] = jnp.zeros_like(groups)
    barrier = pltpu.get_barrier_semaphore()
    for d in range(1, chips):
        pl.semaphore_signal(
            barrier, inc=1, device_id=(group, (chip + d) % chips * 2 + core), device_id_type=mesh_id
        )
    pl.semaphore_signal(barrier, inc=1, device_id=(group, partner), device_id_type=mesh_id)
    for d in range(1, outer):
        pl.semaphore_signal(barrier, inc=1, device_id=((group + d) % outer, me), device_id_type=mesh_id)

    def flip(x):
        return (chip % 2 + x % 2) % 2 + (chip // 2 + x // 2) % 2 * 2

    def target(turn):
        return flip(chips - 1 - turn)

    def lanes_of(turn):
        return pl.ds(pl.multiple_of(target(turn) * 256, 256), 256)

    def k_copy(turn):
        return pltpu.make_async_copy(k_hbm.at[:, :, lanes_of(turn)], k_buf.at[turn], load_k.at[turn])

    def v_copy(turn):
        return pltpu.make_async_copy(v_hbm.at[:, :, lanes_of(turn)], v_buf.at[turn], load_v.at[turn])

    def q_copy(turn):
        return pltpu.make_async_copy(q_hbm.at[:, lanes_of(turn)], q_buf.at[turn], load_q.at[turn])

    for t in range(chips):
        k_copy(t).start()
        v_copy(t).start()
    for t in range(chips):
        q_copy(t).start()

    fill_spread(spread_buf)

    def near_copy(turn):
        return pltpu.make_async_remote_copy(
            src_ref=away.at[turn], dst_ref=near.at[turn],
            send_sem=send0.at[turn], recv_sem=recv0.at[turn],
            device_id=(group, partner), device_id_type=mesh_id,
        )

    def map_copy(d):
        return pltpu.make_async_remote_copy(
            src_ref=sent.at[d], dst_ref=got.at[d],
            send_sem=send1.at[d], recv_sem=recv1.at[d],
            device_id=(group, flip(chips - d) * 2 + core), device_id_type=mesh_id,
        )

    def chip_map(turn):
        near_copy(turn).wait()
        here, there = own[turn], near[turn]
        even = jnp.where(core == 0, here, there)
        odd = jnp.where(core == 0, there, here)
        even_map[turn] = even
        return then(even, odd)

    def parity(i):
        return core if i == 0 else 1 - core

    def head_lanes(i):
        return pl.ds(pl.multiple_of(parity(i) * 128, 128), 128)

    def rows_of(head, n):
        at = slice(n * BLOCK_LEN, (n + 1) * BLOCK_LEN)
        row = pl.ds(head, 1)
        b0, b1 = small_ref[0, row, :][:, at], small_ref[1, row, :][:, at]
        d = small_ref[2, row, :][:, at]
        return jnp.concatenate([d, d], 1), jnp.concatenate([b0, b1], 1)

    def pair_of(buf, turn, i, n):
        at = pl.ds(n * BLOCK_LEN, BLOCK_LEN)
        return jnp.concatenate([buf[turn, 0, at, head_lanes(i)], buf[turn, 1, at, head_lanes(i)]], 0)

    def step(turn, carry):
        heads = [target(turn) * 2 + parity(i) for i in range(2)]
        k_copy(turn).wait()

        def load(i, n):
            d_row, beta_row = rows_of(heads[i], n)
            return pair_of(k_buf, turn, i, n), d_row, beta_row

        work, eye_f = systems(blocks, 2, load, spread_buf)

        @pl.when(turn == 0)
        def _():
            pl.semaphore_wait(barrier, chips + outer - 1)

        @pl.when(turn > 0)
        def _():
            sent[turn] = chip_map(turn - 1)
            map_copy(turn).start()

        v_copy(turn).wait()

        def load_kv(i, n):
            return pair_of(k_buf, turn, i, n), pair_of(v_buf, turn, i, n)

        def keep(i, n, written, c_row, ki_row, state):
            w_buf[turn, i, n] = written
            vec_buf[turn, i, n, 0:1, :] = c_row
            vec_buf[turn, i, n, 1:2, :] = ki_row
            if n:
                p_buf[turn, i, n] = state

        states = state_maps(blocks, 2, work, eye_f, load_kv, keep)
        away[turn] = states[1]
        own[turn] = states[0]

        near_copy(turn).start()
        return carry

    lax.fori_loop(0, chips, step, 0)

    def read_step(turn, carry):
        heads = [target(turn) * 2 + parity(i) for i in range(2)]
        q_copy(turn).wait()

        before = []
        for i in range(2):
            first = p_buf[turn, i, 2]
            before.append([None, p_buf[turn, i, 1], first, then(first, p_buf[turn, i, 3])])

        def load(i, n):
            at = pl.ds(n * BLOCK_LEN, BLOCK_LEN)
            d_row, _ = rows_of(heads[i], n)
            return (
                q_buf[turn, at, head_lanes(i)], pair_of(k_buf, turn, i, n), d_row, w_buf[turn, i, n],
                vec_buf[turn, i, n, 0:1, :], vec_buf[turn, i, n, 1:2, :], before[i][n],
            )

        def emit(i, n, carried, base):
            at = pl.ds(n * BLOCK_LEN, BLOCK_LEN)
            c_buf[turn, i, at, :] = carried
            b_buf[turn, i, at, :] = base

        reads(blocks, 2, load, emit)
        return carry

    lax.fori_loop(0, chips // 2, read_step, 0)
    def slot(i):
        return (chips - flip(i)) % chips

    def pair_map(side):
        return then(got[slot(2 * side)], got[slot(2 * side + 1)])

    got[0] = chip_map(chips - 1)
    map_copy(1).wait()
    map_copy(2).wait()
    pair_buf[1 - chip // 2] = pair_map(1 - chip // 2)
    map_copy(3).wait()
    pair_buf[chip // 2] = pair_map(chip // 2)
    total = then(pair_buf[0], pair_buf[1])
    mine[0] = total[:, :128]
    mine[1] = total[:, 128:]

    def group_copy(part, d):
        sems = (send2, recv2) if part == 0 else (send5, recv5)
        return pltpu.make_async_remote_copy(
            src_ref=mine.at[part], dst_ref=groups.at[part, d],
            send_sem=sems[0].at[d], recv_sem=sems[1].at[d],
            device_id=((group + d) % outer, me), device_id_type=mesh_id,
        )

    for d in range(1, outer):

        @pl.when(group + d < outer)
        def _():
            group_copy(1, d).start()

    for d in range(1, outer):

        @pl.when((group + d < outer) & (group > 0))
        def _():
            group_copy(0, d).start()

    before = [None, got[slot(0)], pair_buf[0], then(pair_buf[0], got[slot(2)])]
    left = wide(jnp.concatenate([before[i][:, :128] for i in range(1, chips)], 0))
    right = jnp.concatenate([before[i][:, 128:] for i in range(1, chips)], 0)

    lax.fori_loop(chips // 2, chips, read_step, 0)

    start = jnp.zeros((128, 128), F32)
    for g in range(outer - 1):
        at = (group - g + outer) % outer

        @pl.when(group > g)
        def _():
            group_copy(1, at).wait_recv()
            if g:
                group_copy(0, at).wait_recv()

        moved = groups[1, at]
        if g:
            moved = mul(groups[0, at], start) + moved
        start = jnp.where(g < group, moved, start)

    sh, sl = split(start)
    row = jnp.concatenate([sh, sl], 1)
    both = dot(left, jnp.concatenate([row, row], 0))
    ready[0] = start
    ready[pl.ds(1, chips - 1)] = (both[:, :128] + both[:, 128:] + right).reshape(chips - 1, 128, 128)

    def back_copy(d):
        to = flip(d)
        return pltpu.make_async_remote_copy(
            src_ref=ready.at[to], dst_ref=came.at[d],
            send_sem=send3.at[d], recv_sem=recv3.at[d],
            device_id=(group, to * 2 + core), device_id_type=mesh_id,
        )

    def side_copy(d):
        return pltpu.make_async_remote_copy(
            src_ref=aside.at[d], dst_ref=beside.at[d],
            send_sem=send4.at[d], recv_sem=recv4.at[d],
            device_id=(group, partner), device_id_type=mesh_id,
        )

    for d in range(1, chips):
        back_copy(d).start()

    def out(turn, i, state):
        head = target(turn) * 2 + parity(i)
        lanes = pl.ds(pl.multiple_of(head * 128, 128), 128)
        o_ref[:, lanes] = normed(c_buf[turn, i], b_buf[turn, i], state, small_ref[3, 0:1, :128])

    for d in range(chips):
        turn = chips - 1 - d
        if d:
            back_copy(d).wait_recv()
            enter = came[d]
        else:
            enter = ready[chip]
        pair = even_map[turn]
        after = mul(pair[:, :128], enter) + pair[:, 128:]
        aside[d] = jnp.where(core == 0, after, enter)
        side_copy(d).start()
        out(turn, 0, jnp.where(core == 0, enter, after))
        if d:
            side_copy(d - 1).wait_recv()
            out(turn + 1, 1, beside[d - 1])
    side_copy(chips - 1).wait_recv()
    out(0, 1, beside[chips - 1])
    for d in range(chips):
        if d:
            back_copy(d).wait_send()
        side_copy(d).wait_send()
    for d in range(1, outer):

        @pl.when(group + d < outer)
        def _():
            group_copy(1, d).wait_send()

        @pl.when((group + d < outer) & (group > 0))
        def _():
            group_copy(0, d).wait_send()


def whole(inner, outer, queries, keys, values, betas, log_decay, out_gain):
    length, width = queries.shape
    blocks = length // BLOCK_LEN
    chips = inner // 2
    gain = lax.broadcast_in_dim(jnp.pad(out_gain, (0, length - 128)), (1, inner, length), (2,))
    small = jnp.concatenate([betas, log_decay[None], gain], 0)
    vmem = pl.BlockSpec(memory_space=pltpu.VMEM)
    hbm = pl.BlockSpec(memory_space=pltpu.HBM)
    dma = pltpu.SemaphoreType.DMA
    return pl.pallas_call(
        functools.partial(whole_kernel, inner, outer),
        in_specs=[hbm] * 3 + [vmem],
        out_specs=vmem,
        out_shape=jax.ShapeDtypeStruct((length, width), BF16),
        scratch_shapes=[
            pltpu.VMEM((8, 128, 256), BF16),
            pltpu.VMEM((chips, length, 256), BF16),
            *[pltpu.VMEM((chips, 2, length, 256), BF16)] * 2,
            *[pltpu.VMEM((chips, 2, blocks, 128, 256), F32)] * 2,
            pltpu.VMEM((chips, 2, blocks, 8, 128), F32),
            *[pltpu.VMEM((chips, 128, 256), F32)] * 6,
            pltpu.VMEM((2, 128, 256), F32),
            pltpu.VMEM((2, outer, 128, 128), F32),
            pltpu.VMEM((2, 128, 128), F32),
            *[pltpu.VMEM((chips, 128, 128), F32)] * 4,
            *[pltpu.VMEM((chips, 2, length, 128), F32)] * 2,
            *[dma((chips,))] * 3,
            *[dma((chips,))] * 4,
            *[dma((outer,))] * 2,
            *[dma((chips,))] * 4,
            *[dma((outer,))] * 2,
        ],
        compiler_params=pltpu.CompilerParams(
            collective_id=0, has_side_effects=True, vmem_limit_bytes=53 * 1024 * 1024
        ),
        name="whole",
    )(queries, keys, values, small)


HIGHEST = lax.Precision.HIGHEST


def join(earlier, later):
    moved = jnp.einsum("hde,hef->hdf", later[..., :128], earlier, precision=HIGHEST)
    return jnp.concatenate([moved[..., :128], moved[..., 128:] + later[..., 128:]], -1)


def entering(pairs, axis, begin):
    gathered = lax.all_gather(pairs, axis)

    def one(hop, state):
        return join(state, lax.dynamic_index_in_dim(gathered, hop, 0, False))

    return lax.fori_loop(0, lax.axis_index(axis), one, begin)


def exchange_plain(pairs):
    eye = jnp.concatenate([jnp.eye(128, dtype=F32), jnp.zeros((128, 128), F32)], 1)
    begin = jnp.zeros_like(pairs) + eye
    before = entering(pairs, "inner", begin)
    through = join(before, pairs)
    last = lax.axis_index("inner") == lax.axis_size("inner") - 1
    total = lax.psum(jnp.where(last, through, 0.0), "inner")
    start = entering(total, "outer", begin)
    return join(start, before)[..., 128:]


def finish_kernel(c_ref, b_ref, e_ref, g_ref, o_ref):
    readout = mul(c_ref[0], e_ref[0]) + b_ref[0]
    mean_sq = jnp.mean(readout * readout, 1, keepdims=True)
    o_ref[...] = (readout * lax.rsqrt(mean_sq + 1e-05) * g_ref[...]).astype(BF16)


def finish(carried, base, state, out_gain):
    heads, length, _ = carried.shape
    return pl.pallas_call(
        finish_kernel,
        grid=(heads,),
        in_specs=[
            pl.BlockSpec((1, length, 128), lambda h: (h, 0, 0)),
            pl.BlockSpec((1, length, 128), lambda h: (h, 0, 0)),
            pl.BlockSpec((1, 128, 128), lambda h: (h, 0, 0)),
            pl.BlockSpec((1, 128), lambda h: (0, 0)),
        ],
        out_specs=pl.BlockSpec((length, 128), lambda h: (0, h)),
        out_shape=jax.ShapeDtypeStruct((length, heads * 128), BF16),
        name="finish",
    )(carried, base, state, out_gain.reshape(1, 128))


def per_device(inner, outer, queries, keys, values, betas, log_decay, out_gain):
    heads = betas.shape[1]
    if inner == heads == 8:
        return whole(inner, outer, queries, keys, values, betas, log_decay, out_gain)
    pairs, carried, base = local_phase(queries, keys, values, betas, log_decay)
    return finish(carried, base, exchange_plain(pairs), out_gain)


def solution(mesh):
    both = ("outer", "inner")
    placed = (P(both, None), P(None, both, None), P(None, both, None), P(None, None, both), P(None, both), P())
    return jax.shard_map(
        functools.partial(per_device, mesh.shape["inner"], mesh.shape["outer"]),
        mesh=mesh,
        in_specs=placed,
        out_specs=P(both, None),
        check_vma=False,
    )
```

```python
import functools

import jax
import jax.numpy as jnp
from jax import lax
from jax.experimental import pallas as pl
from jax.experimental.pallas import tpu as pltpu
from jax.sharding import PartitionSpec as P

BLOCK_LEN = 64
F32 = jnp.float32
BF16 = jnp.bfloat16


def split(x):
    high = x.astype(BF16)
    low = (x - high.astype(F32)).astype(BF16)
    return high, low


def dot(a, b):
    return lax.dot_general(a, b, (((1,), (0,)), ((), ())), preferred_element_type=F32)


def dot_t(a, b):
    return lax.dot_general(a, b, (((1,), (1,)), ((), ())), preferred_element_type=F32)


def wide(x):
    return jnp.concatenate(split(x), 1)


def mul(a, b):
    a2 = wide(a)
    bh, bl = split(b)
    if b.shape[1] == 128:
        row = jnp.concatenate([bh, bl], 1)
        both = dot(a2, jnp.concatenate([row, row], 0))
        return both[:, :128] + both[:, 128:]
    return dot(a2, jnp.concatenate([bh, bh], 0)) + dot(a2[:, :128], bl)


def mul_left(a, b):
    return dot(wide(a), jnp.concatenate([b, b], 0))


def add_right(x, y):
    return jnp.concatenate([x[:, :128], x[:, 128:] + y], 1)


def masks():
    span = BLOCK_LEN
    size = 2 * span
    row = lax.broadcasted_iota(jnp.int32, (size, size), 0)
    col = lax.broadcasted_iota(jnp.int32, (size, size), 1)
    row_t, col_t = row & (span - 1), col & (span - 1)
    row_rank = 2 * row_t + (row >= span).astype(jnp.int32)
    col_rank = 2 * col_t + (col >= span).astype(jnp.int32)
    differ = row_rank ^ col_rank
    eye = row == col
    eye_f = eye.astype(F32)
    lower = row_rank > col_rank
    c_mask = (col_t <= row_t) & (col < span)
    r_mask = (row_t <= col_t) & (row < span)
    levels = []
    width = 1
    while width < size:
        levels.append(
            (differ >= width) & (differ < 2 * width) & lower
        )
        width *= 2

    return row, col_t, row_t, eye, eye_f, lower, c_mask, r_mask, levels


def head_maps(blocks, heads_in, load, emit):
    span = BLOCK_LEN
    row, col_t, row_t, eye, eye_f, lower, c_mask, r_mask, levels = masks()
    work = []
    for i, n in [(i, n) for i in range(heads_in) for n in range(blocks)]:
        q_b, k_b, v_b, d_row, beta_row = load(i, n)
        d_col = jnp.sum(jnp.where(eye, d_row, 0.0), 1, keepdims=True)
        beta_col = jnp.sum(jnp.where(eye, beta_row, 0.0), 1, keepdims=True)
        c_col = jnp.sum(jnp.where(c_mask, d_row, 0.0), 1, keepdims=True)
        c_row = jnp.sum(jnp.where(r_mask, d_col, 0.0), 0, keepdims=True)
        gram = dot_t(k_b, k_b)
        k_f = k_b.astype(F32)
        q_f = q_b.astype(F32)
        ki_col = lax.rsqrt(jnp.sum(k_f * k_f, 1, keepdims=True) + 1e-06)
        ki_row = lax.rsqrt(jnp.sum(jnp.where(eye, gram, 0.0), 0, keepdims=True) + 1e-06)
        qi_col = lax.rsqrt(jnp.sum(q_f * q_f, 1, keepdims=True) + 1e-06)
        fall = jnp.exp(jnp.minimum(c_col - c_row, 0.0))
        low = jnp.where(lower, gram * (beta_col * ki_col) * ki_row * fall, 0.0)
        reach = dot_t(q_b, k_b) * qi_col * ki_row * fall[:span]
        reach = jnp.where(col_t[:span] <= row_t[:span], reach, 0.0)
        query = q_f * (qi_col * jnp.exp(c_col[:span]))
        work.append((k_b, v_b, beta_row, c_row, c_col, ki_row, ki_col, low, reach, query))

    inverse = [eye_f - jnp.where(levels[0], w[7], 0.0) for w in work]
    for mask in levels[1:]:
        part = [mul(jnp.where(mask, w[7], 0.0), t) for w, t in zip(work, inverse)]
        inverse = [t - mul(t, p) for t, p in zip(inverse, part)]

    states = [None] * heads_in
    for n in range(blocks):
        for i in range(heads_in):
            state = states[i]
            k_b, v_b, beta_row, c_row, c_col, ki_row, ki_col, low, reach, query = work[i * blocks + n]
            t = inverse[i * blocks + n] * beta_row
            written = jnp.concatenate(
                [mul_left(t * (ki_row * jnp.exp(c_row)), k_b), mul_left(t, v_b)], 1
            )
            got = mul(reach, written)
            reduced, local_out = query - got[:, :128], got[:, 128:]
            last = c_col[span - 1 : span, :]
            tail = jnp.exp(last - c_col) * ki_col
            wh, wl = split(written * tail)
            k_t = jnp.transpose(k_b.astype(F32)).astype(BF16)
            made = dot(jnp.concatenate([k_t, k_t], 1), jnp.concatenate([wh, wl], 0))
            trans = jnp.exp(last) * eye_f - made[:, :128]
            inject = made[:, 128:]
            if state is None:
                emit(i, n, reduced, local_out)
                states[i] = jnp.concatenate([trans, inject], 1)
            else:
                read = mul(reduced, state)
                emit(i, n, read[:, :128], read[:, 128:] + local_out)
                states[i] = add_right(mul(trans, state), inject)
    return states


def local_kernel(blocks, q_ref, k_ref, v_ref, s_ref, x_ref, c_ref, b_ref):
    def load(i, n):
        at = pl.ds(n * BLOCK_LEN, BLOCK_LEN)
        k_b = jnp.concatenate([k_ref[0, at, :], k_ref[1, at, :]], 0)
        v_b = jnp.concatenate([v_ref[0, at, :], v_ref[1, at, :]], 0)
        return q_ref[at, :], k_b, v_b, s_ref[0, n : n + 1, :], s_ref[0, blocks + n : blocks + n + 1, :]

    def emit(i, n, carried, base):
        at = pl.ds(n * BLOCK_LEN, BLOCK_LEN)
        c_ref[0, at, :] = carried
        b_ref[0, at, :] = base

    x_ref[0] = head_maps(blocks, 1, load, emit)[0]


def small_rows(betas, log_decay):
    heads, length = log_decay.shape
    blocks = length // BLOCK_LEN
    beta = betas.reshape(2, heads, blocks, BLOCK_LEN).transpose(1, 2, 0, 3)
    beta = beta.reshape(heads, blocks, 2 * BLOCK_LEN)
    decay = log_decay.reshape(heads, blocks, 1, BLOCK_LEN)
    decay = jnp.concatenate([decay, decay], 2).reshape(heads, blocks, 2 * BLOCK_LEN)
    small = jnp.concatenate([decay, beta], 1)
    return small


def local_phase(queries, keys, values, betas, log_decay):
    length = queries.shape[0]
    heads = betas.shape[1]
    blocks = length // BLOCK_LEN
    small = small_rows(betas, log_decay)
    return pl.pallas_call(
        functools.partial(local_kernel, blocks),
        grid=(heads,),
        in_specs=[
            pl.BlockSpec((length, 128), lambda h: (0, h)),
            pl.BlockSpec((2, length, 128), lambda h: (0, 0, h)),
            pl.BlockSpec((2, length, 128), lambda h: (0, 0, h)),
            pl.BlockSpec((1, 2 * blocks, 128), lambda h: (h, 0, 0)),
        ],
        out_specs=[
            pl.BlockSpec((1, 128, 256), lambda h: (h, 0, 0)),
            pl.BlockSpec((1, length, 128), lambda h: (h, 0, 0)),
            pl.BlockSpec((1, length, 128), lambda h: (h, 0, 0)),
        ],
        out_shape=[
            jax.ShapeDtypeStruct((heads, 128, 256), F32),
            jax.ShapeDtypeStruct((heads, length, 128), F32),
            jax.ShapeDtypeStruct((heads, length, 128), F32),
        ],
        name="local_phase",
    )(queries, keys, values, small)


def then(earlier, later):
    return add_right(mul(later[:, :128], earlier), later[:, 128:])


def normed(carried, base, state, gain):
    readout = mul(carried, state) + base
    mean_sq = jnp.mean(readout * readout, 1, keepdims=True)
    return (readout * lax.rsqrt(mean_sq + 1e-05) * gain).astype(BF16)


LOG2E = 1.4426950408889634


def split3(x):
    high = x.astype(BF16)
    rest = x - high.astype(F32)
    mid = rest.astype(BF16)
    low = rest - mid.astype(F32)
    return high.astype(F32), mid.astype(F32), low


def tokens_of(shape, dim):
    at = lax.broadcasted_iota(jnp.int32, shape, dim)
    return at & (BLOCK_LEN - 1), at >> 6


def fill_spread(spread_ref):
    t_r, j_r = tokens_of((128, 128), 0)
    t_c, j_c = tokens_of((128, 128), 1)
    rank = 2 * (t_r & 7) + j_r
    same = (t_r >> 3) == (t_c >> 3)
    for p in range(8):
        parts = [jnp.where(same & (rank == 2 * p + q), 1.0, 0.0) for q in range(2)]
        spread_ref[p] = jnp.concatenate(parts, 1).astype(BF16)


def odd_starts(width):
    return [j * BLOCK_LEN + t for j in range(2) for t in range(width, BLOCK_LEN, 2 * width)]


def odd_rows(x, width):
    return jnp.concatenate([x[s : s + width] for s in odd_starts(width)], 0)


def stacked(left, right):
    rows = left[0].shape[0]
    both = dot(jnp.concatenate(left, 0), jnp.concatenate(right, 1))
    return both[:rows, :128] + (both[:rows, 128:] + both[rows:, :128])


def systems(blocks, heads_in, load, spread_ref):
    units = [(i, n) for i in range(heads_in) for n in range(blocks)]
    count = len(units)
    loaded = [load(i, n) for i, n in units]
    t_r, j_r = tokens_of((128, 128), 0)
    t_c, j_c = tokens_of((128, 128), 1)
    eye = (t_r == t_c) & (j_r == j_c)
    running = jnp.where((t_r <= t_c) & (j_r == 0), 1.0, 0.0).astype(BF16)
    decay = jnp.concatenate([u[1] for u in loaded], 0)
    beta = jnp.concatenate([u[2] for u in loaded], 0)
    total = dot(
        jnp.concatenate(split3(decay), 1).astype(BF16), jnp.concatenate([running] * 3, 0)
    )
    grams = [dot_t(u[0], u[0]) for u in loaded]
    squares = jnp.concatenate([jnp.sum(jnp.where(eye, g, 0.0), 0, keepdims=True) for g in grams], 0) + 1e-06
    inv = lax.rsqrt(squares)
    inv_log = -0.5 * jnp.log2(squares)
    fallen = total * LOG2E
    last = fallen[:, BLOCK_LEN - 1 : BLOCK_LEN]
    scale_k = jnp.exp2(fallen) * inv
    tail = jnp.exp2(last - fallen) * inv
    keep_all = jnp.exp2(last)
    ones = jnp.ones((count, 128), F32)
    zeros = jnp.zeros((count, 128), F32)
    stack = [*split3(fallen + inv_log), ones, ones, ones, *split3(beta), *split3(tail)]
    columns = jnp.transpose(jnp.concatenate(stack + [zeros] * (128 // count - len(stack)), 0)).astype(BF16)
    later = split3(inv_log - fallen)
    sub = lax.broadcasted_iota(jnp.int32, (count, 128), 0)

    lane_t, lane_j = tokens_of((8, 128), 1)
    row8 = lax.broadcasted_iota(jnp.int32, (8, 128), 0)
    in_block = [(lane_t >> 3) == b for b in range(8)]
    lane_rank = 2 * (lane_t & 7) + lane_j
    lower_0, lower_1 = 2 * row8 > lane_rank, 2 * row8 + 1 > lane_rank
    first_0 = jnp.where(2 * row8 == lane_rank, 1.0, 0.0)
    first_1 = jnp.where(2 * row8 + 1 == lane_rank, 1.0, 0.0)
    t16 = lax.broadcasted_iota(jnp.int32, (128, 128), 0) & (BLOCK_LEN - 1)
    own_block = jnp.where((t16 >> 3) == (t_c >> 3), 1.0, 0.0).astype(BF16)

    lows, tails, compact = [], [], []
    for u in range(count):
        pick = sub == u
        one = jnp.where(pick, 1.0, 0.0)
        right = [one] * 3 + [jnp.where(pick, g, 0.0) for g in later]
        none = [zeros]
        fill = 128 // count
        cols = [
            right + none * (fill - 6),
            none * 6 + [one] * 3 + none * (fill - 9),
            none * 9 + [one] * 3 + none * (fill - 12),
        ]
        right = jnp.concatenate([jnp.concatenate(c, 0) for c in cols], 1).astype(BF16)
        spread = dot(columns, right)
        low = grams[u] * jnp.exp2(spread[:, :128]) * spread[:, 128:256]
        lows.append(low)
        tails.append(spread[:, 256:])
        for j, lower in ((0, lower_0), (1, lower_1)):
            part = low[j * BLOCK_LEN : j * BLOCK_LEN + 8]
            for b in range(1, 8):
                at = j * BLOCK_LEN + 8 * b
                part = jnp.where(in_block[b], low[at : at + 8], part)
            compact.append(jnp.where(lower, part, 0.0))

    packed = wide(jnp.concatenate(compact, 0))
    pairs = [dot(packed, jnp.concatenate([spread_ref[p]] * 2, 0)) for p in range(8)]
    small = [[first_0, first_1] for _ in range(count)]
    for s in range(15):
        t, j, lanes = s // 2, s % 2, slice(128 * (s % 2), 128 * (s % 2) + 128)
        for u in range(count):
            x0, x1 = small[u]
            source = (x0, x1)[j][t : t + 1]
            coef = pairs[s // 2][16 * u : 16 * u + 16, lanes]
            small[u] = [x0 - coef[:8] * source, x1 - coef[8:] * source]

    highs, slims, updates = [], [], [[] for _ in range(count)]
    pair_of_8 = []
    for u in range(count):
        tiles = []
        for x in small[u]:
            both = jnp.concatenate([x, x], 0)
            tiles.append(split(both))
        high = jnp.concatenate([tiles[0][0]] * 4 + [tiles[1][0]] * 4, 0)
        slim = jnp.concatenate([tiles[0][1]] * 4 + [tiles[1][1]] * 4, 0)
        highs.append(high * own_block)
        slims.append(slim * own_block)
        pair_of_8.append(tiles)

    q = lax.broadcasted_iota(jnp.int32, (64, 128), 0) & 31
    c_t = lax.broadcasted_iota(jnp.int32, (64, 128), 1) & (BLOCK_LEN - 1)
    for width in (8, 16, 32):
        bits = width.bit_length()
        row_t = ((q >> (bits - 1)) << bits) + width + (q & (width - 1))
        mask = ((c_t & width) == 0) & ((c_t >> bits) == (row_t >> bits))
        if width == 8:
            odd_own = jnp.where((c_t >> 3) == (row_t >> 3), 1.0, 0.0).astype(BF16)
        parts = []
        for u in range(count):
            a = split(jnp.where(mask, odd_rows(lows[u], width), 0.0))
            parts.append(stacked(a, (highs[u], slims[u])))
        for u in range(count):
            p = parts[u]
            if width == 8:
                ph = p.astype(BF16).astype(F32)
                pl_ = p - ph
                doubled = [
                    jnp.concatenate([x[8 * (g // 2) : 8 * (g // 2) + 8] for g in range(16)], 0).astype(BF16)
                    for x in (ph, pl_)
                ]
                tiles = pair_of_8[u]
                odd = [jnp.concatenate([tiles[0][k]] * 2 + [tiles[1][k]] * 2, 0) * odd_own for k in range(2)]
            else:
                groups = range(64 // width)
                doubled = [
                    jnp.concatenate([x[width * g : width * g + width] for g in groups for _ in range(2)], 0)
                    for x in split(p)
                ]
                odd = [odd_rows(highs[u], width), odd_rows(slims[u], width)]
            update = stacked(odd, doubled)
            updates[u].append(update)
            if width == 32:
                continue
            if width == 8:
                uh = update.astype(BF16).astype(F32)
                gap = jnp.zeros((8, 128), F32)
                spaced = [
                    jnp.concatenate(
                        [x[8 * (g // 2) : 8 * (g // 2) + 8] if g % 2 else gap for g in range(16)], 0
                    ).astype(BF16)
                    for x in (uh, update - uh)
                ]
            else:
                gap = jnp.zeros((width, 128), BF16)
                spaced = [
                    jnp.concatenate(
                        [
                            x[width * (g // 2) : width * (g // 2) + width] if g % 2 else gap
                            for g in range(128 // width)
                        ],
                        0,
                    )
                    for x in split(update)
                ]
            highs[u] = highs[u] - spaced[0]
            slims[u] = slims[u] - spaced[1]

    work = []
    for u in range(count):
        rows = []
        for j in range(2):
            for b in range(8):
                x = jnp.where(in_block[b], small[u][j], 0.0)
                for width, update in zip((8, 16, 32), updates[u]):
                    t = 8 * b
                    if t & width:
                        at = j * 32 + (t // (2 * width)) * width + t % width
                        x = x - update[at : at + 8]
                rows.append(x)
        at = slice(u, u + 1)
        inverse = jnp.concatenate(rows, 0)
        work.append((inverse, beta[at], scale_k[at], tails[u], keep_all[at], total[at], inv[at]))
    return work, jnp.where(eye, 1.0, 0.0)


def state_maps(blocks, heads_in, work, eye_f, load_kv, keep):
    units = [(i, n) for n in range(blocks) for i in range(heads_in)]
    wrote, pieces = {}, {}
    for i, n in units:
        k_b, v_b = load_kv(i, n)
        inverse, beta_row, scale_k = work[i * blocks + n][:3]
        t = inverse * beta_row
        wrote[i, n] = mul_left(t * scale_k, k_b), mul_left(t, v_b)
    for i, n in units:
        k_b, _ = load_kv(i, n)
        tail, keep_all = work[i * blocks + n][3:5]
        wk, wv = wrote[i, n]
        wh, wl = split(jnp.concatenate([wk * tail, wv * tail], 1))
        k_t = jnp.transpose(k_b.astype(F32)).astype(BF16)
        made = dot(jnp.concatenate([k_t, k_t], 1), jnp.concatenate([wh, wl], 0))
        pieces[i, n] = jnp.concatenate([keep_all * eye_f - made[:, :128], made[:, 128:]], 1)
    firsts = [then(pieces[i, 0], pieces[i, 1]) for i in range(heads_in)]
    seconds = [then(pieces[i, 2], pieces[i, 3]) for i in range(heads_in)]
    states = [then(a, b) for a, b in zip(firsts, seconds)]
    for i, n in units:
        c_row, ki_row = work[i * blocks + n][5:7]
        part = (None, pieces[i, 0], firsts[i], pieces[i, 2])[n]
        keep(i, n, jnp.concatenate(wrote[i, n], 1), c_row, ki_row, part)
    return states


def reads(blocks, heads_in, load, emit):
    span = BLOCK_LEN
    row = lax.broadcasted_iota(jnp.int32, (span, 2 * span), 0)
    col = lax.broadcasted_iota(jnp.int32, (span, 2 * span), 1)
    col_t = col & (span - 1)
    seen = col_t <= row
    for i, n in [(i, n) for i in range(heads_in) for n in range(blocks)]:
        q_b, k_b, d_row, written, c_row, ki_row, state = load(i, n)
        c_col = jnp.sum(jnp.where(seen & (col < span), d_row, 0.0), 1, keepdims=True)
        q_f = q_b.astype(F32)
        qi_col = lax.rsqrt(jnp.sum(q_f * q_f, 1, keepdims=True) + 1e-06)
        fall = jnp.exp(jnp.minimum(c_col - c_row, 0.0))
        reach = jnp.where(seen, dot_t(q_b, k_b) * qi_col * ki_row * fall, 0.0)
        query = q_f * (qi_col * jnp.exp(c_col))
        got = mul(reach, written)
        reduced, local_out = query - got[:, :128], got[:, 128:]
        if n == 0:
            emit(i, n, reduced, local_out)
        else:
            read = mul(reduced, state)
            emit(i, n, read[:, :128], read[:, 128:] + local_out)


def whole_kernel(
    inner, outer, q_hbm, k_hbm, v_hbm, small_ref, o_ref,
    spread_buf, q_buf, k_buf, v_buf, w_buf, p_buf, vec_buf,
    away, near, own, even_map, sent, got, pair_buf, groups, mine, ready, came, aside, beside, c_buf, b_buf,
    load_k, load_v, load_q,
    send0, recv0, send1, recv1, send2, recv2, send3, recv3, send4, recv4, send5, recv5,
):
    mesh_id = pl.DeviceIdType.MESH
    length = q_hbm.shape[0]
    blocks = length // BLOCK_LEN
    me = lax.axis_index("inner")
    group = lax.axis_index("outer")
    core, chip, chips = me % 2, me // 2, inner // 2
    partner = chip * 2 + 1 - core
    groups[...] = jnp.zeros_like(groups)
    barrier = pltpu.get_barrier_semaphore()
    for d in range(1, chips):
        pl.semaphore_signal(
            barrier, inc=1, device_id=(group, (chip + d) % chips * 2 + core), device_id_type=mesh_id
        )
    pl.semaphore_signal(barrier, inc=1, device_id=(group, partner), device_id_type=mesh_id)
    for d in range(1, outer):
        pl.semaphore_signal(barrier, inc=1, device_id=((group + d) % outer, me), device_id_type=mesh_id)

    def flip(x):
        return (chip % 2 + x % 2) % 2 + (chip // 2 + x // 2) % 2 * 2

    def target(turn):
        return flip(chips - 1 - turn)

    def lanes_of(turn):
        return pl.ds(pl.multiple_of(target(turn) * 256, 256), 256)

    def k_copy(turn):
        return pltpu.make_async_copy(k_hbm.at[:, :, lanes_of(turn)], k_buf.at[turn], load_k.at[turn])

    def v_copy(turn):
        return pltpu.make_async_copy(v_hbm.at[:, :, lanes_of(turn)], v_buf.at[turn], load_v.at[turn])

    def q_copy(turn):
        return pltpu.make_async_copy(q_hbm.at[:, lanes_of(turn)], q_buf.at[turn], load_q.at[turn])

    for t in range(chips):
        k_copy(t).start()
        v_copy(t).start()
    for t in range(chips):
        q_copy(t).start()

    fill_spread(spread_buf)

    def near_copy(turn):
        return pltpu.make_async_remote_copy(
            src_ref=away.at[turn], dst_ref=near.at[turn],
            send_sem=send0.at[turn], recv_sem=recv0.at[turn],
            device_id=(group, partner), device_id_type=mesh_id,
        )

    def map_copy(d):
        return pltpu.make_async_remote_copy(
            src_ref=sent.at[d], dst_ref=got.at[d],
            send_sem=send1.at[d], recv_sem=recv1.at[d],
            device_id=(group, flip(chips - d) * 2 + core), device_id_type=mesh_id,
        )

    def chip_map(turn):
        near_copy(turn).wait()
        here, there = own[turn], near[turn]
        even = jnp.where(core == 0, here, there)
        odd = jnp.where(core == 0, there, here)
        even_map[turn] = even
        return then(even, odd)

    def parity(i):
        return core if i == 0 else 1 - core

    def head_lanes(i):
        return pl.ds(pl.multiple_of(parity(i) * 128, 128), 128)

    def rows_of(head, n):
        at = slice(n * BLOCK_LEN, (n + 1) * BLOCK_LEN)
        row = pl.ds(head, 1)
        b0, b1 = small_ref[0, row, :][:, at], small_ref[1, row, :][:, at]
        d = small_ref[2, row, :][:, at]
        return jnp.concatenate([d, d], 1), jnp.concatenate([b0, b1], 1)

    def pair_of(buf, turn, i, n):
        at = pl.ds(n * BLOCK_LEN, BLOCK_LEN)
        return jnp.concatenate([buf[turn, 0, at, head_lanes(i)], buf[turn, 1, at, head_lanes(i)]], 0)

    def step(turn, carry):
        heads = [target(turn) * 2 + parity(i) for i in range(2)]
        k_copy(turn).wait()

        def load(i, n):
            d_row, beta_row = rows_of(heads[i], n)
            return pair_of(k_buf, turn, i, n), d_row, beta_row

        work, eye_f = systems(blocks, 2, load, spread_buf)

        @pl.when(turn == 0)
        def _():
            pl.semaphore_wait(barrier, chips + outer - 1)

        @pl.when(turn > 0)
        def _():
            sent[turn] = chip_map(turn - 1)
            map_copy(turn).start()

        v_copy(turn).wait()

        def load_kv(i, n):
            return pair_of(k_buf, turn, i, n), pair_of(v_buf, turn, i, n)

        def keep(i, n, written, c_row, ki_row, state):
            w_buf[turn, i, n] = written
            vec_buf[turn, i, n, 0:1, :] = c_row
            vec_buf[turn, i, n, 1:2, :] = ki_row
            if n:
                p_buf[turn, i, n] = state

        states = state_maps(blocks, 2, work, eye_f, load_kv, keep)
        away[turn] = states[1]
        own[turn] = states[0]

        near_copy(turn).start()
        return carry

    lax.fori_loop(0, chips, step, 0)

    def read_step(turn, carry):
        heads = [target(turn) * 2 + parity(i) for i in range(2)]
        q_copy(turn).wait()

        before = []
        for i in range(2):
            first = p_buf[turn, i, 2]
            before.append([None, p_buf[turn, i, 1], first, then(first, p_buf[turn, i, 3])])

        def load(i, n):
            at = pl.ds(n * BLOCK_LEN, BLOCK_LEN)
            d_row, _ = rows_of(heads[i], n)
            return (
                q_buf[turn, at, head_lanes(i)], pair_of(k_buf, turn, i, n), d_row, w_buf[turn, i, n],
                vec_buf[turn, i, n, 0:1, :], vec_buf[turn, i, n, 1:2, :], before[i][n],
            )

        def emit(i, n, carried, base):
            at = pl.ds(n * BLOCK_LEN, BLOCK_LEN)
            c_buf[turn, i, at, :] = carried
            b_buf[turn, i, at, :] = base

        reads(blocks, 2, load, emit)
        return carry

    lax.fori_loop(0, chips // 2, read_step, 0)
    def slot(i):
        return (chips - flip(i)) % chips

    def pair_map(side):
        return then(got[slot(2 * side)], got[slot(2 * side + 1)])

    got[0] = chip_map(chips - 1)
    map_copy(1).wait()
    map_copy(2).wait()
    pair_buf[1 - chip // 2] = pair_map(1 - chip // 2)
    map_copy(3).wait()
    pair_buf[chip // 2] = pair_map(chip // 2)
    total = then(pair_buf[0], pair_buf[1])
    mine[0] = total[:, :128]
    mine[1] = total[:, 128:]

    def group_copy(part, d):
        sems = (send2, recv2) if part == 0 else (send5, recv5)
        return pltpu.make_async_remote_copy(
            src_ref=mine.at[part], dst_ref=groups.at[part, d],
            send_sem=sems[0].at[d], recv_sem=sems[1].at[d],
            device_id=((group + d) % outer, me), device_id_type=mesh_id,
        )

    for d in range(1, outer):

        @pl.when(group + d < outer)
        def _():
            group_copy(1, d).start()

    for d in range(1, outer):

        @pl.when((group + d < outer) & (group > 0))
        def _():
            group_copy(0, d).start()

    before = [None, got[slot(0)], pair_buf[0], then(pair_buf[0], got[slot(2)])]
    left = wide(jnp.concatenate([before[i][:, :128] for i in range(1, chips)], 0))
    right = jnp.concatenate([before[i][:, 128:] for i in range(1, chips)], 0)

    lax.fori_loop(chips // 2, chips, read_step, 0)

    start = jnp.zeros((128, 128), F32)
    for g in range(outer - 1):
        at = (group - g + outer) % outer

        @pl.when(group > g)
        def _():
            group_copy(1, at).wait_recv()
            if g:
                group_copy(0, at).wait_recv()

        moved = groups[1, at]
        if g:
            moved = mul(groups[0, at], start) + moved
        start = jnp.where(g < group, moved, start)

    sh, sl = split(start)
    row = jnp.concatenate([sh, sl], 1)
    both = dot(left, jnp.concatenate([row, row], 0))
    ready[0] = start
    ready[pl.ds(1, chips - 1)] = (both[:, :128] + both[:, 128:] + right).reshape(chips - 1, 128, 128)

    def back_copy(d):
        to = flip(d)
        return pltpu.make_async_remote_copy(
            src_ref=ready.at[to], dst_ref=came.at[d],
            send_sem=send3.at[d], recv_sem=recv3.at[d],
            device_id=(group, to * 2 + core), device_id_type=mesh_id,
        )

    def side_copy(d):
        return pltpu.make_async_remote_copy(
            src_ref=aside.at[d], dst_ref=beside.at[d],
            send_sem=send4.at[d], recv_sem=recv4.at[d],
            device_id=(group, partner), device_id_type=mesh_id,
        )

    for d in (1, 3, 2):
        back_copy(d).start()

    def out(turn, i, state):
        head = target(turn) * 2 + parity(i)
        lanes = pl.ds(pl.multiple_of(head * 128, 128), 128)
        o_ref[:, lanes] = normed(c_buf[turn, i], b_buf[turn, i], state, small_ref[3, 0:1, :128])

    for d in range(chips):
        turn = chips - 1 - d
        if d:
            back_copy(d).wait_recv()
            enter = came[d]
        else:
            enter = ready[chip]
        pair = even_map[turn]
        after = mul(pair[:, :128], enter) + pair[:, 128:]
        aside[d] = jnp.where(core == 0, after, enter)
        side_copy(d).start()
        out(turn, 0, jnp.where(core == 0, enter, after))
        if d:
            side_copy(d - 1).wait_recv()
            out(turn + 1, 1, beside[d - 1])
    side_copy(chips - 1).wait_recv()
    out(0, 1, beside[chips - 1])
    for d in range(chips):
        if d:
            back_copy(d).wait_send()
        side_copy(d).wait_send()
    for d in range(1, outer):

        @pl.when(group + d < outer)
        def _():
            group_copy(1, d).wait_send()

        @pl.when((group + d < outer) & (group > 0))
        def _():
            group_copy(0, d).wait_send()


def whole(inner, outer, queries, keys, values, betas, log_decay, out_gain):
    length, width = queries.shape
    blocks = length // BLOCK_LEN
    chips = inner // 2
    gain = lax.broadcast_in_dim(jnp.pad(out_gain, (0, length - 128)), (1, inner, length), (2,))
    small = jnp.concatenate([betas, log_decay[None], gain], 0)
    vmem = pl.BlockSpec(memory_space=pltpu.VMEM)
    hbm = pl.BlockSpec(memory_space=pltpu.HBM)
    dma = pltpu.SemaphoreType.DMA
    return pl.pallas_call(
        functools.partial(whole_kernel, inner, outer),
        in_specs=[hbm] * 3 + [vmem],
        out_specs=vmem,
        out_shape=jax.ShapeDtypeStruct((length, width), BF16),
        scratch_shapes=[
            pltpu.VMEM((8, 128, 256), BF16),
            pltpu.VMEM((chips, length, 256), BF16),
            *[pltpu.VMEM((chips, 2, length, 256), BF16)] * 2,
            *[pltpu.VMEM((chips, 2, blocks, 128, 256), F32)] * 2,
            pltpu.VMEM((chips, 2, blocks, 8, 128), F32),
            *[pltpu.VMEM((chips, 128, 256), F32)] * 6,
            pltpu.VMEM((2, 128, 256), F32),
            pltpu.VMEM((2, outer, 128, 128), F32),
            pltpu.VMEM((2, 128, 128), F32),
            *[pltpu.VMEM((chips, 128, 128), F32)] * 4,
            *[pltpu.VMEM((chips, 2, length, 128), F32)] * 2,
            *[dma((chips,))] * 3,
            *[dma((chips,))] * 4,
            *[dma((outer,))] * 2,
            *[dma((chips,))] * 4,
            *[dma((outer,))] * 2,
        ],
        compiler_params=pltpu.CompilerParams(
            collective_id=0, has_side_effects=True, vmem_limit_bytes=53 * 1024 * 1024
        ),
        name="whole",
    )(queries, keys, values, small)


HIGHEST = lax.Precision.HIGHEST


def join(earlier, later):
    moved = jnp.einsum("hde,hef->hdf", later[..., :128], earlier, precision=HIGHEST)
    return jnp.concatenate([moved[..., :128], moved[..., 128:] + later[..., 128:]], -1)


def entering(pairs, axis, begin):
    gathered = lax.all_gather(pairs, axis)

    def one(hop, state):
        return join(state, lax.dynamic_index_in_dim(gathered, hop, 0, False))

    return lax.fori_loop(0, lax.axis_index(axis), one, begin)


def exchange_plain(pairs):
    eye = jnp.concatenate([jnp.eye(128, dtype=F32), jnp.zeros((128, 128), F32)], 1)
    begin = jnp.zeros_like(pairs) + eye
    before = entering(pairs, "inner", begin)
    through = join(before, pairs)
    last = lax.axis_index("inner") == lax.axis_size("inner") - 1
    total = lax.psum(jnp.where(last, through, 0.0), "inner")
    start = entering(total, "outer", begin)
    return join(start, before)[..., 128:]


def finish_kernel(c_ref, b_ref, e_ref, g_ref, o_ref):
    readout = mul(c_ref[0], e_ref[0]) + b_ref[0]
    mean_sq = jnp.mean(readout * readout, 1, keepdims=True)
    o_ref[...] = (readout * lax.rsqrt(mean_sq + 1e-05) * g_ref[...]).astype(BF16)


def finish(carried, base, state, out_gain):
    heads, length, _ = carried.shape
    return pl.pallas_call(
        finish_kernel,
        grid=(heads,),
        in_specs=[
            pl.BlockSpec((1, length, 128), lambda h: (h, 0, 0)),
            pl.BlockSpec((1, length, 128), lambda h: (h, 0, 0)),
            pl.BlockSpec((1, 128, 128), lambda h: (h, 0, 0)),
            pl.BlockSpec((1, 128), lambda h: (0, 0)),
        ],
        out_specs=pl.BlockSpec((length, 128), lambda h: (0, h)),
        out_shape=jax.ShapeDtypeStruct((length, heads * 128), BF16),
        name="finish",
    )(carried, base, state, out_gain.reshape(1, 128))


def per_device(inner, outer, queries, keys, values, betas, log_decay, out_gain):
    heads = betas.shape[1]
    if inner == heads == 8:
        return whole(inner, outer, queries, keys, values, betas, log_decay, out_gain)
    pairs, carried, base = local_phase(queries, keys, values, betas, log_decay)
    return finish(carried, base, exchange_plain(pairs), out_gain)


def solution(mesh):
    both = ("outer", "inner")
    placed = (P(both, None), P(None, both, None), P(None, both, None), P(None, None, both), P(None, both), P())
    return jax.shard_map(
        functools.partial(per_device, mesh.shape["inner"], mesh.shape["outer"]),
        mesh=mesh,
        in_specs=placed,
        out_specs=P(both, None),
        check_vma=False,
    )
```

```python
import functools

import jax
import jax.numpy as jnp
from jax import lax
from jax.experimental import pallas as pl
from jax.experimental.pallas import tpu as pltpu
from jax.sharding import PartitionSpec as P

BLOCK_LEN = 64
F32 = jnp.float32
BF16 = jnp.bfloat16


def split(x):
    high = x.astype(BF16)
    low = (x - high.astype(F32)).astype(BF16)
    return high, low


def dot(a, b):
    return lax.dot_general(a, b, (((1,), (0,)), ((), ())), preferred_element_type=F32)


def dot_t(a, b):
    return lax.dot_general(a, b, (((1,), (1,)), ((), ())), preferred_element_type=F32)


def wide(x):
    return jnp.concatenate(split(x), 1)


def mul(a, b):
    a2 = wide(a)
    bh, bl = split(b)
    if b.shape[1] == 128:
        row = jnp.concatenate([bh, bl], 1)
        both = dot(a2, jnp.concatenate([row, row], 0))
        return both[:, :128] + both[:, 128:]
    return dot(a2, jnp.concatenate([bh, bh], 0)) + dot(a2[:, :128], bl)


def mul_left(a, b):
    return dot(wide(a), jnp.concatenate([b, b], 0))


def add_right(x, y):
    return jnp.concatenate([x[:, :128], x[:, 128:] + y], 1)


def masks():
    span = BLOCK_LEN
    size = 2 * span
    row = lax.broadcasted_iota(jnp.int32, (size, size), 0)
    col = lax.broadcasted_iota(jnp.int32, (size, size), 1)
    row_t, col_t = row & (span - 1), col & (span - 1)
    row_rank = 2 * row_t + (row >= span).astype(jnp.int32)
    col_rank = 2 * col_t + (col >= span).astype(jnp.int32)
    differ = row_rank ^ col_rank
    eye = row == col
    eye_f = eye.astype(F32)
    lower = row_rank > col_rank
    c_mask = (col_t <= row_t) & (col < span)
    r_mask = (row_t <= col_t) & (row < span)
    levels = []
    width = 1
    while width < size:
        levels.append(
            (differ >= width) & (differ < 2 * width) & lower
        )
        width *= 2

    return row, col_t, row_t, eye, eye_f, lower, c_mask, r_mask, levels


def head_maps(blocks, heads_in, load, emit):
    span = BLOCK_LEN
    row, col_t, row_t, eye, eye_f, lower, c_mask, r_mask, levels = masks()
    work = []
    for i, n in [(i, n) for i in range(heads_in) for n in range(blocks)]:
        q_b, k_b, v_b, d_row, beta_row = load(i, n)
        d_col = jnp.sum(jnp.where(eye, d_row, 0.0), 1, keepdims=True)
        beta_col = jnp.sum(jnp.where(eye, beta_row, 0.0), 1, keepdims=True)
        c_col = jnp.sum(jnp.where(c_mask, d_row, 0.0), 1, keepdims=True)
        c_row = jnp.sum(jnp.where(r_mask, d_col, 0.0), 0, keepdims=True)
        gram = dot_t(k_b, k_b)
        k_f = k_b.astype(F32)
        q_f = q_b.astype(F32)
        ki_col = lax.rsqrt(jnp.sum(k_f * k_f, 1, keepdims=True) + 1e-06)
        ki_row = lax.rsqrt(jnp.sum(jnp.where(eye, gram, 0.0), 0, keepdims=True) + 1e-06)
        qi_col = lax.rsqrt(jnp.sum(q_f * q_f, 1, keepdims=True) + 1e-06)
        fall = jnp.exp(jnp.minimum(c_col - c_row, 0.0))
        low = jnp.where(lower, gram * (beta_col * ki_col) * ki_row * fall, 0.0)
        reach = dot_t(q_b, k_b) * qi_col * ki_row * fall[:span]
        reach = jnp.where(col_t[:span] <= row_t[:span], reach, 0.0)
        query = q_f * (qi_col * jnp.exp(c_col[:span]))
        work.append((k_b, v_b, beta_row, c_row, c_col, ki_row, ki_col, low, reach, query))

    inverse = [eye_f - jnp.where(levels[0], w[7], 0.0) for w in work]
    for mask in levels[1:]:
        part = [mul(jnp.where(mask, w[7], 0.0), t) for w, t in zip(work, inverse)]
        inverse = [t - mul(t, p) for t, p in zip(inverse, part)]

    states = [None] * heads_in
    for n in range(blocks):
        for i in range(heads_in):
            state = states[i]
            k_b, v_b, beta_row, c_row, c_col, ki_row, ki_col, low, reach, query = work[i * blocks + n]
            t = inverse[i * blocks + n] * beta_row
            written = jnp.concatenate(
                [mul_left(t * (ki_row * jnp.exp(c_row)), k_b), mul_left(t, v_b)], 1
            )
            got = mul(reach, written)
            reduced, local_out = query - got[:, :128], got[:, 128:]
            last = c_col[span - 1 : span, :]
            tail = jnp.exp(last - c_col) * ki_col
            wh, wl = split(written * tail)
            k_t = jnp.transpose(k_b.astype(F32)).astype(BF16)
            made = dot(jnp.concatenate([k_t, k_t], 1), jnp.concatenate([wh, wl], 0))
            trans = jnp.exp(last) * eye_f - made[:, :128]
            inject = made[:, 128:]
            if state is None:
                emit(i, n, reduced, local_out)
                states[i] = jnp.concatenate([trans, inject], 1)
            else:
                read = mul(reduced, state)
                emit(i, n, read[:, :128], read[:, 128:] + local_out)
                states[i] = add_right(mul(trans, state), inject)
    return states


def local_kernel(blocks, q_ref, k_ref, v_ref, s_ref, x_ref, c_ref, b_ref):
    def load(i, n):
        at = pl.ds(n * BLOCK_LEN, BLOCK_LEN)
        k_b = jnp.concatenate([k_ref[0, at, :], k_ref[1, at, :]], 0)
        v_b = jnp.concatenate([v_ref[0, at, :], v_ref[1, at, :]], 0)
        return q_ref[at, :], k_b, v_b, s_ref[0, n : n + 1, :], s_ref[0, blocks + n : blocks + n + 1, :]

    def emit(i, n, carried, base):
        at = pl.ds(n * BLOCK_LEN, BLOCK_LEN)
        c_ref[0, at, :] = carried
        b_ref[0, at, :] = base

    x_ref[0] = head_maps(blocks, 1, load, emit)[0]


def small_rows(betas, log_decay):
    heads, length = log_decay.shape
    blocks = length // BLOCK_LEN
    beta = betas.reshape(2, heads, blocks, BLOCK_LEN).transpose(1, 2, 0, 3)
    beta = beta.reshape(heads, blocks, 2 * BLOCK_LEN)
    decay = log_decay.reshape(heads, blocks, 1, BLOCK_LEN)
    decay = jnp.concatenate([decay, decay], 2).reshape(heads, blocks, 2 * BLOCK_LEN)
    small = jnp.concatenate([decay, beta], 1)
    return small


def local_phase(queries, keys, values, betas, log_decay):
    length = queries.shape[0]
    heads = betas.shape[1]
    blocks = length // BLOCK_LEN
    small = small_rows(betas, log_decay)
    return pl.pallas_call(
        functools.partial(local_kernel, blocks),
        grid=(heads,),
        in_specs=[
            pl.BlockSpec((length, 128), lambda h: (0, h)),
            pl.BlockSpec((2, length, 128), lambda h: (0, 0, h)),
            pl.BlockSpec((2, length, 128), lambda h: (0, 0, h)),
            pl.BlockSpec((1, 2 * blocks, 128), lambda h: (h, 0, 0)),
        ],
        out_specs=[
            pl.BlockSpec((1, 128, 256), lambda h: (h, 0, 0)),
            pl.BlockSpec((1, length, 128), lambda h: (h, 0, 0)),
            pl.BlockSpec((1, length, 128), lambda h: (h, 0, 0)),
        ],
        out_shape=[
            jax.ShapeDtypeStruct((heads, 128, 256), F32),
            jax.ShapeDtypeStruct((heads, length, 128), F32),
            jax.ShapeDtypeStruct((heads, length, 128), F32),
        ],
        name="local_phase",
    )(queries, keys, values, small)


def then(earlier, later):
    return add_right(mul(later[:, :128], earlier), later[:, 128:])


def normed(carried, base, state, gain):
    readout = mul(carried, state) + base
    mean_sq = jnp.mean(readout * readout, 1, keepdims=True)
    return (readout * lax.rsqrt(mean_sq + 1e-05) * gain).astype(BF16)


LOG2E = 1.4426950408889634


def split3(x):
    high = x.astype(BF16)
    rest = x - high.astype(F32)
    mid = rest.astype(BF16)
    low = rest - mid.astype(F32)
    return high.astype(F32), mid.astype(F32), low


def tokens_of(shape, dim):
    at = lax.broadcasted_iota(jnp.int32, shape, dim)
    return at & (BLOCK_LEN - 1), at >> 6


def fill_spread(spread_ref):
    t_r, j_r = tokens_of((128, 128), 0)
    t_c, j_c = tokens_of((128, 128), 1)
    rank = 2 * (t_r & 7) + j_r
    same = (t_r >> 3) == (t_c >> 3)
    for p in range(8):
        parts = [jnp.where(same & (rank == 2 * p + q), 1.0, 0.0) for q in range(2)]
        spread_ref[p] = jnp.concatenate(parts, 1).astype(BF16)


def odd_starts(width):
    return [j * BLOCK_LEN + t for j in range(2) for t in range(width, BLOCK_LEN, 2 * width)]


def odd_rows(x, width):
    return jnp.concatenate([x[s : s + width] for s in odd_starts(width)], 0)


def stacked(left, right):
    rows = left[0].shape[0]
    both = dot(jnp.concatenate(left, 0), jnp.concatenate(right, 1))
    return both[:rows, :128] + (both[:rows, 128:] + both[rows:, :128])


def systems(blocks, heads_in, load, spread_ref):
    units = [(i, n) for i in range(heads_in) for n in range(blocks)]
    count = len(units)
    loaded = [load(i, n) for i, n in units]
    t_r, j_r = tokens_of((128, 128), 0)
    t_c, j_c = tokens_of((128, 128), 1)
    eye = (t_r == t_c) & (j_r == j_c)
    running = jnp.where((t_r <= t_c) & (j_r == 0), 1.0, 0.0).astype(BF16)
    decay = jnp.concatenate([u[1] for u in loaded], 0)
    beta = jnp.concatenate([u[2] for u in loaded], 0)
    total = dot(
        jnp.concatenate(split3(decay), 1).astype(BF16), jnp.concatenate([running] * 3, 0)
    )
    grams = [dot_t(u[0], u[0]) for u in loaded]
    squares = jnp.concatenate([jnp.sum(jnp.where(eye, g, 0.0), 0, keepdims=True) for g in grams], 0) + 1e-06
    inv = lax.rsqrt(squares)
    inv_log = -0.5 * jnp.log2(squares)
    fallen = total * LOG2E
    last = fallen[:, BLOCK_LEN - 1 : BLOCK_LEN]
    scale_k = jnp.exp2(fallen) * inv
    tail = jnp.exp2(last - fallen) * inv
    keep_all = jnp.exp2(last)
    ones = jnp.ones((count, 128), F32)
    zeros = jnp.zeros((count, 128), F32)
    stack = [*split3(fallen + inv_log), ones, ones, ones, *split3(beta), *split3(tail)]
    columns = jnp.transpose(jnp.concatenate(stack + [zeros] * (128 // count - len(stack)), 0)).astype(BF16)
    later = split3(inv_log - fallen)
    sub = lax.broadcasted_iota(jnp.int32, (count, 128), 0)

    lane_t, lane_j = tokens_of((8, 128), 1)
    row8 = lax.broadcasted_iota(jnp.int32, (8, 128), 0)
    in_block = [(lane_t >> 3) == b for b in range(8)]
    lane_rank = 2 * (lane_t & 7) + lane_j
    lower_0, lower_1 = 2 * row8 > lane_rank, 2 * row8 + 1 > lane_rank
    first_0 = jnp.where(2 * row8 == lane_rank, 1.0, 0.0)
    first_1 = jnp.where(2 * row8 + 1 == lane_rank, 1.0, 0.0)
    t16 = lax.broadcasted_iota(jnp.int32, (128, 128), 0) & (BLOCK_LEN - 1)
    own_block = jnp.where((t16 >> 3) == (t_c >> 3), 1.0, 0.0).astype(BF16)

    lows, tails, compact = [], [], []
    for u in range(count):
        pick = sub == u
        one = jnp.where(pick, 1.0, 0.0)
        right = [one] * 3 + [jnp.where(pick, g, 0.0) for g in later]
        none = [zeros]
        fill = 128 // count
        cols = [
            right + none * (fill - 6),
            none * 6 + [one] * 3 + none * (fill - 9),
            none * 9 + [one] * 3 + none * (fill - 12),
        ]
        right = jnp.concatenate([jnp.concatenate(c, 0) for c in cols], 1).astype(BF16)
        spread = dot(columns, right)
        low = grams[u] * jnp.exp2(spread[:, :128]) * spread[:, 128:256]
        lows.append(low)
        tails.append(spread[:, 256:])
        for j, lower in ((0, lower_0), (1, lower_1)):
            part = low[j * BLOCK_LEN : j * BLOCK_LEN + 8]
            for b in range(1, 8):
                at = j * BLOCK_LEN + 8 * b
                part = jnp.where(in_block[b], low[at : at + 8], part)
            compact.append(jnp.where(lower, part, 0.0))

    packed = wide(jnp.concatenate(compact, 0))
    pairs = [dot(packed, jnp.concatenate([spread_ref[p]] * 2, 0)) for p in range(8)]
    small = [[first_0, first_1] for _ in range(count)]
    for s in range(15):
        t, j, lanes = s // 2, s % 2, slice(128 * (s % 2), 128 * (s % 2) + 128)
        for u in range(count):
            x0, x1 = small[u]
            source = (x0, x1)[j][t : t + 1]
            coef = pairs[s // 2][16 * u : 16 * u + 16, lanes]
            small[u] = [x0 - coef[:8] * source, x1 - coef[8:] * source]

    highs, slims, updates = [], [], [[] for _ in range(count)]
    pair_of_8 = []
    for u in range(count):
        tiles = []
        for x in small[u]:
            both = jnp.concatenate([x, x], 0)
            tiles.append(split(both))
        high = jnp.concatenate([tiles[0][0]] * 4 + [tiles[1][0]] * 4, 0)
        slim = jnp.concatenate([tiles[0][1]] * 4 + [tiles[1][1]] * 4, 0)
        highs.append(high * own_block)
        slims.append(slim * own_block)
        pair_of_8.append(tiles)

    q = lax.broadcasted_iota(jnp.int32, (64, 128), 0) & 31
    c_t = lax.broadcasted_iota(jnp.int32, (64, 128), 1) & (BLOCK_LEN - 1)
    for width in (8, 16, 32):
        bits = width.bit_length()
        row_t = ((q >> (bits - 1)) << bits) + width + (q & (width - 1))
        mask = ((c_t & width) == 0) & ((c_t >> bits) == (row_t >> bits))
        if width == 8:
            odd_own = jnp.where((c_t >> 3) == (row_t >> 3), 1.0, 0.0).astype(BF16)
        parts = []
        for u in range(count):
            a = split(jnp.where(mask, odd_rows(lows[u], width), 0.0))
            parts.append(stacked(a, (highs[u], slims[u])))
        for u in range(count):
            p = parts[u]
            if width == 8:
                ph = p.astype(BF16).astype(F32)
                pl_ = p - ph
                doubled = [
                    jnp.concatenate([x[8 * (g // 2) : 8 * (g // 2) + 8] for g in range(16)], 0).astype(BF16)
                    for x in (ph, pl_)
                ]
                tiles = pair_of_8[u]
                odd = [jnp.concatenate([tiles[0][k]] * 2 + [tiles[1][k]] * 2, 0) * odd_own for k in range(2)]
            else:
                groups = range(64 // width)
                doubled = [
                    jnp.concatenate([x[width * g : width * g + width] for g in groups for _ in range(2)], 0)
                    for x in split(p)
                ]
                odd = [odd_rows(highs[u], width), odd_rows(slims[u], width)]
            update = stacked(odd, doubled)
            updates[u].append(update)
            if width == 32:
                continue
            if width == 8:
                uh = update.astype(BF16).astype(F32)
                gap = jnp.zeros((8, 128), F32)
                spaced = [
                    jnp.concatenate(
                        [x[8 * (g // 2) : 8 * (g // 2) + 8] if g % 2 else gap for g in range(16)], 0
                    ).astype(BF16)
                    for x in (uh, update - uh)
                ]
            else:
                gap = jnp.zeros((width, 128), BF16)
                spaced = [
                    jnp.concatenate(
                        [
                            x[width * (g // 2) : width * (g // 2) + width] if g % 2 else gap
                            for g in range(128 // width)
                        ],
                        0,
                    )
                    for x in split(update)
                ]
            highs[u] = highs[u] - spaced[0]
            slims[u] = slims[u] - spaced[1]

    work = []
    for u in range(count):
        rows = []
        for j in range(2):
            for b in range(8):
                x = jnp.where(in_block[b], small[u][j], 0.0)
                for width, update in zip((8, 16, 32), updates[u]):
                    t = 8 * b
                    if t & width:
                        at = j * 32 + (t // (2 * width)) * width + t % width
                        x = x - update[at : at + 8]
                rows.append(x)
        at = slice(u, u + 1)
        inverse = jnp.concatenate(rows, 0)
        work.append((inverse, beta[at], scale_k[at], tails[u], keep_all[at], total[at], inv[at]))
    return work, jnp.where(eye, 1.0, 0.0)


def state_maps(blocks, heads_in, work, eye_f, load_kv, keep):
    units = [(i, n) for n in range(blocks) for i in range(heads_in)]
    wrote, pieces = {}, {}
    for i, n in units:
        k_b, v_b = load_kv(i, n)
        inverse, beta_row, scale_k = work[i * blocks + n][:3]
        t = inverse * beta_row
        wrote[i, n] = mul_left(t * scale_k, k_b), mul_left(t, v_b)
    for i, n in units:
        k_b, _ = load_kv(i, n)
        tail, keep_all = work[i * blocks + n][3:5]
        wk, wv = wrote[i, n]
        wh, wl = split(jnp.concatenate([wk * tail, wv * tail], 1))
        k_t = jnp.transpose(k_b.astype(F32)).astype(BF16)
        made = dot(jnp.concatenate([k_t, k_t], 1), jnp.concatenate([wh, wl], 0))
        pieces[i, n] = jnp.concatenate([keep_all * eye_f - made[:, :128], made[:, 128:]], 1)
    firsts = [then(pieces[i, 0], pieces[i, 1]) for i in range(heads_in)]
    seconds = [then(pieces[i, 2], pieces[i, 3]) for i in range(heads_in)]
    states = [then(a, b) for a, b in zip(firsts, seconds)]
    for i, n in units:
        c_row, ki_row = work[i * blocks + n][5:7]
        part = (None, pieces[i, 0], firsts[i], pieces[i, 2])[n]
        keep(i, n, jnp.concatenate(wrote[i, n], 1), c_row, ki_row, part)
    return states


def reads(blocks, heads_in, load, emit):
    span = BLOCK_LEN
    row = lax.broadcasted_iota(jnp.int32, (span, 2 * span), 0)
    col = lax.broadcasted_iota(jnp.int32, (span, 2 * span), 1)
    col_t = col & (span - 1)
    seen = col_t <= row
    for i, n in [(i, n) for i in range(heads_in) for n in range(blocks)]:
        q_b, k_b, d_row, written, c_row, ki_row, state = load(i, n)
        c_col = jnp.sum(jnp.where(seen & (col < span), d_row, 0.0), 1, keepdims=True)
        q_f = q_b.astype(F32)
        qi_col = lax.rsqrt(jnp.sum(q_f * q_f, 1, keepdims=True) + 1e-06)
        fall = jnp.exp(jnp.minimum(c_col - c_row, 0.0))
        reach = jnp.where(seen, dot_t(q_b, k_b) * qi_col * ki_row * fall, 0.0)
        query = q_f * (qi_col * jnp.exp(c_col))
        got = mul(reach, written)
        reduced, local_out = query - got[:, :128], got[:, 128:]
        if n == 0:
            emit(i, n, reduced, local_out)
        else:
            read = mul(reduced, state)
            emit(i, n, read[:, :128], read[:, 128:] + local_out)


def whole_kernel(
    inner, outer, q_hbm, k_hbm, v_hbm, small_ref, o_ref,
    spread_buf, q_buf, k_buf, v_buf, w_buf, p_buf, vec_buf,
    away, near, own, even_map, sent, got, pair_buf, groups, mine, ready, came, aside, beside, c_buf, b_buf,
    load_k, load_v, load_q,
    send0, recv0, send1, recv1, send2, recv2, send3, recv3, send4, recv4, send5, recv5,
):
    mesh_id = pl.DeviceIdType.MESH
    length = q_hbm.shape[0]
    blocks = length // BLOCK_LEN
    me = lax.axis_index("inner")
    group = lax.axis_index("outer")
    core, chip, chips = me % 2, me // 2, inner // 2
    partner = chip * 2 + 1 - core
    groups[...] = jnp.zeros_like(groups)
    barrier = pltpu.get_barrier_semaphore()
    for d in range(1, chips):
        pl.semaphore_signal(
            barrier, inc=1, device_id=(group, (chip + d) % chips * 2 + core), device_id_type=mesh_id
        )
    pl.semaphore_signal(barrier, inc=1, device_id=(group, partner), device_id_type=mesh_id)
    for d in range(1, outer):
        pl.semaphore_signal(barrier, inc=1, device_id=((group + d) % outer, me), device_id_type=mesh_id)

    def flip(x):
        return (chip % 2 + x % 2) % 2 + (chip // 2 + x // 2) % 2 * 2

    def target(turn):
        return flip(chips - 1 - turn)

    def lanes_of(turn):
        return pl.ds(pl.multiple_of(target(turn) * 256, 256), 256)

    def k_copy(turn):
        return pltpu.make_async_copy(k_hbm.at[:, :, lanes_of(turn)], k_buf.at[turn], load_k.at[turn])

    def v_copy(turn):
        return pltpu.make_async_copy(v_hbm.at[:, :, lanes_of(turn)], v_buf.at[turn], load_v.at[turn])

    def q_copy(turn):
        return pltpu.make_async_copy(q_hbm.at[:, lanes_of(turn)], q_buf.at[turn], load_q.at[turn])

    for t in range(chips):
        k_copy(t).start()
        v_copy(t).start()
    for t in range(chips):
        q_copy(t).start()

    fill_spread(spread_buf)

    def near_copy(turn):
        return pltpu.make_async_remote_copy(
            src_ref=away.at[turn], dst_ref=near.at[turn],
            send_sem=send0.at[turn], recv_sem=recv0.at[turn],
            device_id=(group, partner), device_id_type=mesh_id,
        )

    def map_copy(d):
        return pltpu.make_async_remote_copy(
            src_ref=sent.at[d], dst_ref=got.at[d],
            send_sem=send1.at[d], recv_sem=recv1.at[d],
            device_id=(group, flip(chips - d) * 2 + core), device_id_type=mesh_id,
        )

    def chip_map(turn):
        near_copy(turn).wait()
        here, there = own[turn], near[turn]
        even = jnp.where(core == 0, here, there)
        odd = jnp.where(core == 0, there, here)
        even_map[turn] = even
        return then(even, odd)

    def parity(i):
        return core if i == 0 else 1 - core

    def head_lanes(i):
        return pl.ds(pl.multiple_of(parity(i) * 128, 128), 128)

    def rows_of(head, n):
        at = slice(n * BLOCK_LEN, (n + 1) * BLOCK_LEN)
        row = pl.ds(head, 1)
        b0, b1 = small_ref[0, row, :][:, at], small_ref[1, row, :][:, at]
        d = small_ref[2, row, :][:, at]
        return jnp.concatenate([d, d], 1), jnp.concatenate([b0, b1], 1)

    def pair_of(buf, turn, i, n):
        at = pl.ds(n * BLOCK_LEN, BLOCK_LEN)
        return jnp.concatenate([buf[turn, 0, at, head_lanes(i)], buf[turn, 1, at, head_lanes(i)]], 0)

    def step(turn, carry):
        heads = [target(turn) * 2 + parity(i) for i in range(2)]
        k_copy(turn).wait()

        def load(i, n):
            d_row, beta_row = rows_of(heads[i], n)
            return pair_of(k_buf, turn, i, n), d_row, beta_row

        work, eye_f = systems(blocks, 2, load, spread_buf)

        @pl.when(turn == 0)
        def _():
            pl.semaphore_wait(barrier, chips + outer - 1)

        @pl.when(turn > 0)
        def _():
            sent[turn] = chip_map(turn - 1)
            map_copy(turn).start()

        v_copy(turn).wait()

        def load_kv(i, n):
            return pair_of(k_buf, turn, i, n), pair_of(v_buf, turn, i, n)

        def keep(i, n, written, c_row, ki_row, state):
            w_buf[turn, i, n] = written
            vec_buf[turn, i, n, 0:1, :] = c_row
            vec_buf[turn, i, n, 1:2, :] = ki_row
            if n:
                p_buf[turn, i, n] = state

        states = state_maps(blocks, 2, work, eye_f, load_kv, keep)
        away[turn] = states[1]
        own[turn] = states[0]

        near_copy(turn).start()
        return carry

    lax.fori_loop(0, chips, step, 0)

    def read_step(turn, carry):
        heads = [target(turn) * 2 + parity(i) for i in range(2)]
        q_copy(turn).wait()

        before = []
        for i in range(2):
            first = p_buf[turn, i, 2]
            before.append([None, p_buf[turn, i, 1], first, then(first, p_buf[turn, i, 3])])

        def load(i, n):
            at = pl.ds(n * BLOCK_LEN, BLOCK_LEN)
            d_row, _ = rows_of(heads[i], n)
            return (
                q_buf[turn, at, head_lanes(i)], pair_of(k_buf, turn, i, n), d_row, w_buf[turn, i, n],
                vec_buf[turn, i, n, 0:1, :], vec_buf[turn, i, n, 1:2, :], before[i][n],
            )

        def emit(i, n, carried, base):
            at = pl.ds(n * BLOCK_LEN, BLOCK_LEN)
            c_buf[turn, i, at, :] = carried
            b_buf[turn, i, at, :] = base

        reads(blocks, 2, load, emit)
        return carry

    lax.fori_loop(0, 1, lambda i, c: read_step(chips - 1 - i, c), 0)
    def slot(i):
        return (chips - flip(i)) % chips

    def pair_map(side):
        return then(got[slot(2 * side)], got[slot(2 * side + 1)])

    got[0] = chip_map(chips - 1)
    map_copy(1).wait()
    map_copy(2).wait()
    pair_buf[1 - chip // 2] = pair_map(1 - chip // 2)
    map_copy(3).wait()
    pair_buf[chip // 2] = pair_map(chip // 2)
    total = then(pair_buf[0], pair_buf[1])
    mine[0] = total[:, :128]
    mine[1] = total[:, 128:]

    def group_copy(part, d):
        sems = (send2, recv2) if part == 0 else (send5, recv5)
        return pltpu.make_async_remote_copy(
            src_ref=mine.at[part], dst_ref=groups.at[part, d],
            send_sem=sems[0].at[d], recv_sem=sems[1].at[d],
            device_id=((group + d) % outer, me), device_id_type=mesh_id,
        )

    for d in range(1, outer):

        @pl.when(group + d < outer)
        def _():
            group_copy(1, d).start()

    for d in range(1, outer):

        @pl.when((group + d < outer) & (group > 0))
        def _():
            group_copy(0, d).start()

    before = [None, got[slot(0)], pair_buf[0], then(pair_buf[0], got[slot(2)])]
    left = wide(jnp.concatenate([before[i][:, :128] for i in range(1, chips)], 0))
    right = jnp.concatenate([before[i][:, 128:] for i in range(1, chips)], 0)

    lax.fori_loop(1, 2, lambda i, c: read_step(chips - 1 - i, c), 0)

    start = jnp.zeros((128, 128), F32)
    for g in range(outer - 1):
        at = (group - g + outer) % outer

        @pl.when(group > g)
        def _():
            group_copy(1, at).wait_recv()
            if g:
                group_copy(0, at).wait_recv()

        moved = groups[1, at]
        if g:
            moved = mul(groups[0, at], start) + moved
        start = jnp.where(g < group, moved, start)

    sh, sl = split(start)
    row = jnp.concatenate([sh, sl], 1)
    both = dot(left, jnp.concatenate([row, row], 0))
    ready[0] = start
    ready[pl.ds(1, chips - 1)] = (both[:, :128] + both[:, 128:] + right).reshape(chips - 1, 128, 128)

    def back_copy(d):
        to = flip(d)
        return pltpu.make_async_remote_copy(
            src_ref=ready.at[to], dst_ref=came.at[d],
            send_sem=send3.at[d], recv_sem=recv3.at[d],
            device_id=(group, to * 2 + core), device_id_type=mesh_id,
        )

    def side_copy(d):
        return pltpu.make_async_remote_copy(
            src_ref=aside.at[d], dst_ref=beside.at[d],
            send_sem=send4.at[d], recv_sem=recv4.at[d],
            device_id=(group, partner), device_id_type=mesh_id,
        )

    for d in (1, 3, 2):
        back_copy(d).start()

    def out(turn, i, state):
        head = target(turn) * 2 + parity(i)
        lanes = pl.ds(pl.multiple_of(head * 128, 128), 128)
        o_ref[:, lanes] = normed(c_buf[turn, i], b_buf[turn, i], state, small_ref[3, 0:1, :128])

    for d in range(chips):
        turn = chips - 1 - d
        if d:
            back_copy(d).wait_recv()
            enter = came[d]
        else:
            enter = ready[chip]
        pair = even_map[turn]
        after = mul(pair[:, :128], enter) + pair[:, 128:]
        aside[d] = jnp.where(core == 0, after, enter)
        side_copy(d).start()
        out(turn, 0, jnp.where(core == 0, enter, after))
        if d == 0:
            lax.fori_loop(2, 4, lambda i, c: read_step(chips - 1 - i, c), 0)
        if d:
            side_copy(d - 1).wait_recv()
            out(turn + 1, 1, beside[d - 1])
    side_copy(chips - 1).wait_recv()
    out(0, 1, beside[chips - 1])
    for d in range(chips):
        if d:
            back_copy(d).wait_send()
        side_copy(d).wait_send()
    for d in range(1, outer):

        @pl.when(group + d < outer)
        def _():
            group_copy(1, d).wait_send()

        @pl.when((group + d < outer) & (group > 0))
        def _():
            group_copy(0, d).wait_send()


def whole(inner, outer, queries, keys, values, betas, log_decay, out_gain):
    length, width = queries.shape
    blocks = length // BLOCK_LEN
    chips = inner // 2
    gain = lax.broadcast_in_dim(jnp.pad(out_gain, (0, length - 128)), (1, inner, length), (2,))
    small = jnp.concatenate([betas, log_decay[None], gain], 0)
    vmem = pl.BlockSpec(memory_space=pltpu.VMEM)
    hbm = pl.BlockSpec(memory_space=pltpu.HBM)
    dma = pltpu.SemaphoreType.DMA
    return pl.pallas_call(
        functools.partial(whole_kernel, inner, outer),
        in_specs=[hbm] * 3 + [vmem],
        out_specs=vmem,
        out_shape=jax.ShapeDtypeStruct((length, width), BF16),
        scratch_shapes=[
            pltpu.VMEM((8, 128, 256), BF16),
            pltpu.VMEM((chips, length, 256), BF16),
            *[pltpu.VMEM((chips, 2, length, 256), BF16)] * 2,
            *[pltpu.VMEM((chips, 2, blocks, 128, 256), F32)] * 2,
            pltpu.VMEM((chips, 2, blocks, 8, 128), F32),
            *[pltpu.VMEM((chips, 128, 256), F32)] * 6,
            pltpu.VMEM((2, 128, 256), F32),
            pltpu.VMEM((2, outer, 128, 128), F32),
            pltpu.VMEM((2, 128, 128), F32),
            *[pltpu.VMEM((chips, 128, 128), F32)] * 4,
            *[pltpu.VMEM((chips, 2, length, 128), F32)] * 2,
            *[dma((chips,))] * 3,
            *[dma((chips,))] * 4,
            *[dma((outer,))] * 2,
            *[dma((chips,))] * 4,
            *[dma((outer,))] * 2,
        ],
        compiler_params=pltpu.CompilerParams(
            collective_id=0, has_side_effects=True, vmem_limit_bytes=53 * 1024 * 1024
        ),
        name="whole",
    )(queries, keys, values, small)


HIGHEST = lax.Precision.HIGHEST


def join(earlier, later):
    moved = jnp.einsum("hde,hef->hdf", later[..., :128], earlier, precision=HIGHEST)
    return jnp.concatenate([moved[..., :128], moved[..., 128:] + later[..., 128:]], -1)


def entering(pairs, axis, begin):
    gathered = lax.all_gather(pairs, axis)

    def one(hop, state):
        return join(state, lax.dynamic_index_in_dim(gathered, hop, 0, False))

    return lax.fori_loop(0, lax.axis_index(axis), one, begin)


def exchange_plain(pairs):
    eye = jnp.concatenate([jnp.eye(128, dtype=F32), jnp.zeros((128, 128), F32)], 1)
    begin = jnp.zeros_like(pairs) + eye
    before = entering(pairs, "inner", begin)
    through = join(before, pairs)
    last = lax.axis_index("inner") == lax.axis_size("inner") - 1
    total = lax.psum(jnp.where(last, through, 0.0), "inner")
    start = entering(total, "outer", begin)
    return join(start, before)[..., 128:]


def finish_kernel(c_ref, b_ref, e_ref, g_ref, o_ref):
    readout = mul(c_ref[0], e_ref[0]) + b_ref[0]
    mean_sq = jnp.mean(readout * readout, 1, keepdims=True)
    o_ref[...] = (readout * lax.rsqrt(mean_sq + 1e-05) * g_ref[...]).astype(BF16)


def finish(carried, base, state, out_gain):
    heads, length, _ = carried.shape
    return pl.pallas_call(
        finish_kernel,
        grid=(heads,),
        in_specs=[
            pl.BlockSpec((1, length, 128), lambda h: (h, 0, 0)),
            pl.BlockSpec((1, length, 128), lambda h: (h, 0, 0)),
            pl.BlockSpec((1, 128, 128), lambda h: (h, 0, 0)),
            pl.BlockSpec((1, 128), lambda h: (0, 0)),
        ],
        out_specs=pl.BlockSpec((length, 128), lambda h: (0, h)),
        out_shape=jax.ShapeDtypeStruct((length, heads * 128), BF16),
        name="finish",
    )(carried, base, state, out_gain.reshape(1, 128))


def per_device(inner, outer, queries, keys, values, betas, log_decay, out_gain):
    heads = betas.shape[1]
    if inner == heads == 8:
        return whole(inner, outer, queries, keys, values, betas, log_decay, out_gain)
    pairs, carried, base = local_phase(queries, keys, values, betas, log_decay)
    return finish(carried, base, exchange_plain(pairs), out_gain)


def solution(mesh):
    both = ("outer", "inner")
    placed = (P(both, None), P(None, both, None), P(None, both, None), P(None, None, both), P(None, both), P())
    return jax.shard_map(
        functools.partial(per_device, mesh.shape["inner"], mesh.shape["outer"]),
        mesh=mesh,
        in_specs=placed,
        out_specs=P(both, None),
        check_vma=False,
    )
```
